32 devices in a mesh: gx: 8 (over y, x, core), gy: 4 (over z).
Axes of the slice: x: 2, y: 2, z: 4, core: 2. Of those that a mesh axis runs over, the one named last changes fastest.
Arguments:
- populations: float32 [19, 32, 128, 128], P(None, 'gx', 'gy'), may hold values from 0.02 to 0.09
- marker_weights: bfloat16 [1536, 64, 128], P(('gx', 'gy')), may hold values from 0 to 0.03125
- marker_force: bfloat16 [1536, 3, 128], P(('gx', 'gy')), may hold values from -0.59765625 to 0.59765625
- owner_device: int32 [1536, 1], P(('gx', 'gy')), may hold values from 0 to 31; in each aligned block of 48 rows (0 to 47, 48 to 95, ...) at most 3 rows name the same one
- stencil_base: int32 [1536, 3], P(('gx', 'gy')), may hold values from 0 to 124, as said below
- block_swimmer: int32 [1536], P(('gx', 'gy')), may hold values from 0 to 127, as said below
Outputs:
- new_populations: float32 [19, 32, 128, 128], P(None, 'gx', 'gy')
- marker_velocity: float32 [1536, 3, 128], P(('gx', 'gy'))
- swimmer_velocity: float32 [3, 128], P(None, ('gx', 'gy'))
The draws below stay inside these ranges and needn't reach their ends.
Inputs may be any that keep to these rules, and one draw needn't show every extreme that they name: `owner_device`: among the blocks held by one device (aligned runs of 48 rows), no device is named more than 3 times, and some device is named exactly 3 times. `stencil_base`: component 0 lies in 0 to 0, component 1 in 0 to 28, component 2 in 0 to 124; each bound is taken by some block. `block_swimmer`: the blocks held by device d (gx slowest) belong to swimmers d * 4 to d * 4 + 3, and every swimmer has a block.
All inputs are finite; a program needn't handle non-finite values.
Results may differ from the reference program's by a relative error of at most 0.00056.
Values may be sent and summed in bfloat16 or wider, within the bound.
No kernel may reach another device: no remote copies, remote signals or barrier semaphores. Data moves between devices by JAX's collectives and lax.ppermute only.
A program may use at most 64 MiB of HBM per device.

```python
import math
import jax
import jax.numpy as jnp
import numpy as np
from jax import lax

CX = 4
CY = 32
NZ = 128
STEN = 4
MARK = 128
BLK_DEV = 48
SWIM_DEV = 4
NX = 32
NY = 128
BLOCKS = 1536
SWIMMERS = 128
CAP = 3
N_GY = 4
DEVICES = 32


def draw_stencil_base(key, part):
    key_slab, key_strip, key_column = jax.random.split(jax.random.fold_in(key, 11), 3)
    along_slab = jax.random.randint(key_slab, (BLOCKS,), 0, CX - 3, dtype=jnp.int32).at[0].set(CX - 4)
    along_strip = jax.random.randint(key_strip, (BLOCKS,), 0, CY - 3, dtype=jnp.int32).at[0].set(CY - 4)
    along_column = jax.random.randint(key_column, (BLOCKS,), 0, NZ - 3, dtype=jnp.int32).at[0].set(NZ - 4)
    return jnp.stack([along_slab, along_strip, along_column], axis=1)


def draw_block_swimmer(key, part):
    block_rows = jnp.arange(BLOCKS, dtype=jnp.int32)
    device_rank = block_rows // BLK_DEV
    within = block_rows % BLK_DEV
    random_slot = jax.random.randint(jax.random.fold_in(key, 7), (BLOCKS,), 0, SWIM_DEV, dtype=jnp.int32)
    return device_rank * SWIM_DEV + jnp.where(within < SWIM_DEV, within, random_slot)


def block_scale(rng, shape, pieces, least, largest):
    level, own = 1.0, jax.random.fold_in(rng, 6)
    for position, blocks in pieces:
        steps = jnp.exp(jax.random.uniform(jax.random.fold_in(own, position), (blocks,), jnp.float32, least / len(pieces), largest / len(pieces)))
        level = level * jnp.repeat(steps, shape[position] // blocks).reshape([-1 if axis == position else 1 for axis in range(len(shape))])
    return level


def deal_out(rng, own, number, rows, number_of, top, bound, slope):
    ranking = jax.random.permutation(rng, number_of)
    crowded, common = load_shares(number_of, rows * top, bound, slope, True), load_shares(number_of, rows * top, bound, slope, False)
    places = jnp.arange(number_of)

    def named(lengths, offset_by):
        used = int((lengths > 0).sum())
        fixed = max(1, used // 4)
        shifted = fixed + (places - fixed + offset_by * (used - fixed)) % max(1, number_of - fixed)
        return jnp.zeros((number_of,), jnp.int32).at[ranking[jnp.where(places < fixed, places, shifted)]].set(jnp.asarray(lengths, jnp.int32))

    lengths = jnp.where(number % 4 == 0, named(crowded, number // 4), named(common, number - number // 4 - 1))
    mixed = jax.random.permutation(jax.random.fold_in(own, 3), number_of)
    donor, sink = mixed[0:number_of // 2 * 2:2], mixed[1:number_of // 2 * 2:2]
    margin = jnp.minimum(lengths[donor] - 1, bound - lengths[sink]) // 2
    margin = jnp.where((donor == ranking[0]) | (sink == ranking[0]) | (lengths[sink] == 0), 0, jnp.maximum(margin, 0))
    shifted = jax.random.randint(jax.random.fold_in(own, 4), (number_of // 2,), 0, 1 << 20) % (margin + 1)
    lengths = lengths.at[donor].add(-shifted).at[sink].add(shifted)
    items = jnp.searchsorted(jnp.cumsum(lengths), jnp.arange(rows * top), side="right").astype(jnp.int32)
    grid = items.reshape(top, rows).T
    grid = grid[jax.random.permutation(jax.random.fold_in(own, 1), rows)]
    offset_by = jax.random.randint(jax.random.fold_in(own, 2), (rows, 1), 0, top)
    return jnp.take_along_axis(grid, (jnp.arange(top)[None, :] + offset_by) % top, axis=1)


def load_shares(count, total, most, lean, full):
    weights = [(1 << 20) // math.isqrt(grade ** lean) + 1 for grade in range(1, count + 1)]
    largest = most if full else min(most, max(-(-total // count), total * weights[0] // sum(weights)))
    least = 1 if total - largest >= count - 1 else 0
    given, spare = [largest] + [least] * (count - 1), total - largest - least * (count - 1)
    while spare > 0:
        movable = [i for i in range(1, count) if given[i] < largest] or [i for i in range(1, count) if given[i] < most]
        pool, remaining = sum([weights[i] for i in movable]), spare
        for i in movable:
            addition = min(most - given[i], max(1, remaining * weights[i] // pool), spare)
            given[i] = given[i] + addition
            spare = spare - addition
    return np.array(given)


def gaussian(stream_key, dims, spread, most, cuts=(), kind=jnp.bfloat16):
    values = jax.random.normal(stream_key, dims, jnp.float32) * spread
    if len(cuts) > 0:
        values = block_scale(stream_key, dims, cuts, -0.22, 0.18) * values
    return jnp.clip(values, min=-most, max=most).astype(kind)


def setup_inputs(seed: int = 0) -> dict:
    keys = jax.random.split(jax.random.key(seed), 7)
    populations = jnp.clip(0.02 + 0.07000000402331352 * jax.random.uniform(keys[0], (19, NX, NY, NZ), jnp.float32) ** block_scale(keys[0], (19, NX, NY, NZ), ((1, 8), (2, 4)), -0.2, 0.2), 0.02, 0.09)
    marker_weights = jnp.clip(0.03125 * jax.random.uniform(keys[1], (BLOCKS, STEN * STEN * STEN, MARK), jnp.float32) ** block_scale(keys[1], (BLOCKS, STEN * STEN * STEN, MARK), ((0, 32),), -0.2, 0.2), 0.0, 0.03125).astype(jnp.bfloat16)
    marker_force = gaussian(keys[2], (BLOCKS, 3, MARK), 0.1, 0.59765625, ((0, 32),))
    owner_device_keys = jax.random.split(jax.random.fold_in(keys[3], 1), BLOCKS // BLK_DEV)
    owner_device_turns = jax.random.permutation(jax.random.fold_in(keys[3], 3), BLOCKS // BLK_DEV)
    owner_device = jax.vmap(lambda own, number: deal_out(jax.random.fold_in(keys[3], 2), own, number, BLK_DEV, DEVICES, 1, CAP, 2))(owner_device_keys, owner_device_turns).reshape((BLOCKS, 1))
    stencil_base = draw_stencil_base(jax.random.fold_in(keys[6], 71), 0)
    block_swimmer = draw_block_swimmer(jax.random.fold_in(keys[6], 71), 0)
    return {"populations": populations, "marker_weights": marker_weights, "marker_force": marker_force, "owner_device": owner_device, "stencil_base": stencil_base, "block_swimmer": block_swimmer}


velocities = np.array([[0, 0, 0], [1, 0, 0], [-1, 0, 0], [0, 1, 0], [0, -1, 0], [0, 0, 1], [0, 0, -1], [1, 1, 0], [-1, -1, 0], [1, -1, 0], [-1, 1, 0], [1, 0, 1], [-1, 0, -1], [1, 0, -1], [-1, 0, 1], [0, 1, 1], [0, -1, -1], [0, 1, -1], [0, -1, 1]])
opposite = [0, 2, 1, 4, 3, 6, 5, 8, 7, 10, 9, 12, 11, 14, 13, 16, 15, 18, 17]
lattice_weights = np.array([1.0 / 3.0] + [1.0 / 18.0] * 6 + [1.0 / 36.0] * 12)
relax_time = 0.8
speed_scale = 20.0


def signed_total(stack, component):
    plus_list = [i for i in range(19) if velocities[i, component] == 1]
    minus_list = [i for i in range(19) if velocities[i, component] == -1]
    return jnp.sum(stack[np.array(plus_list)], axis=0) - jnp.sum(stack[np.array(minus_list)], axis=0)


def moments(fields):
    density = jnp.sum(fields, axis=0)
    momentum = jnp.stack([signed_total(fields, k) for k in range(3)])
    return density, momentum


def collide(fields, forcing):
    density, momentum = moments(fields)
    velocity = (momentum + relax_time * forcing) / density
    project_list = []
    for direction in range(19):
        term = jnp.zeros_like(density)
        for k in range(3):
            sign = int(velocities[direction, k])
            if sign == 1:
                term = term + velocity[k]
            elif sign == -1:
                term = term - velocity[k]
        project_list.append(term)
    project = jnp.stack(project_list)
    square = jnp.sum(velocity * velocity, axis=0)
    weights = jnp.asarray(lattice_weights, jnp.float32)[:, None, None, None]
    equilibrium = weights * density * (1.0 + 3.0 * project + 4.5 * project * project - 1.5 * square)
    return fields - (fields - equilibrium) / relax_time


def stream(padded, first_row, total_rows):
    slab_cells = padded.shape[1] - 2
    strip_cells = padded.shape[2] - 2
    height = padded.shape[3]
    global_rows = first_row + jnp.arange(strip_cells, dtype=jnp.int32)
    column_cells = jnp.arange(height, dtype=jnp.int32)
    result = []
    for direction in range(19):
        move_east = int(velocities[direction, 0])
        move_north = int(velocities[direction, 1])
        move_up = int(velocities[direction, 2])
        source = padded[direction, 1 - move_east:1 - move_east + slab_cells, 1 - move_north:1 - move_north + strip_cells, :]
        source = jnp.roll(source, move_up, axis=2)
        bounce = padded[opposite[direction], 1:1 + slab_cells, 1:1 + strip_cells, :]
        anchor_row = global_rows - move_north
        anchor_cell = column_cells - move_up
        outside = ((anchor_row < 0) | (anchor_row >= total_rows))[:, None] | ((anchor_cell < 0) | (anchor_cell >= height))[None, :]
        result.append(jnp.where(outside[None], bounce, source))
    return jnp.stack(result)


def fluid_speed(fields, forcing):
    density, momentum = moments(fields)
    return (momentum + 0.5 * forcing) / density


def reference(populations, marker_weights, marker_force, owner_device, stencil_base, block_swimmer):
    weights_wide = marker_weights.astype(jnp.float32)
    patches = jnp.einsum('bcm,bkm->bkc', weights_wide, marker_force.astype(jnp.float32), precision=lax.Precision.HIGHEST)
    owner_rank = owner_device[:, 0]
    corner_slab = (owner_rank // N_GY) * CX + stencil_base[:, 0]
    corner_strip = (owner_rank % N_GY) * CY + stencil_base[:, 1]
    corner_column = stencil_base[:, 2]
    anchor_zero = jnp.zeros((), jnp.int32)

    def place_patch(force_grid, block_item):
        patch, slab_at, strip_at, column_at = block_item
        patch_cube = patch.reshape(3, STEN, STEN, STEN)
        start = (anchor_zero, slab_at.astype(jnp.int32), strip_at.astype(jnp.int32), column_at.astype(jnp.int32))
        existing = lax.dynamic_slice(force_grid, start, (3, STEN, STEN, STEN))
        return lax.dynamic_update_slice(force_grid, existing + patch_cube, start), None

    forcing, _ = lax.scan(place_patch, jnp.zeros((3, NX, NY, NZ), jnp.float32), (patches, corner_slab, corner_strip, corner_column))
    fields = populations
    for substep in range(2):
        relaxed = collide(fields, forcing)
        padded = jnp.pad(relaxed, ((0, 0), (1, 1), (1, 1), (0, 0)), mode='wrap')
        fields = stream(padded, 0, NY)
    velocity_field = fluid_speed(fields, forcing)

    def sample_cube(slab_at, strip_at, column_at):
        start = (anchor_zero, slab_at.astype(jnp.int32), strip_at.astype(jnp.int32), column_at.astype(jnp.int32))
        return lax.dynamic_slice(velocity_field, start, (3, STEN, STEN, STEN)).reshape(3, STEN * STEN * STEN)

    samples = jax.vmap(sample_cube)(corner_slab, corner_strip, corner_column)
    cell_speed = lax.optimization_barrier(samples.astype(jnp.bfloat16)).astype(jnp.float32)
    marker_velocity = speed_scale * jnp.einsum('bcm,bkc->bkm', weights_wide, cell_speed, precision=lax.Precision.HIGHEST)
    block_mean = jnp.mean(marker_velocity, axis=2)
    swimmer_velocity = jax.ops.segment_sum(block_mean, block_swimmer, SWIMMERS).T
    return fields, marker_velocity, swimmer_velocity
```

```python
import functools

import jax
import jax.numpy as jnp
import numpy as np
from jax import lax
from jax.experimental import pallas as pl
from jax.experimental.pallas import tpu as pltpu
from jax.sharding import PartitionSpec as P

STEN = 4
SWIM_DEV = 4
LANES = 128
SUB = 8
GROUP = STEN * STEN
CODE_LANE = 96

velocities = np.array(
    [
        [0, 0, 0],
        [1, 0, 0],
        [-1, 0, 0],
        [0, 1, 0],
        [0, -1, 0],
        [0, 0, 1],
        [0, 0, -1],
        [1, 1, 0],
        [-1, -1, 0],
        [1, -1, 0],
        [-1, 1, 0],
        [1, 0, 1],
        [-1, 0, -1],
        [1, 0, -1],
        [-1, 0, 1],
        [0, 1, 1],
        [0, -1, -1],
        [0, 1, -1],
        [0, -1, 1],
    ]
)
opposite = [0, 2, 1, 4, 3, 6, 5, 8, 7, 10, 9, 12, 11, 14, 13, 16, 15, 18, 17]
lattice_weights = [1.0 / 3.0] + [1.0 / 18.0] * 6 + [1.0 / 36.0] * 12
relax_time = 0.8
speed_scale = 20.0
going_east = [1, 7, 9, 11, 13]
going_west = [2, 8, 10, 12, 14]


def lane_iota(rows=SUB):
    return lax.broadcasted_iota(jnp.int32, (rows, LANES), 1)


def sub_iota(rows=SUB):
    return lax.broadcasted_iota(jnp.int32, (rows, LANES), 0)


def swapped(first, second, axis, periodic):
    size = lax.axis_size(axis)
    inner = [(i, i ^ 1) for i in range(size)]
    outer = []
    for i in range(size):
        j = i + 1 if i % 2 == 1 else i - 1
        if periodic:
            outer.append((i, j % size))
        elif 0 <= j < size:
            outer.append((i, j))
    return lax.ppermute(first, axis, inner), lax.ppermute(second, axis, outer)


def patch_kernel(
    capacity, strips, strip_cells, owner, base, weights, force, send, force_rows, patches, count
):
    held = weights.shape[0]
    cells = weights.shape[1]
    targets = send.shape[0] // 3
    lane, sub = lane_iota(16), sub_iota(16)
    force_rows[...] = jnp.zeros_like(force_rows)

    def zero(i, _):
        send[i] = jnp.zeros((4, LANES), jnp.float32)
        return 0

    lax.fori_loop(0, send.shape[0], zero, 0, unroll=8)

    def reset(i, _):
        count[i] = 0
        return 0

    lax.fori_loop(0, targets, reset, 0, unroll=8)

    def group_step(g, _):
        for j in range(4):
            rows = force[g * 4 + j].astype(jnp.float32)
            for k in range(3):
                force_rows[16 * j + 4 * k : 16 * j + 4 * k + 4, :] = jnp.broadcast_to(
                    rows[k : k + 1, :], (4, LANES)
                )
        four = weights[pl.ds(g * 4, 4)].reshape(4 * cells, LANES)
        out = lax.dot_general(
            force_rows[...].astype(jnp.bfloat16),
            four,
            (((1,), (1,)), ((), ())),
            preferred_element_type=jnp.float32,
        )
        for j in range(4):
            half = j // 2
            part = out[16 * j : 16 * j + 16, LANES * half : LANES * half + LANES]
            part = jnp.where(lane // GROUP == 4 * (j % 2) + sub % 4, part, 0.0)
            part = part + pltpu.roll(part, 64, 1)
            part = part + pltpu.roll(part, 32, 1)
            part = part + pltpu.roll(part, 16, 1)
            patches[g * 4 + j] = part
        return 0

    lax.fori_loop(0, held // 4, group_step, 0)
    lane4, sub4 = lane_iota(4), sub_iota(4)

    def place(b, _):
        target = owner[b, 0]
        rank = count[target]
        count[target] = rank + 1
        y = base[b, 1]
        z = base[b, 2]
        tiles = [patches[b, 4 * k : 4 * k + 4, :] for k in range(3)]

        def put(dest, low, wide, code_at, frame_y):
            code = ((frame_y + SUB) * LANES + z + 1).astype(jnp.float32)
            inside = (lane4 >= low) & (lane4 < low + wide)
            for k in range(3):
                tile = jnp.where(inside, tiles[k], send[dest * 3 + k])
                if k == 0:
                    tile = jnp.where((sub4 == 0) & (lane4 == code_at), code, tile)
                send[dest * 3 + k] = tile

        put(target, GROUP * rank, GROUP, CODE_LANE + rank, y)
        strip = lax.rem(target, strips)

        @pl.when((y >= strip_cells - 5) & (strip < strips - 1))
        def _():
            put(
                target + 1,
                GROUP * (capacity + rank) + 8,
                8,
                CODE_LANE + capacity + rank,
                y - strip_cells,
            )

        @pl.when((y <= 1) & (strip > 0))
        def _():
            put(
                target - 1,
                GROUP * (capacity + rank),
                8,
                CODE_LANE + 2 * capacity + rank,
                y + strip_cells,
            )

        return 0

    lax.fori_loop(0, held, place, 0)


def collided(fields, forcing):
    pair_sum, pair_diff = {}, {}
    for i in range(1, 19, 2):
        pair_sum[i] = fields[i] + fields[i + 1]
        pair_diff[i] = fields[i] - fields[i + 1]
    density = fields[0]
    for i in range(1, 19, 2):
        density = density + pair_sum[i]
    momentum = []
    for k in range(3):
        total = relax_time * forcing[k]
        for i in range(1, 19, 2):
            if velocities[i, k] == 1:
                total = total + pair_diff[i]
            elif velocities[i, k] == -1:
                total = total - pair_diff[i]
        momentum.append(total)
    inverse = 1.0 / density
    keep = 1.0 - 1.0 / relax_time
    squares = momentum[0] * momentum[0] + momentum[1] * momentum[1] + momentum[2] * momentum[2]
    level = density - 1.5 * inverse * squares
    curve = 4.5 * inverse
    result = [None] * 19
    result[0] = keep * fields[0] + (lattice_weights[0] / relax_time) * level
    for i in range(1, 19, 2):
        along = None
        for k in range(3):
            if velocities[i, k] == 1:
                along = momentum[k] if along is None else along + momentum[k]
            elif velocities[i, k] == -1:
                along = -momentum[k] if along is None else along - momentum[k]
        share = lattice_weights[i] / relax_time
        even = share * (level + curve * along * along)
        odd = (3.0 * share) * along
        result[i] = keep * fields[i] + (even + odd)
        result[i + 1] = keep * fields[i + 1] + (even - odd)
    return result


def keep_tile(relaxed, tiles, x, t, values):
    for i in range(19):
        if t < tiles:
            relaxed[i, x, SUB + SUB * t : 2 * SUB + SUB * t, :] = values[i]
        else:
            relaxed[i, x, 0:SUB, :] = values[i]
            relaxed[i, x, SUB + SUB * tiles : 2 * SUB + SUB * tiles, :] = values[i]


def write_faces(relaxed, slabs, tiles, face_a, face_b):
    even = lax.rem(lax.axis_index("gx"), 2) == 0
    for n in range(5):
        for t in range(tiles + 1):
            low = SUB + SUB * t
            east = relaxed[going_east[n], slabs - 1, low : low + SUB, :]
            west = relaxed[going_west[n], 0, low : low + SUB, :]
            face_a[n, SUB * t : SUB * t + SUB, :] = jnp.where(even, east, west)
            face_b[n, SUB * t : SUB * t + SUB, :] = jnp.where(even, west, east)


def unpack_faces(face_a, face_b, tiles, rim_west, rim_east):
    even = lax.rem(lax.axis_index("gx"), 2) == 0
    for n in range(5):
        for t in range(tiles + 1):
            a = face_a[n, SUB * t : SUB * t + SUB, :]
            b = face_b[n, SUB * t : SUB * t + SUB, :]
            west = jnp.where(even, b, a)
            east = jnp.where(even, a, b)
            low = SUB + SUB * t
            rim_west[n, low : low + SUB, :] = west
            rim_east[n, low : low + SUB, :] = east
            if t == tiles:
                rim_west[n, 0:SUB, :] = west
                rim_east[n, 0:SUB, :] = east


def streamed(relaxed, rim_west, rim_east, slabs, tiles, x, t, walls):
    lane, sub = lane_iota(), sub_iota()

    def rows(i, plane, low):
        if plane < 0:
            return rim_west[going_east.index(i), low : low + SUB, :]
        if plane >= slabs:
            return rim_east[going_west.index(i), low : low + SUB, :]
        return relaxed[i, plane, low : low + SUB, :]

    low = SUB + SUB * t if t < tiles else 0
    high = SUB + SUB * tiles
    result = []
    for i in range(19):
        ex, ey, ez = (int(v) for v in velocities[i])
        plane = x - ex
        if t < tiles or ey == 0:
            source = rows(i, plane, low - ey)
        elif ey == 1:
            source = jnp.where(
                sub >= 4, pltpu.roll(rows(i, plane, 0), 1, 0), rows(i, plane, high - 1)
            )
        else:
            source = jnp.where(
                sub >= 4, rows(i, plane, 1), pltpu.roll(rows(i, plane, high), SUB - 1, 0)
            )
        outside = None
        if ez == 1:
            source = pltpu.roll(source, 1, 1)
            outside = lane == 0
        elif ez == -1:
            source = pltpu.roll(source, LANES - 1, 1)
            outside = lane == LANES - 1
        wall = None
        if t == 0 and ey == 1:
            wall = (sub == 0) & walls[0]
        if t == tiles - 1 and ey == -1:
            wall = (sub == SUB - 1) & walls[1]
        if wall is not None:
            outside = wall if outside is None else outside | wall
        if outside is not None:
            source = jnp.where(outside, relaxed[opposite[i], x, low : low + SUB, :], source)
        result.append(source)
    return result


def wall_flags():
    strip = lax.axis_index("gy")
    return strip == 0, strip == lax.axis_size("gy") - 1


def first_kernel(
    capacity,
    got,
    populations,
    rim_a,
    rim_b,
    relaxed,
    face_a,
    face_b,
    forcing,
    listing,
    codes,
    arrived,
    placed,
    rim,
    spare,
    sem,
):
    slabs, strip_cells = populations.shape[1], populations.shape[2]
    tiles = strip_cells // SUB
    sources = got.shape[0]
    copy = pltpu.make_async_copy(got.at[:, 0, 0, :], codes, sem)
    copy.start()
    even = lax.rem(lax.axis_index("gy"), 2) == 0
    for i in range(19):
        for x in range(slabs):
            a, b = rim_a[i, x], rim_b[i, x]
            rim[i, x, 0:2, :] = jnp.where(even, a, b)
            rim[i, x, 6:8, :] = jnp.where(even, b, a)
    placed[...] = jnp.zeros_like(placed)

    def gather(s, _):
        for k in range(3):
            arrived[s, 4 * k : 4 * k + 4, :] = got[s, k]
        return 0

    lax.fori_loop(0, sources, gather, 0, unroll=4)
    copy.wait()

    def note(s, carry):
        own, dup = carry
        for r in range(capacity):
            code = codes[s, CODE_LANE + r].astype(jnp.int32)
            listing[1 + own] = (s * 4 + r) * 8192 + (code - 1)
            own = own + jnp.where(code > 0, 1, 0)
        for r in range(2 * capacity):
            code = codes[s, CODE_LANE + capacity + r].astype(jnp.int32)
            spare[dup] = (s * 8 + r) * 8192 + (code - 1)
            dup = dup + jnp.where(code > 0, 1, 0)
        return own, dup

    own_count, dup_count = lax.fori_loop(0, sources, note, (jnp.int32(0), jnp.int32(0)))
    listing[0] = own_count
    lane = lane_iota()

    def add_rows(source, y, z, lanes_at, row_list):
        inside = (lane >= z) & (lane < z + STEN)
        for h in range(2):
            tile = arrived[source, SUB * h : SUB * h + SUB, :]
            for step, b in row_list:
                shift = (z - lanes_at - STEN * step + 2 * LANES) & (LANES - 1)
                moved = jnp.where(inside, pltpu.roll(tile, shift, 1), 0.0)
                at = pl.multiple_of((y + b) * 16 + SUB * h, SUB)
                placed[pl.ds(at, SUB), :] = placed[pl.ds(at, SUB), :] + moved

    def place_own(n, _):
        item = listing[1 + n]
        slot, code = item >> 13, item & 8191
        add_rows(
            slot >> 2, code >> 7, code & (LANES - 1), GROUP * (slot & 3), [(b, b) for b in range(4)]
        )
        return 0

    lax.fori_loop(0, own_count, place_own, 0)

    def place_dup(n, _):
        item = spare[n]
        slot, code = item >> 13, item & 8191
        r = slot & 7
        south = r < capacity
        low = jnp.where(south, 2, 0)
        rank = jnp.where(south, r, r - capacity)
        add_rows(
            slot >> 3,
            (code >> 7) + low,
            code & (LANES - 1),
            GROUP * (capacity + rank) + STEN * low,
            [(0, 0), (1, 1)],
        )
        return 0

    lax.fori_loop(0, dup_count, place_dup, 0)
    sub = sub_iota()
    for x in range(slabs):
        for t in range(tiles + 1):
            push = []
            for k in range(3):
                if t < tiles:
                    value = placed[pl.ds((SUB + SUB * t) * 16 + 4 * k + x, SUB, stride=16), :]
                else:
                    value = jnp.where(
                        sub >= 4,
                        placed[pl.ds(4 * k + x, SUB, stride=16), :],
                        placed[pl.ds((SUB + SUB * tiles) * 16 + 4 * k + x, SUB, stride=16), :],
                    )
                forcing[k, x, SUB * t : SUB * t + SUB, :] = value
                push.append(value)
            if t < tiles:
                fields = [populations[i, x, SUB * t : SUB * t + SUB, :] for i in range(19)]
            else:
                fields = [rim[i, x] for i in range(19)]
            keep_tile(relaxed, tiles, x, t, collided(fields, push))
    write_faces(relaxed, slabs, tiles, face_a, face_b)


def second_kernel(before, got_a, got_b, forcing, relaxed, face_a, face_b, rim_west, rim_east):
    slabs = before.shape[1]
    tiles = before.shape[2] // SUB - 2
    unpack_faces(got_a, got_b, tiles, rim_west, rim_east)
    walls = wall_flags()
    for x in range(slabs):
        for t in range(tiles + 1):
            fields = streamed(before, rim_west, rim_east, slabs, tiles, x, t, walls)
            push = [forcing[k, x, SUB * t : SUB * t + SUB, :] for k in range(3)]
            keep_tile(relaxed, tiles, x, t, collided(fields, push))
    write_faces(relaxed, slabs, tiles, face_a, face_b)


def third_kernel(
    listing, before, got_a, got_b, forcing, populations, speeds, rim_west, rim_east, fluid, picked
):
    slabs = before.shape[1]
    tiles = before.shape[2] // SUB - 2
    unpack_faces(got_a, got_b, tiles, rim_west, rim_east)
    picked[...] = jnp.zeros_like(picked)
    walls = wall_flags()
    for x in range(slabs):
        for t in range(tiles):
            fields = streamed(before, rim_west, rim_east, slabs, tiles, x, t, walls)
            density = fields[0]
            for i in range(1, 19):
                density = density + fields[i]
            inverse = 1.0 / density
            for i in range(19):
                populations[i, x, SUB * t : SUB * t + SUB, :] = fields[i]
            for k in range(3):
                total = 0.5 * forcing[k, x, SUB * t : SUB * t + SUB, :]
                for i in range(19):
                    if velocities[i, k] == 1:
                        total = total + fields[i]
                    elif velocities[i, k] == -1:
                        total = total - fields[i]
                fluid[pl.ds(SUB * t * 16 + 4 * k + x, SUB, stride=16), :] = total * inverse
    lane = lane_iota()

    def pick(n, _):
        item = listing[1 + n]
        slot, code = item >> 13, item & 8191
        y, z = (code >> 7) - SUB, code & (LANES - 1)
        source, at = slot >> 2, GROUP * (slot & 3)
        for h in range(2):
            tile = picked[source, SUB * h : SUB * h + SUB, :]
            for b in range(4):
                low = at + STEN * b
                row = pl.multiple_of((y + b) * 16 + SUB * h, SUB)
                moved = pltpu.roll(fluid[pl.ds(row, SUB), :], (low - z + LANES) & (LANES - 1), 1)
                tile = jnp.where((lane >= low) & (lane < low + STEN), moved, tile)
            picked[source, SUB * h : SUB * h + SUB, :] = tile
        return 0

    lax.fori_loop(0, listing[0], pick, 0)
    speeds[...] = picked[...].astype(jnp.bfloat16)


def marker_kernel(
    owner, swimmer, returned, weights, velocity, total, wide, expanded, sums, count
):
    held = weights.shape[0]
    cells = weights.shape[1]
    targets = returned.shape[0]
    lane, sub = lane_iota(16), sub_iota(16)

    def reset(i, _):
        count[i] = 0
        return 0

    lax.fori_loop(0, targets, reset, 0, unroll=8)
    sums[...] = jnp.zeros_like(sums)
    chosen = (lane // GROUP) % 4 == sub % 4

    def widen(s, _):
        wide[s] = returned[s].astype(jnp.float32)
        return 0

    lax.fori_loop(0, targets, widen, 0, unroll=4)

    def expand(b, _):
        target = owner[b, 0]
        rank = count[target]
        count[target] = rank + 1
        low = GROUP * rank
        tile = jnp.where((lane >= low) & (lane < low + GROUP), wide[target], 0.0)
        tile = tile + pltpu.roll(tile, 64, 1)
        tile = tile + pltpu.roll(tile, 32, 1)
        tile = tile + pltpu.roll(tile, 16, 1)
        expanded[pl.ds(pl.multiple_of(b * 16, 16), 16), :] = jnp.where(chosen, tile, 0.0)
        return 0

    lax.fori_loop(0, held, expand, 0)
    sub8, lane8 = sub_iota(), lane_iota()

    def group_step(g, _):
        pieces = []
        for k in range(3):
            row = None
            for x in range(4):
                part = expanded[pl.ds(g * 128 + 4 * k + x, SUB, stride=16), :]
                row = part if row is None else row + part
            pieces.append(
                jnp.concatenate(
                    [
                        jnp.where(sub8 == 2 * pair + lane8 // 64, row, 0.0).astype(jnp.bfloat16)
                        for pair in range(4)
                    ],
                    axis=1,
                )
            )
        left = jnp.concatenate(pieces, axis=0)
        right = weights[pl.ds(g * SUB, SUB)].reshape(SUB * cells, LANES)
        out = speed_scale * jnp.dot(left, right, preferred_element_type=jnp.float32)
        for k in range(3):
            for j in range(SUB):
                velocity[g * SUB + j, k : k + 1, :] = out[SUB * k + j : SUB * k + j + 1, :]
        return 0

    lax.fori_loop(0, held // SUB, group_step, 0)

    def add_up(b, _):
        s = lax.rem(swimmer[b], SWIM_DEV)
        sums[s, 0:3, :] = sums[s, 0:3, :] + velocity[b]
        return 0

    lax.fori_loop(0, held, add_up, 0)
    columns = jnp.zeros((SUB, LANES), jnp.float32)
    for s in range(SWIM_DEV):
        mean = jnp.sum(sums[s], axis=1, keepdims=True) * (1.0 / LANES)
        columns = jnp.where(lane8 == s, mean, columns)
    total[...] = columns[0:3, 0:SWIM_DEV]


VM = pl.BlockSpec(memory_space=pltpu.VMEM)
SM = pl.BlockSpec(memory_space=pltpu.SMEM)


def shaped(shape, dtype=jnp.float32):
    return jax.ShapeDtypeStruct(shape, dtype)


def body(populations, marker_weights, marker_force, owner_device, stencil_base, block_swimmer):
    slab_cells, strip_cells, height = populations.shape[1:]
    strips = lax.axis_size("gy")
    devices = lax.axis_size("gx") * strips
    held = marker_weights.shape[0]
    capacity = max(2, (2 * held + devices - 1) // devices)
    tiles = strip_cells // SUB
    padded_rows = strip_cells + 2 * SUB
    packed_rows = strip_cells + SUB
    f32 = jnp.float32

    even = lax.rem(lax.axis_index("gy"), 2) == 0
    top = populations[:, :, strip_cells - 2 :, :]
    bottom = populations[:, :, :2, :]
    rim_a, rim_b = swapped(
        jnp.where(even, top, bottom), jnp.where(even, bottom, top), "gy", False
    )
    sent = pl.pallas_call(
        functools.partial(patch_kernel, capacity, strips, strip_cells),
        out_shape=shaped((devices * 3, 4, LANES)),
        in_specs=[SM, SM, VM, VM],
        out_specs=VM,
        scratch_shapes=[
            pltpu.VMEM((64, LANES), f32),
            pltpu.VMEM((held, 16, LANES), f32),
            pltpu.SMEM((devices,), jnp.int32),
        ],
        name="patches",
    )(owner_device, stencil_base, marker_weights, marker_force)
    got = lax.all_to_all(sent, ("gx", "gy"), split_axis=0, concat_axis=0, tiled=True)
    got = got.reshape(devices, 3, 4, LANES)

    planes = shaped((19, slab_cells, padded_rows, height))
    face = shaped((5, packed_rows, height))
    push = shaped((3, slab_cells, packed_rows, height))
    rims = [pltpu.VMEM((5, padded_rows, height), f32)] * 2
    relaxed, face_a, face_b, forcing, listing = pl.pallas_call(
        functools.partial(first_kernel, capacity),
        out_shape=(planes, face, face, push, shaped((devices * capacity + 2,), jnp.int32)),
        in_specs=[VM] * 4,
        out_specs=(VM, VM, VM, VM, SM),
        scratch_shapes=[
            pltpu.SMEM((devices, LANES), f32),
            pltpu.VMEM((devices, 16, LANES), f32),
            pltpu.VMEM((padded_rows * 16, LANES), f32),
            pltpu.VMEM((19, slab_cells, SUB, LANES), f32),
            pltpu.SMEM((devices * 2 * capacity + 1,), jnp.int32),
            pltpu.SemaphoreType.DMA,
        ],
        name="first",
    )(got, populations, rim_a, rim_b)
    got_a, got_b = swapped(face_a, face_b, "gx", True)
    relaxed, face_a, face_b = pl.pallas_call(
        second_kernel,
        out_shape=(planes, face, face),
        in_specs=[VM] * 4,
        out_specs=(VM, VM, VM),
        scratch_shapes=rims,
        name="second",
    )(relaxed, got_a, got_b, forcing)
    got_a, got_b = swapped(face_a, face_b, "gx", True)
    fields, speeds = pl.pallas_call(
        third_kernel,
        out_shape=(shaped(populations.shape), shaped((devices, 16, LANES), jnp.bfloat16)),
        in_specs=[SM, VM, VM, VM, VM],
        out_specs=(VM, VM),
        scratch_shapes=rims
        + [pltpu.VMEM((strip_cells * 16, LANES), f32), pltpu.VMEM((devices, 16, LANES), f32)],
        name="third",
    )(listing, relaxed, got_a, got_b, forcing)
    returned = lax.all_to_all(speeds, ("gx", "gy"), split_axis=0, concat_axis=0, tiled=True)
    marker_velocity, swimmer_velocity = pl.pallas_call(
        marker_kernel,
        out_shape=(shaped((held, 3, LANES)), shaped((3, SWIM_DEV))),
        in_specs=[SM, SM, VM, VM],
        out_specs=(VM, VM),
        scratch_shapes=[
            pltpu.VMEM((devices, 16, LANES), f32),
            pltpu.VMEM((held * 16, LANES), f32),
            pltpu.VMEM((SWIM_DEV, SUB, LANES), f32),
            pltpu.SMEM((devices,), jnp.int32),
        ],
        name="markers",
    )(owner_device, block_swimmer, returned, marker_weights)
    return fields, marker_velocity, swimmer_velocity


def solution(mesh):
    in_specs = (
        P(None, "gx", "gy", None),
        P(("gx", "gy"), None, None),
        P(("gx", "gy"), None, None),
        P(("gx", "gy"), None),
        P(("gx", "gy"), None),
        P(("gx", "gy")),
    )
    out_specs = (P(None, "gx", "gy", None), P(("gx", "gy"), None, None), P(None, ("gx", "gy")))
    return jax.shard_map(body, mesh=mesh, in_specs=in_specs, out_specs=out_specs, check_vma=False)
```

```python
import functools

import jax
import jax.numpy as jnp
import numpy as np
from jax import lax
from jax.experimental import pallas as pl
from jax.experimental.pallas import tpu as pltpu
from jax.sharding import PartitionSpec as P

STEN = 4
SWIM_DEV = 4
LANES = 128
SUB = 8
GROUP = STEN * STEN
CODE_LANE = 96
STEP = 4

velocities = np.array(
    [
        [0, 0, 0],
        [1, 0, 0],
        [-1, 0, 0],
        [0, 1, 0],
        [0, -1, 0],
        [0, 0, 1],
        [0, 0, -1],
        [1, 1, 0],
        [-1, -1, 0],
        [1, -1, 0],
        [-1, 1, 0],
        [1, 0, 1],
        [-1, 0, -1],
        [1, 0, -1],
        [-1, 0, 1],
        [0, 1, 1],
        [0, -1, -1],
        [0, 1, -1],
        [0, -1, 1],
    ]
)
opposite = [0, 2, 1, 4, 3, 6, 5, 8, 7, 10, 9, 12, 11, 14, 13, 16, 15, 18, 17]
lattice_weights = [1.0 / 3.0] + [1.0 / 18.0] * 6 + [1.0 / 36.0] * 12
relax_time = 0.8
speed_scale = 20.0
going_east = [1, 7, 9, 11, 13]
going_west = [2, 8, 10, 12, 14]


def lane_iota(rows=SUB):
    return lax.broadcasted_iota(jnp.int32, (rows, LANES), 1)


def sub_iota(rows=SUB):
    return lax.broadcasted_iota(jnp.int32, (rows, LANES), 0)


def swapped(first, second, axis, periodic):
    size = lax.axis_size(axis)
    inner = [(i, i ^ 1) for i in range(size)]
    outer = []
    for i in range(size):
        j = i + 1 if i % 2 == 1 else i - 1
        if periodic:
            outer.append((i, j % size))
        elif 0 <= j < size:
            outer.append((i, j))
    return lax.ppermute(first, axis, inner), lax.ppermute(second, axis, outer)


def patch_kernel(
    capacity, strips, strip_cells, owner, base, weights, force, send, rows, spread, patches, count, again
):
    held = weights.shape[0]
    cells = weights.shape[1]
    targets = send.shape[0] // 3
    lane, sub = lane_iota(16), sub_iota(16)

    def clear(i, _):
        send[i] = jnp.zeros((4, LANES), jnp.float32)
        return 0

    lax.fori_loop(0, send.shape[0], clear, 0, unroll=16)

    def reset(i, _):
        count[i] = 0
        return 0

    lax.fori_loop(0, targets, reset, 0, unroll=16)
    for k in range(3):
        rows[k] = force[k].astype(jnp.float32)
    for b in range(held):
        for k in range(3):
            spread[16 * b + 4 * k : 16 * b + 4 * k + 4, :] = jnp.broadcast_to(
                rows[k, b : b + 1, :], (4, LANES)
            )
        spread[16 * b + 12 : 16 * b + 16, :] = jnp.zeros((4, LANES), jnp.float32)
    for g in range(held // 4):
        out = lax.dot_general(
            spread[64 * g : 64 * g + 64, :].astype(jnp.bfloat16),
            weights[4 * g : 4 * g + 4].reshape(4 * cells, LANES),
            (((1,), (1,)), ((), ())),
            preferred_element_type=jnp.float32,
        )
        for j in range(4):
            half = j // 2
            part = out[16 * j : 16 * j + 16, LANES * half : LANES * half + LANES]
            part = jnp.where(lane // GROUP == 4 * (j % 2) + sub % 4, part, 0.0)
            part = part + pltpu.roll(part, 64, 1)
            part = part + pltpu.roll(part, 32, 1)
            part = part + pltpu.roll(part, 16, 1)
            patches[g * 4 + j] = part
    lane4, sub4 = lane_iota(4), sub_iota(4)

    def put(dest, tiles, low, wide, code_at, frame_y, z):
        code = ((frame_y + SUB) * LANES + z + 1).astype(jnp.float32)
        inside = (lane4 >= low) & (lane4 < low + wide)
        for k in range(3):
            tile = jnp.where(inside, tiles[k], send[dest * 3 + k])
            if k == 0:
                tile = jnp.where((sub4 == 0) & (lane4 == code_at), code, tile)
            send[dest * 3 + k] = tile

    def block_tiles(b):
        return [patches[b, 4 * k : 4 * k + 4, :] for k in range(3)]

    extra = jnp.int32(0)
    for b in range(held):
        target = owner[0, b]
        rank = count[target]
        count[target] = rank + 1
        y, z = base[1, b], base[2, b]
        put(target, block_tiles(b), GROUP * rank, GROUP, CODE_LANE + rank, y, z)
        strip = lax.rem(target, strips)
        north = (y >= strip_cells - 5) & (strip < strips - 1)
        south = (y <= 1) & (strip > 0)
        again[extra] = b * 4 + rank
        extra = extra + jnp.where(north | south, 1, 0)

    def put_again(n, _):
        item = again[n]
        b, rank = item >> 2, item & 3
        target, y, z = owner[0, b], base[1, b], base[2, b]
        south = y <= 1
        put(
            target + jnp.where(south, -1, 1),
            block_tiles(b),
            GROUP * (capacity + rank) + jnp.where(south, 0, 8),
            8,
            CODE_LANE + capacity + rank + jnp.where(south, capacity, 0),
            y + jnp.where(south, strip_cells, -strip_cells),
            z,
        )
        return 0

    lax.fori_loop(0, extra, put_again, 0)


def collided(fields, forcing):
    pair_sum, pair_diff = {}, {}
    for i in range(1, 19, 2):
        pair_sum[i] = fields[i] + fields[i + 1]
        pair_diff[i] = fields[i] - fields[i + 1]
    density = fields[0]
    for i in range(1, 19, 2):
        density = density + pair_sum[i]
    momentum = []
    for k in range(3):
        total = relax_time * forcing[k]
        for i in range(1, 19, 2):
            if velocities[i, k] == 1:
                total = total + pair_diff[i]
            elif velocities[i, k] == -1:
                total = total - pair_diff[i]
        momentum.append(total)
    inverse = 1.0 / density
    keep = 1.0 - 1.0 / relax_time
    squares = momentum[0] * momentum[0] + momentum[1] * momentum[1] + momentum[2] * momentum[2]
    level = density - 1.5 * inverse * squares
    curve = 4.5 * inverse
    result = [None] * 19
    result[0] = keep * fields[0] + (lattice_weights[0] / relax_time) * level
    for i in range(1, 19, 2):
        along = None
        for k in range(3):
            if velocities[i, k] == 1:
                along = momentum[k] if along is None else along + momentum[k]
            elif velocities[i, k] == -1:
                along = -momentum[k] if along is None else along - momentum[k]
        share = lattice_weights[i] / relax_time
        even = share * (level + curve * along * along)
        odd = (3.0 * share) * along
        result[i] = keep * fields[i] + (even + odd)
        result[i + 1] = keep * fields[i + 1] + (even - odd)
    return result


def keep_tile(relaxed, tiles, x, t, values):
    for i in range(19):
        if t < tiles:
            relaxed[i, x, SUB + SUB * t : 2 * SUB + SUB * t, :] = values[i]
        else:
            relaxed[i, x, 0:SUB, :] = values[i]
            relaxed[i, x, SUB + SUB * tiles : 2 * SUB + SUB * tiles, :] = values[i]


def write_faces(relaxed, slabs, tiles, face_a, face_b):
    even = lax.rem(lax.axis_index("gx"), 2) == 0
    for n in range(5):
        for t in range(tiles + 1):
            low = SUB + SUB * t
            east = relaxed[going_east[n], slabs - 1, low : low + SUB, :]
            west = relaxed[going_west[n], 0, low : low + SUB, :]
            face_a[n, SUB * t : SUB * t + SUB, :] = jnp.where(even, east, west)
            face_b[n, SUB * t : SUB * t + SUB, :] = jnp.where(even, west, east)


def unpack_faces(face_a, face_b, tiles, rim_west, rim_east):
    even = lax.rem(lax.axis_index("gx"), 2) == 0
    for n in range(5):
        for t in range(tiles + 1):
            a = face_a[n, SUB * t : SUB * t + SUB, :]
            b = face_b[n, SUB * t : SUB * t + SUB, :]
            west = jnp.where(even, b, a)
            east = jnp.where(even, a, b)
            low = SUB + SUB * t
            rim_west[n, low : low + SUB, :] = west
            rim_east[n, low : low + SUB, :] = east
            if t == tiles:
                rim_west[n, 0:SUB, :] = west
                rim_east[n, 0:SUB, :] = east


def streamed(relaxed, rim_west, rim_east, slabs, tiles, x, t, walls):
    lane, sub = lane_iota(), sub_iota()

    def rows(i, plane, low):
        if plane < 0:
            return rim_west[going_east.index(i), low : low + SUB, :]
        if plane >= slabs:
            return rim_east[going_west.index(i), low : low + SUB, :]
        return relaxed[i, plane, low : low + SUB, :]

    low = SUB + SUB * t if t < tiles else 0
    high = SUB + SUB * tiles
    result = []
    for i in range(19):
        ex, ey, ez = (int(v) for v in velocities[i])
        plane = x - ex
        if t < tiles or ey == 0:
            source = rows(i, plane, low - ey)
        elif ey == 1:
            source = jnp.where(
                sub >= 4, pltpu.roll(rows(i, plane, 0), 1, 0), rows(i, plane, high - 1)
            )
        else:
            source = jnp.where(
                sub >= 4, rows(i, plane, 1), pltpu.roll(rows(i, plane, high), SUB - 1, 0)
            )
        outside = None
        if ez == 1:
            source = pltpu.roll(source, 1, 1)
            outside = lane == 0
        elif ez == -1:
            source = pltpu.roll(source, LANES - 1, 1)
            outside = lane == LANES - 1
        wall = None
        if t == 0 and ey == 1:
            wall = (sub == 0) & walls[0]
        if t == tiles - 1 and ey == -1:
            wall = (sub == SUB - 1) & walls[1]
        if wall is not None:
            outside = wall if outside is None else outside | wall
        if outside is not None:
            source = jnp.where(outside, relaxed[opposite[i], x, low : low + SUB, :], source)
        result.append(source)
    return result


def wall_flags():
    strip = lax.axis_index("gy")
    return strip == 0, strip == lax.axis_size("gy") - 1


def first_kernel(
    capacity,
    got,
    populations,
    rim_a,
    rim_b,
    relaxed,
    face_a,
    face_b,
    forcing,
    corners,
    codes,
    arrived,
    placed,
    rim,
    listing,
    spare,
    sem,
):
    slabs, strip_cells = populations.shape[1], populations.shape[2]
    tiles = strip_cells // SUB
    sources = got.shape[0]
    copy = pltpu.make_async_copy(got.at[:, 0, 0, :], codes, sem)
    copy.start()
    even = lax.rem(lax.axis_index("gy"), 2) == 0
    for i in range(19):
        for x in range(slabs):
            a, b = rim_a[i, x], rim_b[i, x]
            rim[i, x, 0:2, :] = jnp.where(even, a, b)
            rim[i, x, 6:8, :] = jnp.where(even, b, a)
    placed[...] = jnp.zeros_like(placed)
    arrived[sources] = jnp.zeros((16, LANES), jnp.float32)

    def gather(s, _):
        for k in range(3):
            arrived[s, 4 * k : 4 * k + 4, :] = got[s, k]
        return 0

    lax.fori_loop(0, sources, gather, 0, unroll=8)
    copy.wait()
    nowhere = SUB * LANES

    def note(s, carry):
        own, dup = carry
        for r in range(capacity):
            code = codes[s, CODE_LANE + r].astype(jnp.int32)
            corners[s * capacity + r] = jnp.maximum(code - 1, nowhere)
            listing[own] = (s * 4 + r) * 8192 + (code - 1)
            own = own + jnp.where(code > 0, 1, 0)
        for r in range(2 * capacity):
            code = codes[s, CODE_LANE + capacity + r].astype(jnp.int32)
            spare[dup] = (s * 8 + r) * 8192 + (code - 1)
            dup = dup + jnp.where(code > 0, 1, 0)
        return own, dup

    own_count, dup_count = lax.fori_loop(
        0, sources, note, (jnp.int32(0), jnp.int32(0)), unroll=4
    )
    for j in range(STEP - 1):
        listing[own_count + j] = sources * 4 * 8192 + nowhere
    lane = lane_iota()

    def moved_rows(source, z, lanes_at, steps):
        inside = (lane >= z) & (lane < z + STEN)
        rows = {}
        for h in range(2):
            tile = arrived[source, SUB * h : SUB * h + SUB, :]
            for b in range(steps):
                shift = (z - lanes_at - STEN * b + 2 * LANES) & (LANES - 1)
                rows[b, h] = jnp.where(inside, pltpu.roll(tile, shift, 1), 0.0)
        return rows

    def add_rows(rows, y):
        at = {
            (b, h): pl.ds(pl.multiple_of((y + b) * 16 + SUB * h, SUB), SUB) for b, h in rows
        }
        old = {key: placed[at[key], :] for key in rows}
        for key in rows:
            placed[at[key], :] = old[key] + rows[key]

    def place_own(n, _):
        todo = []
        for j in range(STEP):
            item = listing[STEP * n + j]
            slot, code = item >> 13, item & 8191
            todo.append(
                (moved_rows(slot >> 2, code & (LANES - 1), GROUP * (slot & 3), 4), code >> 7)
            )
        for rows, y in todo:
            add_rows(rows, y)
        return 0

    lax.fori_loop(0, (own_count + STEP - 1) // STEP, place_own, 0)

    def place_dup(n, _):
        item = spare[n]
        slot, code = item >> 13, item & 8191
        r = slot & 7
        south = r < capacity
        low = jnp.where(south, 2, 0)
        rank = jnp.where(south, r, r - capacity)
        rows = moved_rows(
            slot >> 3, code & (LANES - 1), GROUP * (capacity + rank) + STEN * low, 2
        )
        add_rows(rows, (code >> 7) + low)
        return 0

    lax.fori_loop(0, dup_count, place_dup, 0)
    sub = sub_iota()
    for x in range(slabs):
        for t in range(tiles + 1):
            push = []
            for k in range(3):
                if t < tiles:
                    value = placed[pl.ds((SUB + SUB * t) * 16 + 4 * k + x, SUB, stride=16), :]
                else:
                    value = jnp.where(
                        sub >= 4,
                        placed[pl.ds(4 * k + x, SUB, stride=16), :],
                        placed[pl.ds((SUB + SUB * tiles) * 16 + 4 * k + x, SUB, stride=16), :],
                    )
                forcing[k, x, SUB * t : SUB * t + SUB, :] = value
                push.append(value)
            if t < tiles:
                fields = [populations[i, x, SUB * t : SUB * t + SUB, :] for i in range(19)]
            else:
                fields = [rim[i, x] for i in range(19)]
            keep_tile(relaxed, tiles, x, t, collided(fields, push))
    write_faces(relaxed, slabs, tiles, face_a, face_b)


def second_kernel(before, got_a, got_b, forcing, relaxed, face_a, face_b, rim_west, rim_east):
    slabs = before.shape[1]
    tiles = before.shape[2] // SUB - 2
    unpack_faces(got_a, got_b, tiles, rim_west, rim_east)
    walls = wall_flags()
    for x in range(slabs):
        for t in range(tiles + 1):
            fields = streamed(before, rim_west, rim_east, slabs, tiles, x, t, walls)
            push = [forcing[k, x, SUB * t : SUB * t + SUB, :] for k in range(3)]
            keep_tile(relaxed, tiles, x, t, collided(fields, push))
    write_faces(relaxed, slabs, tiles, face_a, face_b)


def third_kernel(
    capacity, corners, before, got_a, got_b, forcing, populations, speeds, rim_west, rim_east, fluid
):
    slabs = before.shape[1]
    tiles = before.shape[2] // SUB - 2
    unpack_faces(got_a, got_b, tiles, rim_west, rim_east)
    walls = wall_flags()
    for x in range(slabs):
        for t in range(tiles):
            fields = streamed(before, rim_west, rim_east, slabs, tiles, x, t, walls)
            density = fields[0]
            for i in range(1, 19):
                density = density + fields[i]
            inverse = 1.0 / density
            for i in range(19):
                populations[i, x, SUB * t : SUB * t + SUB, :] = fields[i]
            for k in range(3):
                total = 0.5 * forcing[k, x, SUB * t : SUB * t + SUB, :]
                for i in range(19):
                    if velocities[i, k] == 1:
                        total = total + fields[i]
                    elif velocities[i, k] == -1:
                        total = total - fields[i]
                fluid[pl.ds(SUB * t * 16 + 4 * k + x, SUB, stride=16), :] = total * inverse
    lane = lane_iota()

    def pick(s, _):
        corner = [corners[s * capacity + r] for r in range(capacity)]
        halves = []
        for h in range(2):
            tile = jnp.zeros((SUB, LANES), jnp.float32)
            for r in range(capacity):
                y, z = (corner[r] >> 7) - SUB, corner[r] & (LANES - 1)
                for b in range(4):
                    low = GROUP * r + STEN * b
                    row = pl.multiple_of((y + b) * 16 + SUB * h, SUB)
                    shift = (low - z + LANES) & (LANES - 1)
                    moved = pltpu.roll(fluid[pl.ds(row, SUB), :], shift, 1)
                    tile = jnp.where((lane >= low) & (lane < low + STEN), moved, tile)
            halves.append(tile)
        speeds[s] = jnp.concatenate(halves, axis=0).astype(jnp.bfloat16)
        return 0

    lax.fori_loop(0, speeds.shape[0], pick, 0, unroll=4)


def marker_kernel(
    owner, swimmer, returned, weights, velocity, total, chosen, expanded, count
):
    held = weights.shape[0]
    cells = weights.shape[1]
    targets = returned.shape[0]
    lane, sub = lane_iota(16), sub_iota(16)

    def reset(i, _):
        count[i] = 0
        return 0

    lax.fori_loop(0, targets, reset, 0, unroll=16)
    for b in range(held):
        target = owner[0, b]
        rank = count[target]
        count[target] = rank + 1
        low = GROUP * rank
        tile = returned[target].astype(jnp.float32)
        tile = jnp.where((lane >= low) & (lane < low + GROUP), tile, 0.0)
        chosen[16 * b : 16 * b + 16, :] = tile.astype(jnp.bfloat16)
    across = lax.broadcasted_iota(jnp.int32, (LANES, LANES), 1)
    down = lax.broadcasted_iota(jnp.int32, (LANES, LANES), 0)
    repeat = jnp.where(across % GROUP == down % GROUP, 1.0, 0.0).astype(jnp.bfloat16)
    own_cells = (lane // GROUP) % 4 == sub % 4
    for g in range(held // SUB):
        wide = jnp.dot(
            chosen[LANES * g : LANES * g + LANES, :], repeat, preferred_element_type=jnp.float32
        )
        for j in range(SUB):
            expanded[LANES * g + 16 * j : LANES * g + 16 * j + 16, :] = jnp.where(
                own_cells, wide[16 * j : 16 * j + 16, :], 0.0
            )
    sub8, lane8 = sub_iota(), lane_iota()
    sums = {}
    for g in range(held // SUB):
        pieces = []
        for k in range(3):
            row = None
            for x in range(4):
                part = expanded[pl.ds(LANES * g + 4 * k + x, SUB, stride=16), :]
                row = part if row is None else row + part
            pieces.append(
                jnp.concatenate(
                    [
                        jnp.where(sub8 == 2 * pair + lane8 // 64, row, 0.0).astype(jnp.bfloat16)
                        for pair in range(4)
                    ],
                    axis=1,
                )
            )
        left = jnp.concatenate(pieces, axis=0)
        right = weights[SUB * g : SUB * g + SUB].reshape(SUB * cells, LANES)
        out = speed_scale * jnp.dot(left, right, preferred_element_type=jnp.float32)
        member = jnp.zeros((SUB, LANES), jnp.int32)
        for j in range(SUB):
            member = jnp.where(sub8 == j, lax.rem(swimmer[SUB * g + j], SWIM_DEV), member)
        for k in range(3):
            part = out[SUB * k : SUB * k + SUB, :]
            velocity[k, SUB * g : SUB * g + SUB, :] = part
            for s in range(SWIM_DEV):
                term = jnp.where(member == s, part, 0.0)
                sums[k, s] = term if g == 0 else sums[k, s] + term
    table = jnp.zeros((SUB, LANES), jnp.float32)
    for (k, s), value in sums.items():
        mean = jnp.sum(value) * (1.0 / LANES)
        table = jnp.where((sub8 == k) & (lane8 == s), mean, table)
    total[...] = table[0:3, 0:SWIM_DEV]


VM = pl.BlockSpec(memory_space=pltpu.VMEM)
SM = pl.BlockSpec(memory_space=pltpu.SMEM)


def shaped(shape, dtype=jnp.float32):
    return jax.ShapeDtypeStruct(shape, dtype)


def body(populations, marker_weights, marker_force, owner_device, stencil_base, block_swimmer):
    slab_cells, strip_cells, height = populations.shape[1:]
    strips = lax.axis_size("gy")
    devices = lax.axis_size("gx") * strips
    held = marker_weights.shape[0]
    capacity = max(2, (2 * held + devices - 1) // devices)
    tiles = strip_cells // SUB
    padded_rows = strip_cells + 2 * SUB
    packed_rows = strip_cells + SUB
    f32 = jnp.float32
    small = pltpu.CompilerParams(vmem_limit_bytes=12 * 1024 * 1024)

    even = lax.rem(lax.axis_index("gy"), 2) == 0
    top = populations[:, :, strip_cells - 2 :, :]
    bottom = populations[:, :, :2, :]
    rim_a, rim_b = swapped(
        jnp.where(even, top, bottom), jnp.where(even, bottom, top), "gy", False
    )
    owner = owner_device.T
    sent = pl.pallas_call(
        functools.partial(patch_kernel, capacity, strips, strip_cells),
        out_shape=shaped((devices * 3, 4, LANES)),
        in_specs=[SM, SM, VM, VM],
        out_specs=VM,
        scratch_shapes=[
            pltpu.VMEM((3, held, LANES), f32),
            pltpu.VMEM((held * 16, LANES), f32),
            pltpu.VMEM((held, 16, LANES), f32),
            pltpu.SMEM((devices,), jnp.int32),
            pltpu.SMEM((held + 1,), jnp.int32),
        ],
        compiler_params=small,
        name="patches",
    )(owner, stencil_base.T, marker_weights, marker_force.transpose(1, 0, 2))
    got = lax.all_to_all(sent, ("gx", "gy"), split_axis=0, concat_axis=0, tiled=True)
    got = got.reshape(devices, 3, 4, LANES)

    planes = shaped((19, slab_cells, padded_rows, height))
    face = shaped((5, packed_rows, height))
    push = shaped((3, slab_cells, packed_rows, height))
    rims = [pltpu.VMEM((5, padded_rows, height), f32)] * 2
    relaxed, face_a, face_b, forcing, corners = pl.pallas_call(
        functools.partial(first_kernel, capacity),
        out_shape=(planes, face, face, push, shaped((devices * capacity,), jnp.int32)),
        in_specs=[VM] * 4,
        out_specs=(VM, VM, VM, VM, SM),
        scratch_shapes=[
            pltpu.SMEM((devices, LANES), f32),
            pltpu.VMEM((devices + 1, 16, LANES), f32),
            pltpu.VMEM((padded_rows * 16, LANES), f32),
            pltpu.VMEM((19, slab_cells, SUB, LANES), f32),
            pltpu.SMEM((devices * capacity + STEP,), jnp.int32),
            pltpu.SMEM((devices * 2 * capacity + 1,), jnp.int32),
            pltpu.SemaphoreType.DMA,
        ],
        compiler_params=small,
        name="first",
    )(got, populations, rim_a, rim_b)
    got_a, got_b = swapped(face_a, face_b, "gx", True)
    relaxed, face_a, face_b = pl.pallas_call(
        second_kernel,
        out_shape=(planes, face, face),
        in_specs=[VM] * 4,
        out_specs=(VM, VM, VM),
        scratch_shapes=rims,
        compiler_params=small,
        name="second",
    )(relaxed, got_a, got_b, forcing)
    got_a, got_b = swapped(face_a, face_b, "gx", True)
    fields, speeds = pl.pallas_call(
        functools.partial(third_kernel, capacity),
        out_shape=(shaped(populations.shape), shaped((devices, 16, LANES), jnp.bfloat16)),
        in_specs=[SM, VM, VM, VM, VM],
        out_specs=(VM, VM),
        scratch_shapes=rims + [pltpu.VMEM((strip_cells * 16, LANES), f32)],
        compiler_params=small,
        name="third",
    )(corners, relaxed, got_a, got_b, forcing)
    returned = lax.all_to_all(speeds, ("gx", "gy"), split_axis=0, concat_axis=0, tiled=True)
    marker_velocity, swimmer_velocity = pl.pallas_call(
        marker_kernel,
        out_shape=(shaped((3, held, LANES)), shaped((3, SWIM_DEV))),
        in_specs=[SM, SM, VM, VM],
        out_specs=(VM, VM),
        scratch_shapes=[
            pltpu.VMEM((held * 16, LANES), jnp.bfloat16),
            pltpu.VMEM((held * 16, LANES), f32),
            pltpu.SMEM((devices,), jnp.int32),
        ],
        compiler_params=small,
        name="markers",
    )(owner, block_swimmer, returned, marker_weights)
    return fields, marker_velocity.transpose(1, 0, 2), swimmer_velocity


def solution(mesh):
    in_specs = (
        P(None, "gx", "gy", None),
        P(("gx", "gy"), None, None),
        P(("gx", "gy"), None, None),
        P(("gx", "gy"), None),
        P(("gx", "gy"), None),
        P(("gx", "gy")),
    )
    out_specs = (P(None, "gx", "gy", None), P(("gx", "gy"), None, None), P(None, ("gx", "gy")))
    return jax.shard_map(body, mesh=mesh, in_specs=in_specs, out_specs=out_specs, check_vma=False)
```

```python
import functools

import jax
import jax.numpy as jnp
import numpy as np
from jax import lax
from jax.experimental import pallas as pl
from jax.experimental.pallas import tpu as pltpu
from jax.sharding import PartitionSpec as P

STEN = 4
SWIM_DEV = 4
LANES = 128
SUB = 8
GROUP = STEN * STEN
CODE_LANE = 96
STEP = 4

velocities = np.array(
    [
        [0, 0, 0],
        [1, 0, 0],
        [-1, 0, 0],
        [0, 1, 0],
        [0, -1, 0],
        [0, 0, 1],
        [0, 0, -1],
        [1, 1, 0],
        [-1, -1, 0],
        [1, -1, 0],
        [-1, 1, 0],
        [1, 0, 1],
        [-1, 0, -1],
        [1, 0, -1],
        [-1, 0, 1],
        [0, 1, 1],
        [0, -1, -1],
        [0, 1, -1],
        [0, -1, 1],
    ]
)
opposite = [0, 2, 1, 4, 3, 6, 5, 8, 7, 10, 9, 12, 11, 14, 13, 16, 15, 18, 17]
lattice_weights = [1.0 / 3.0] + [1.0 / 18.0] * 6 + [1.0 / 36.0] * 12
relax_time = 0.8
speed_scale = 20.0
going_east = [1, 7, 9, 11, 13]
going_west = [2, 8, 10, 12, 14]


def lane_iota(rows=SUB):
    return lax.broadcasted_iota(jnp.int32, (rows, LANES), 1)


def sub_iota(rows=SUB):
    return lax.broadcasted_iota(jnp.int32, (rows, LANES), 0)


def swapped(first, second, axis, periodic):
    size = lax.axis_size(axis)
    inner = [(i, i ^ 1) for i in range(size)]
    outer = []
    for i in range(size):
        j = i + 1 if i % 2 == 1 else i - 1
        if periodic:
            outer.append((i, j % size))
        elif 0 <= j < size:
            outer.append((i, j))
    return lax.ppermute(first, axis, inner), lax.ppermute(second, axis, outer)


def patch_kernel(
    capacity,
    strips,
    owner,
    base,
    weights_far,
    force,
    populations,
    send,
    rim_a,
    rim_b,
    weights,
    top,
    bottom,
    rows,
    spread,
    patches,
    count,
    again,
    sems,
):
    held = weights.shape[0]
    cells = weights.shape[1]
    strip_cells = populations.shape[2]
    pieces = sems.shape[0] - 2
    part_blocks = held // pieces
    copies = [
        pltpu.make_async_copy(
            weights_far.at[part_blocks * n : part_blocks * (n + 1)],
            weights.at[part_blocks * n : part_blocks * (n + 1)],
            sems.at[n],
        )
        for n in range(pieces)
    ]
    copies.append(
        pltpu.make_async_copy(populations.at[:, :, 0:SUB, :], bottom, sems.at[pieces])
    )
    copies.append(
        pltpu.make_async_copy(
            populations.at[:, :, strip_cells - SUB : strip_cells, :], top, sems.at[pieces + 1]
        )
    )
    for copy in copies:
        copy.start()
    targets = send.shape[0] // 3
    lane, sub = lane_iota(16), sub_iota(16)

    def clear(i, _):
        send[i] = jnp.zeros((4, LANES), jnp.float32)
        return 0

    lax.fori_loop(0, send.shape[0], clear, 0, unroll=16)

    def reset(i, _):
        count[i] = 0
        return 0

    lax.fori_loop(0, targets, reset, 0, unroll=16)
    for k in range(3):
        rows[k] = force[k].astype(jnp.float32)
    for b in range(held):
        for k in range(3):
            spread[16 * b + 4 * k : 16 * b + 4 * k + 4, :] = jnp.broadcast_to(
                rows[k, b : b + 1, :], (4, LANES)
            )
        spread[16 * b + 12 : 16 * b + 16, :] = jnp.zeros((4, LANES), jnp.float32)
    for g in range(held // 4):
        if 4 * g % part_blocks == 0:
            copies[4 * g // part_blocks].wait()
        out = lax.dot_general(
            spread[64 * g : 64 * g + 64, :].astype(jnp.bfloat16),
            weights[4 * g : 4 * g + 4].reshape(4 * cells, LANES),
            (((1,), (1,)), ((), ())),
            preferred_element_type=jnp.float32,
        )
        for j in range(4):
            half = j // 2
            part = out[16 * j : 16 * j + 16, LANES * half : LANES * half + LANES]
            part = jnp.where(lane // GROUP == 4 * (j % 2) + sub % 4, part, 0.0)
            part = part + pltpu.roll(part, 64, 1)
            part = part + pltpu.roll(part, 32, 1)
            part = part + pltpu.roll(part, 16, 1)
            patches[g * 4 + j] = part
    lane4, sub4 = lane_iota(4), sub_iota(4)

    def put(dest, tiles, low, wide, code_at, frame_y, z):
        code = ((frame_y + SUB) * LANES + z + 1).astype(jnp.float32)
        inside = (lane4 >= low) & (lane4 < low + wide)
        for k in range(3):
            tile = jnp.where(inside, tiles[k], send[dest * 3 + k])
            if k == 0:
                tile = jnp.where((sub4 == 0) & (lane4 == code_at), code, tile)
            send[dest * 3 + k] = tile

    def block_tiles(b):
        return [patches[b, 4 * k : 4 * k + 4, :] for k in range(3)]

    extra = jnp.int32(0)
    for b in range(held):
        target = owner[0, b]
        rank = count[target]
        count[target] = rank + 1
        y, z = base[1, b], base[2, b]
        put(target, block_tiles(b), GROUP * rank, GROUP, CODE_LANE + rank, y, z)
        strip = lax.rem(target, strips)
        north = (y >= strip_cells - 5) & (strip < strips - 1)
        south = (y <= 1) & (strip > 0)
        again[extra] = b * 4 + rank
        extra = extra + jnp.where(north | south, 1, 0)

    def put_again(n, _):
        item = again[n]
        b, rank = item >> 2, item & 3
        target, y, z = owner[0, b], base[1, b], base[2, b]
        south = y <= 1
        put(
            target + jnp.where(south, -1, 1),
            block_tiles(b),
            GROUP * (capacity + rank) + jnp.where(south, 0, 8),
            8,
            CODE_LANE + capacity + rank + jnp.where(south, capacity, 0),
            y + jnp.where(south, strip_cells, -strip_cells),
            z,
        )
        return 0

    lax.fori_loop(0, extra, put_again, 0)
    copies[pieces].wait()
    copies[pieces + 1].wait()
    even = lax.rem(lax.axis_index("gy"), 2) == 0
    for i in range(19):
        for x in range(populations.shape[1]):
            high, low = top[i, x, SUB - 2 : SUB, :], bottom[i, x, 0:2, :]
            rim_a[i, x] = jnp.where(even, high, low)
            rim_b[i, x] = jnp.where(even, low, high)


def collided(fields, forcing):
    pair_sum, pair_diff = {}, {}
    for i in range(1, 19, 2):
        pair_sum[i] = fields[i] + fields[i + 1]
        pair_diff[i] = fields[i] - fields[i + 1]
    density = fields[0]
    for i in range(1, 19, 2):
        density = density + pair_sum[i]
    momentum = []
    for k in range(3):
        total = relax_time * forcing[k]
        for i in range(1, 19, 2):
            if velocities[i, k] == 1:
                total = total + pair_diff[i]
            elif velocities[i, k] == -1:
                total = total - pair_diff[i]
        momentum.append(total)
    inverse = 1.0 / density
    keep = 1.0 - 1.0 / relax_time
    squares = momentum[0] * momentum[0] + momentum[1] * momentum[1] + momentum[2] * momentum[2]
    level = density - 1.5 * inverse * squares
    curve = 4.5 * inverse
    result = [None] * 19
    result[0] = keep * fields[0] + (lattice_weights[0] / relax_time) * level
    for i in range(1, 19, 2):
        along = None
        for k in range(3):
            if velocities[i, k] == 1:
                along = momentum[k] if along is None else along + momentum[k]
            elif velocities[i, k] == -1:
                along = -momentum[k] if along is None else along - momentum[k]
        share = lattice_weights[i] / relax_time
        even = share * (level + curve * along * along)
        odd = (3.0 * share) * along
        result[i] = keep * fields[i] + (even + odd)
        result[i + 1] = keep * fields[i + 1] + (even - odd)
    return result


def keep_tile(relaxed, tiles, x, t, values):
    for i in range(19):
        if t < tiles:
            relaxed[i, x, SUB + SUB * t : 2 * SUB + SUB * t, :] = values[i]
        else:
            relaxed[i, x, 0:SUB, :] = values[i]
            relaxed[i, x, SUB + SUB * tiles : 2 * SUB + SUB * tiles, :] = values[i]


def write_faces(relaxed, slabs, tiles, face_a, face_b):
    even = lax.rem(lax.axis_index("gx"), 2) == 0
    for n in range(5):
        for t in range(tiles + 1):
            low = SUB + SUB * t
            east = relaxed[going_east[n], slabs - 1, low : low + SUB, :]
            west = relaxed[going_west[n], 0, low : low + SUB, :]
            face_a[n, SUB * t : SUB * t + SUB, :] = jnp.where(even, east, west)
            face_b[n, SUB * t : SUB * t + SUB, :] = jnp.where(even, west, east)


def unpack_faces(face_a, face_b, tiles, rim_west, rim_east):
    even = lax.rem(lax.axis_index("gx"), 2) == 0
    for n in range(5):
        for t in range(tiles + 1):
            a = face_a[n, SUB * t : SUB * t + SUB, :]
            b = face_b[n, SUB * t : SUB * t + SUB, :]
            west = jnp.where(even, b, a)
            east = jnp.where(even, a, b)
            low = SUB + SUB * t
            rim_west[n, low : low + SUB, :] = west
            rim_east[n, low : low + SUB, :] = east
            if t == tiles:
                rim_west[n, 0:SUB, :] = west
                rim_east[n, 0:SUB, :] = east


def streamed(relaxed, rim_west, rim_east, slabs, tiles, x, t, walls):
    lane, sub = lane_iota(), sub_iota()

    def rows(i, plane, low):
        if plane < 0:
            return rim_west[going_east.index(i), low : low + SUB, :]
        if plane >= slabs:
            return rim_east[going_west.index(i), low : low + SUB, :]
        return relaxed[i, plane, low : low + SUB, :]

    low = SUB + SUB * t if t < tiles else 0
    high = SUB + SUB * tiles
    result = []
    for i in range(19):
        ex, ey, ez = (int(v) for v in velocities[i])
        plane = x - ex
        if t < tiles or ey == 0:
            source = rows(i, plane, low - ey)
        elif ey == 1:
            source = jnp.where(
                sub >= 4, pltpu.roll(rows(i, plane, 0), 1, 0), rows(i, plane, high - 1)
            )
        else:
            source = jnp.where(
                sub >= 4, rows(i, plane, 1), pltpu.roll(rows(i, plane, high), SUB - 1, 0)
            )
        outside = None
        if ez == 1:
            source = pltpu.roll(source, 1, 1)
            outside = lane == 0
        elif ez == -1:
            source = pltpu.roll(source, LANES - 1, 1)
            outside = lane == LANES - 1
        wall = None
        if t == 0 and ey == 1:
            wall = (sub == 0) & walls[0]
        if t == tiles - 1 and ey == -1:
            wall = (sub == SUB - 1) & walls[1]
        if wall is not None:
            outside = wall if outside is None else outside | wall
        if outside is not None:
            source = jnp.where(outside, relaxed[opposite[i], x, low : low + SUB, :], source)
        result.append(source)
    return result


def wall_flags():
    strip = lax.axis_index("gy")
    return strip == 0, strip == lax.axis_size("gy") - 1


def first_kernel(
    capacity,
    got,
    populations,
    rim_a,
    rim_b,
    relaxed,
    face_a,
    face_b,
    forcing,
    items,
    codes,
    arrived,
    placed,
    rim,
    listing,
    spare,
    crowd,
    sem,
):
    slabs, strip_cells = populations.shape[1], populations.shape[2]
    tiles = strip_cells // SUB
    sources = got.shape[0]
    nowhere = SUB * LANES
    lane, sub = lane_iota(), sub_iota()
    arrived[pl.ds(sources * 16, 16), :] = jnp.zeros((16, LANES), jnp.float32)

    def gather(s, _):
        for k in range(3):
            arrived[pl.ds(pl.multiple_of(s * 16, 16) + 4 * k, 4), :] = got[s, k]
        return 0

    lax.fori_loop(0, sources, gather, 0, unroll=8)
    first_dup = CODE_LANE + capacity
    for n in range(sources // SUB):
        code = arrived[pl.ds(SUB * n * 16, SUB, stride=16), :].astype(jnp.int32) - 1
        source = sub + SUB * n
        is_dup = lane >= first_dup
        slot = jnp.where(is_dup, source * 8 + lane - first_dup, source * 4 + lane - CODE_LANE)
        item = jnp.where(code >= 0, slot * 8192 + code, -1)
        busy = jnp.where(is_dup & (lane < first_dup + 2 * capacity) & (code >= 0), 1.0, 0.0)
        busy = jnp.sum(busy, axis=1, keepdims=True)
        item = jnp.where(lane == LANES - 1, jnp.where(busy > 0.0, 1, 0), item)
        corner = pltpu.roll(jnp.maximum(code, nowhere), LANES - CODE_LANE, 1)
        items[SUB * n : SUB * n + SUB, :] = jnp.where(lane < LANES - CODE_LANE, corner, item)
    copy = pltpu.make_async_copy(items, codes, sem)
    copy.start()
    even = lax.rem(lax.axis_index("gy"), 2) == 0
    for i in range(19):
        for x in range(slabs):
            a, b = rim_a[i, x], rim_b[i, x]
            rim[i, x, 0:2, :] = jnp.where(even, a, b)
            rim[i, x, 6:8, :] = jnp.where(even, b, a)
    placed[...] = jnp.zeros_like(placed)
    copy.wait()

    def note(s, carry):
        own, some = carry
        for r in range(capacity):
            item = codes[s, CODE_LANE + r]
            listing[own] = item
            own = own + 1 + (item >> 31)
        crowd[some] = s
        return own, some + codes[s, LANES - 1]

    own_count, some = lax.fori_loop(0, sources, note, (jnp.int32(0), jnp.int32(0)), unroll=8)

    def note_dup(n, dup):
        s = crowd[n]
        for r in range(2 * capacity):
            item = codes[s, first_dup + r]
            spare[dup] = item
            dup = dup + 1 + (item >> 31)
        return dup

    dup_count = lax.fori_loop(0, some, note_dup, jnp.int32(0))
    for j in range(STEP - 1):
        listing[own_count + j] = sources * 4 * 8192 + nowhere

    def moved_rows(source, z, lanes_at, steps):
        inside = (lane >= z) & (lane < z + STEN)
        rows = {}
        for h in range(2):
            tile = arrived[pl.ds(pl.multiple_of(source * 16, 16) + SUB * h, SUB), :]
            for b in range(steps):
                shift = (z - lanes_at - STEN * b + 2 * LANES) & (LANES - 1)
                rows[b, h] = jnp.where(inside, pltpu.roll(tile, shift, 1), 0.0)
        return rows

    def add_rows(rows, y):
        at = {
            (b, h): pl.ds(pl.multiple_of((y + b) * 16 + SUB * h, SUB), SUB) for b, h in rows
        }
        old = {key: placed[at[key], :] for key in rows}
        for key in rows:
            placed[at[key], :] = old[key] + rows[key]

    def place_own(n, _):
        todo = []
        for j in range(STEP):
            item = listing[STEP * n + j]
            slot, code = item >> 13, item & 8191
            todo.append(
                (moved_rows(slot >> 2, code & (LANES - 1), GROUP * (slot & 3), 4), code >> 7)
            )
        for rows, y in todo:
            add_rows(rows, y)
        return 0

    lax.fori_loop(0, (own_count + STEP - 1) // STEP, place_own, 0)

    def place_dup(n, _):
        item = spare[n]
        slot, code = item >> 13, item & 8191
        r = slot & 7
        south = r < capacity
        low = jnp.where(south, 2, 0)
        rank = jnp.where(south, r, r - capacity)
        rows = moved_rows(
            slot >> 3, code & (LANES - 1), GROUP * (capacity + rank) + STEN * low, 2
        )
        add_rows(rows, (code >> 7) + low)
        return 0

    lax.fori_loop(0, dup_count, place_dup, 0)
    for x in range(slabs):
        for t in range(tiles + 1):
            push = []
            for k in range(3):
                if t < tiles:
                    value = placed[pl.ds((SUB + SUB * t) * 16 + 4 * k + x, SUB, stride=16), :]
                else:
                    value = jnp.where(
                        sub >= 4,
                        placed[pl.ds(4 * k + x, SUB, stride=16), :],
                        placed[pl.ds((SUB + SUB * tiles) * 16 + 4 * k + x, SUB, stride=16), :],
                    )
                forcing[k, x, SUB * t : SUB * t + SUB, :] = value
                push.append(value)
            if t < tiles:
                fields = [populations[i, x, SUB * t : SUB * t + SUB, :] for i in range(19)]
            else:
                fields = [rim[i, x] for i in range(19)]
            keep_tile(relaxed, tiles, x, t, collided(fields, push))
    write_faces(relaxed, slabs, tiles, face_a, face_b)


def second_kernel(before, got_a, got_b, forcing, relaxed, face_a, face_b, rim_west, rim_east):
    slabs = before.shape[1]
    tiles = before.shape[2] // SUB - 2
    unpack_faces(got_a, got_b, tiles, rim_west, rim_east)
    walls = wall_flags()
    for x in range(slabs):
        for t in range(tiles + 1):
            fields = streamed(before, rim_west, rim_east, slabs, tiles, x, t, walls)
            push = [forcing[k, x, SUB * t : SUB * t + SUB, :] for k in range(3)]
            keep_tile(relaxed, tiles, x, t, collided(fields, push))
    write_faces(relaxed, slabs, tiles, face_a, face_b)


def third_kernel(
    capacity,
    items,
    before,
    got_a,
    got_b,
    forcing,
    populations_far,
    speeds,
    corners,
    populations,
    rim_west,
    rim_east,
    fluid,
    sems,
):
    slabs = before.shape[1]
    corner_copy = pltpu.make_async_copy(items, corners, sems.at[slabs])
    corner_copy.start()
    tiles = before.shape[2] // SUB - 2
    unpack_faces(got_a, got_b, tiles, rim_west, rim_east)
    walls = wall_flags()
    copies = []
    for x in range(slabs):
        for t in range(tiles):
            fields = streamed(before, rim_west, rim_east, slabs, tiles, x, t, walls)
            density = fields[0]
            for i in range(1, 19):
                density = density + fields[i]
            inverse = 1.0 / density
            for i in range(19):
                populations[i, x, SUB * t : SUB * t + SUB, :] = fields[i]
            for k in range(3):
                total = 0.5 * forcing[k, x, SUB * t : SUB * t + SUB, :]
                for i in range(19):
                    if velocities[i, k] == 1:
                        total = total + fields[i]
                    elif velocities[i, k] == -1:
                        total = total - fields[i]
                fluid[pl.ds(SUB * t * 16 + 4 * k + x, SUB, stride=16), :] = total * inverse
        copies.append(
            pltpu.make_async_copy(populations.at[:, x], populations_far.at[:, x], sems.at[x])
        )
        copies[x].start()
    lane = lane_iota()
    corner_copy.wait()

    def pick(s, _):
        corner = [corners[s, r] for r in range(capacity)]
        tile = jnp.zeros((SUB, LANES), jnp.float32)
        for h in range(2):
            for r in range(capacity):
                y, z = (corner[r] >> 7) - SUB, corner[r] & (LANES - 1)
                for b in range(4):
                    low = GROUP * (h * capacity + r) + STEN * b
                    row = pl.multiple_of((y + b) * 16 + SUB * h, SUB)
                    shift = (low - z + LANES) & (LANES - 1)
                    moved = pltpu.roll(fluid[pl.ds(row, SUB), :], shift, 1)
                    tile = jnp.where((lane >= low) & (lane < low + STEN), moved, tile)
        speeds[s] = tile.astype(jnp.bfloat16)
        return 0

    lax.fori_loop(0, speeds.shape[0], pick, 0, unroll=4)
    for copy in copies:
        copy.wait()


def marker_kernel(
    capacity, owner, swimmer, returned, weights, velocity, total, chosen, expanded, count
):
    held = weights.shape[0]
    cells = weights.shape[1]
    targets = returned.shape[0]
    lane, sub = lane_iota(16), sub_iota(16)
    sub8, lane8 = sub_iota(), lane_iota()

    def reset(i, _):
        count[i] = 0
        return 0

    lax.fori_loop(0, targets, reset, 0, unroll=16)
    for b in range(held):
        target = owner[0, b]
        rank = count[target]
        count[target] = rank + 1
        low = GROUP * rank
        tile = returned[target].astype(jnp.float32)
        first = jnp.where((lane8 >= low) & (lane8 < low + GROUP), tile, 0.0)
        low = low + GROUP * capacity
        second = jnp.where((lane8 >= low) & (lane8 < low + GROUP), tile, 0.0)
        chosen[16 * b : 16 * b + 16, :] = jnp.concatenate([first, second], axis=0).astype(
            jnp.bfloat16
        )
    across = lax.broadcasted_iota(jnp.int32, (LANES, LANES), 1)
    down = lax.broadcasted_iota(jnp.int32, (LANES, LANES), 0)
    repeat = jnp.where(across % GROUP == down % GROUP, 1.0, 0.0).astype(jnp.bfloat16)
    own_cells = (lane // GROUP) % 4 == sub % 4
    for g in range(held // SUB):
        wide = jnp.dot(
            chosen[LANES * g : LANES * g + LANES, :], repeat, preferred_element_type=jnp.float32
        )
        for j in range(SUB):
            expanded[LANES * g + 16 * j : LANES * g + 16 * j + 16, :] = jnp.where(
                own_cells, wide[16 * j : 16 * j + 16, :], 0.0
            )
    sums = {}
    for g in range(held // SUB):
        pieces = []
        for k in range(3):
            row = None
            for x in range(4):
                part = expanded[pl.ds(LANES * g + 4 * k + x, SUB, stride=16), :]
                row = part if row is None else row + part
            pieces.append(
                jnp.concatenate(
                    [
                        jnp.where(sub8 == 2 * pair + lane8 // 64, row, 0.0).astype(jnp.bfloat16)
                        for pair in range(4)
                    ],
                    axis=1,
                )
            )
        left = jnp.concatenate(pieces, axis=0)
        right = weights[SUB * g : SUB * g + SUB].reshape(SUB * cells, LANES)
        out = speed_scale * jnp.dot(left, right, preferred_element_type=jnp.float32)
        member = jnp.zeros((SUB, LANES), jnp.int32)
        for j in range(SUB):
            member = jnp.where(sub8 == j, lax.rem(swimmer[SUB * g + j], SWIM_DEV), member)
        for k in range(3):
            part = out[SUB * k : SUB * k + SUB, :]
            velocity[k, SUB * g : SUB * g + SUB, :] = part
            for s in range(SWIM_DEV):
                term = jnp.where(member == s, part, 0.0)
                sums[k, s] = term if g == 0 else sums[k, s] + term
    table = jnp.zeros((SUB, LANES), jnp.float32)
    for (k, s), value in sums.items():
        mean = jnp.sum(value) * (1.0 / LANES)
        table = jnp.where((sub8 == k) & (lane8 == s), mean, table)
    total[...] = table[0:3, 0:SWIM_DEV]


VM = pl.BlockSpec(memory_space=pltpu.VMEM)
SM = pl.BlockSpec(memory_space=pltpu.SMEM)
FAR = pl.BlockSpec(memory_space=pl.ANY)


def shaped(shape, dtype=jnp.float32):
    return jax.ShapeDtypeStruct(shape, dtype)


def body(populations, marker_weights, marker_force, owner_device, stencil_base, block_swimmer):
    slab_cells, strip_cells, height = populations.shape[1:]
    strips = lax.axis_size("gy")
    devices = lax.axis_size("gx") * strips
    held = marker_weights.shape[0]
    capacity = max(2, (2 * held + devices - 1) // devices)
    tiles = strip_cells // SUB
    padded_rows = strip_cells + 2 * SUB
    packed_rows = strip_cells + SUB
    f32 = jnp.float32
    small = pltpu.CompilerParams(vmem_limit_bytes=12 * 1024 * 1024)

    owner = owner_device.T
    rim = shaped((19, slab_cells, 2, height))
    edge = pltpu.VMEM((19, slab_cells, SUB, height), f32)
    sent, rim_a, rim_b = pl.pallas_call(
        functools.partial(patch_kernel, capacity, strips),
        out_shape=(shaped((devices * 3, 4, LANES)), rim, rim),
        in_specs=[SM, SM, FAR, VM, FAR],
        out_specs=(VM, VM, VM),
        scratch_shapes=[
            pltpu.VMEM(marker_weights.shape, jnp.bfloat16),
            edge,
            edge,
            pltpu.VMEM((3, held, LANES), f32),
            pltpu.VMEM((held * 16, LANES), f32),
            pltpu.VMEM((held, 16, LANES), f32),
            pltpu.SMEM((devices,), jnp.int32),
            pltpu.SMEM((held + 1,), jnp.int32),
            pltpu.SemaphoreType.DMA((6,)),
        ],
        name="patches",
    )(owner, stencil_base.T, marker_weights, marker_force.transpose(1, 0, 2), populations)
    rim_a, rim_b = swapped(rim_a, rim_b, "gy", False)
    got = lax.all_to_all(sent, ("gx", "gy"), split_axis=0, concat_axis=0, tiled=True)
    got = got.reshape(devices, 3, 4, LANES)

    planes = shaped((19, slab_cells, padded_rows, height))
    face = shaped((5, packed_rows, height))
    push = shaped((3, slab_cells, packed_rows, height))
    rims = [pltpu.VMEM((5, padded_rows, height), f32)] * 2
    relaxed, face_a, face_b, forcing, items = pl.pallas_call(
        functools.partial(first_kernel, capacity),
        out_shape=(planes, face, face, push, shaped((devices, LANES), jnp.int32)),
        in_specs=[VM] * 4,
        out_specs=(VM, VM, VM, VM, VM),
        scratch_shapes=[
            pltpu.SMEM((devices, LANES), jnp.int32),
            pltpu.VMEM(((devices + 1) * 16, LANES), f32),
            pltpu.VMEM((padded_rows * 16, LANES), f32),
            pltpu.VMEM((19, slab_cells, SUB, LANES), f32),
            pltpu.SMEM((devices * capacity + STEP,), jnp.int32),
            pltpu.SMEM((devices * 2 * capacity + 1,), jnp.int32),
            pltpu.SMEM((devices + 1,), jnp.int32),
            pltpu.SemaphoreType.DMA,
        ],
        compiler_params=small,
        name="first",
    )(got, populations, rim_a, rim_b)
    got_a, got_b = swapped(face_a, face_b, "gx", True)
    relaxed, face_a, face_b = pl.pallas_call(
        second_kernel,
        out_shape=(planes, face, face),
        in_specs=[VM] * 4,
        out_specs=(VM, VM, VM),
        scratch_shapes=rims,
        compiler_params=small,
        name="second",
    )(relaxed, got_a, got_b, forcing)
    got_a, got_b = swapped(face_a, face_b, "gx", True)
    fields, speeds = pl.pallas_call(
        functools.partial(third_kernel, capacity),
        out_shape=(shaped(populations.shape), shaped((devices, SUB, LANES), jnp.bfloat16)),
        in_specs=[VM, VM, VM, VM, VM],
        out_specs=(FAR, VM),
        scratch_shapes=[
            pltpu.SMEM((devices, LANES), jnp.int32),
            pltpu.VMEM(populations.shape, f32),
        ]
        + rims
        + [
            pltpu.VMEM((strip_cells * 16, LANES), f32),
            pltpu.SemaphoreType.DMA((slab_cells + 1,)),
        ],
        compiler_params=small,
        name="third",
    )(items, relaxed, got_a, got_b, forcing)
    returned = lax.all_to_all(speeds, ("gx", "gy"), split_axis=0, concat_axis=0, tiled=True)
    marker_velocity, swimmer_velocity = pl.pallas_call(
        functools.partial(marker_kernel, capacity),
        out_shape=(shaped((3, held, LANES)), shaped((3, SWIM_DEV))),
        in_specs=[SM, SM, VM, VM],
        out_specs=(VM, VM),
        scratch_shapes=[
            pltpu.VMEM((held * 16, LANES), jnp.bfloat16),
            pltpu.VMEM((held * 16, LANES), f32),
            pltpu.SMEM((devices,), jnp.int32),
        ],
        compiler_params=small,
        name="markers",
    )(owner, block_swimmer, returned, marker_weights)
    return fields, marker_velocity.transpose(1, 0, 2), swimmer_velocity


def solution(mesh):
    in_specs = (
        P(None, "gx", "gy", None),
        P(("gx", "gy"), None, None),
        P(("gx", "gy"), None, None),
        P(("gx", "gy"), None),
        P(("gx", "gy"), None),
        P(("gx", "gy")),
    )
    out_specs = (P(None, "gx", "gy", None), P(("gx", "gy"), None, None), P(None, ("gx", "gy")))
    return jax.shard_map(body, mesh=mesh, in_specs=in_specs, out_specs=out_specs, check_vma=False)
```

```python
import functools

import jax
import jax.numpy as jnp
import numpy as np
from jax import lax
from jax.experimental import pallas as pl
from jax.experimental.pallas import tpu as pltpu
from jax.sharding import PartitionSpec as P


STEN = 4
SWIM_DEV = 4
LANES = 128
SUB = 8
GROUP = STEN * STEN
CODE_LANE = 64
REST_LANE = 48
DUP_LANE = 96
WIDE_DUPS = 4
STEP = 4

velocities = np.array(
    [
        [0, 0, 0],
        [1, 0, 0],
        [-1, 0, 0],
        [0, 1, 0],
        [0, -1, 0],
        [0, 0, 1],
        [0, 0, -1],
        [1, 1, 0],
        [-1, -1, 0],
        [1, -1, 0],
        [-1, 1, 0],
        [1, 0, 1],
        [-1, 0, -1],
        [1, 0, -1],
        [-1, 0, 1],
        [0, 1, 1],
        [0, -1, -1],
        [0, 1, -1],
        [0, -1, 1],
    ]
)
opposite = [0, 2, 1, 4, 3, 6, 5, 8, 7, 10, 9, 12, 11, 14, 13, 16, 15, 18, 17]
lattice_weights = [1.0 / 3.0] + [1.0 / 18.0] * 6 + [1.0 / 36.0] * 12
relax_time = 0.8
speed_scale = 20.0
going_east = [1, 7, 9, 11, 13]
going_west = [2, 8, 10, 12, 14]


def lane_iota(rows=SUB):
    return lax.broadcasted_iota(jnp.int32, (rows, LANES), 1)


def sub_iota(rows=SUB):
    return lax.broadcasted_iota(jnp.int32, (rows, LANES), 0)


def swapped(first, second, axis, periodic):
    size = lax.axis_size(axis)
    inner = [(i, i ^ 1) for i in range(size)]
    outer = []
    for i in range(size):
        j = i + 1 if i % 2 == 1 else i - 1
        if periodic:
            outer.append((i, j % size))
        elif 0 <= j < size:
            outer.append((i, j))
    second = lax.ppermute(second, axis, outer)
    first = lax.ppermute(first, axis, inner)
    return first, second


def patch_kernel(
    capacity,
    strips,
    owner_far,
    base_far,
    weights_far,
    force_far,
    populations,
    send,
    rim_a,
    rim_b,
    owner,
    base,
    weights,
    force,
    bottom,
    top,
    rows,
    spread,
    patches,
    record,
    count,
    place,
    again,
    sems,
):
    held = weights.shape[0]
    cells = weights.shape[1]
    strip_cells = populations.shape[2]
    pieces = sems.shape[0] - 5
    part_blocks = held // pieces
    force_copy = pltpu.make_async_copy(force_far, force, sems.at[pieces])
    force_copy.start()
    copies = [
        pltpu.make_async_copy(
            weights_far.at[part_blocks * n : part_blocks * (n + 1)],
            weights.at[part_blocks * n : part_blocks * (n + 1)],
            sems.at[n],
        )
        for n in range(pieces)
    ]
    copies.append(pltpu.make_async_copy(owner_far, owner, sems.at[pieces + 1]))
    copies.append(pltpu.make_async_copy(base_far, base, sems.at[pieces + 2]))
    edge_copies = [
        pltpu.make_async_copy(populations.at[:, :, 0:SUB, :], bottom, sems.at[pieces + 3]),
        pltpu.make_async_copy(
            populations.at[:, :, strip_cells - SUB : strip_cells, :], top, sems.at[pieces + 4]
        ),
    ]
    for copy in copies + edge_copies:
        copy.start()
    targets = send.shape[0]
    lane, sub = lane_iota(16), sub_iota(16)

    def clear(i, _):
        record[i] = jnp.zeros((16, LANES), jnp.float32)
        return 0

    lax.fori_loop(0, targets, clear, 0, unroll=16)

    def reset(i, _):
        count[i] = 0
        return 0

    lax.fori_loop(0, targets, reset, 0, unroll=16)
    for copy in copies[pieces:]:
        copy.wait()
    extra = jnp.int32(0)
    for b in range(held):
        target = owner[0, b]
        rank = count[target]
        count[target] = rank + 1
        place[b] = target * 4 + rank
        strip = lax.rem(target, strips)
        y = base[1, b]
        north = (y >= strip_cells - 5) & (strip < strips - 1)
        south = (y <= 1) & (strip > 0)
        again[extra] = b * 4 + rank
        extra = extra + jnp.where(north | south, 1, 0)
    force_copy.wait()
    for k in range(3):
        rows[k] = force[k].astype(jnp.float32)
    for b in range(held):
        for k in range(3):
            spread[16 * b + 4 * k : 16 * b + 4 * k + 4, :] = jnp.broadcast_to(
                rows[k, b : b + 1, :], (4, LANES)
            )
        spread[16 * b + 12 : 16 * b + 16, :] = jnp.zeros((4, LANES), jnp.float32)
    for g in range(held // 4):
        if 4 * g % part_blocks == 0:
            copies[4 * g // part_blocks].wait()
        out = lax.dot_general(
            spread[64 * g : 64 * g + 64, :].astype(jnp.bfloat16),
            weights[4 * g : 4 * g + 4].reshape(4 * cells, LANES),
            (((1,), (1,)), ((), ())),
            preferred_element_type=jnp.float32,
        )
        for j in range(4):
            half = j // 2
            part = out[16 * j : 16 * j + 16, LANES * half : LANES * half + LANES]
            part = jnp.where(lane // GROUP == 4 * (j % 2) + sub % 4, part, 0.0)
            part = part + pltpu.roll(part, 64, 1)
            part = part + pltpu.roll(part, 32, 1)
            part = part + pltpu.roll(part, 16, 1)
            patches[g * 4 + j] = part

    def labelled(tile, slot, frame_y, z):
        label = jnp.where(sub == 12, frame_y + SUB, z + 1).astype(jnp.float32)
        return jnp.where((lane == CODE_LANE + slot) & ((sub == 12) | (sub == 13)), label, tile)

    for b in range(held):
        target, rank = place[b] >> 2, place[b] & 3
        low = GROUP * rank
        inside = (lane >= low) & (lane < low + GROUP) & (sub < 12)
        tile = jnp.where(inside, patches[b], record[target])
        record[target] = labelled(tile, rank, base[1, b], base[2, b])

    def put_again(n, _):
        item = again[n]
        b, rank = item >> 2, item & 3
        y, z = base[1, b], base[2, b]
        to_south = y <= 1
        target = owner[0, b] + jnp.where(to_south, -1, 1)
        half = jnp.where(to_south, 0, 1)
        q = rank + jnp.where(to_south, capacity, 0)
        moved = pltpu.roll(patches[b], 8 * ((q + half) & 1), 1)
        wide = q < WIDE_DUPS
        low = jnp.where(wide, DUP_LANE + 8 * q, 2 * LANES)
        tile = jnp.where((lane >= low) & (lane < low + 8) & (sub < 12), moved, record[target])
        tile = labelled(
            tile, capacity + q, y + jnp.where(to_south, strip_cells, -strip_cells), z
        )
        if 2 * capacity > WIDE_DUPS:
            last = tile[12:16, :]
            lane4 = lane_iota(4)
            for k in range(3):
                low = jnp.where(wide, 2 * LANES, GROUP * k + 8 * (q - WIDE_DUPS))
                last = jnp.where(
                    (lane4 >= low) & (lane4 < low + 8), moved[4 * k : 4 * k + 4, :], last
                )
            tile = jnp.concatenate([tile[0:12, :], last], axis=0)
        record[target] = tile
        return 0

    lax.fori_loop(0, extra, put_again, 0)
    for copy in edge_copies:
        copy.wait()
    write_rims(bottom, top, rim_a, rim_b)
    rest_lanes = (lane >= REST_LANE) & (lane < 2 * REST_LANE) & (sub < 12)

    def finish(i, _):
        tile = record[i]
        rest = tile - tile.astype(jnp.bfloat16).astype(jnp.float32)
        tile = jnp.where(rest_lanes, pltpu.roll(rest, REST_LANE, 1), tile)
        send[i] = tile.astype(jnp.bfloat16)
        return 0

    lax.fori_loop(0, targets, finish, 0, unroll=8)


def fold_tables(toward):
    ahead = [i for i in range(19) if velocities[i, 1] == toward]
    plain = 4 if toward == 1 else 3
    to_east, to_west = (9, 8) if toward == 1 else (7, 10)
    near = [i for i in range(19) if i != to_west]
    far = ahead + [0, 1, 5, plain]
    return ahead, near, far, (plain, to_east, to_west)


def rim_message(near_row, far_row, toward):
    ahead, near, far, (plain, to_east, to_west) = fold_tables(toward)
    folded = {i: near_row[i] for i in near}
    folded[plain] = near_row[plain] + 2.0 * near_row[to_west]
    folded[to_east] = near_row[to_east] - near_row[to_west]
    message = [folded[i] for i in near]
    others = [i for i in range(19) if i not in ahead]
    total = [None, None, None]
    mass = None
    for i in others:
        mass = far_row[i] if mass is None else mass + far_row[i]
        for k in (0, 2):
            if velocities[i, k] != 0:
                term = far_row[i] if velocities[i, k] == 1 else -far_row[i]
                total[k] = term if total[k] is None else total[k] + term
        if velocities[i, 1] == -toward:
            total[1] = far_row[i] if total[1] is None else total[1] + far_row[i]
    rest = {0: mass - total[0] - total[1] - total[2], 1: total[0], 5: total[2], plain: total[1]}
    return message + [rest[i] if i in rest else far_row[i] for i in far]


def write_rims(bottom, top, rim_a, rim_b):
    even = lax.rem(lax.axis_index("gy"), 2) == 0

    def row(edge, n):
        return [edge[i, :, n, :] for i in range(19)]

    up = rim_message(row(top, SUB - 1), row(top, SUB - 2), 1)
    down = rim_message(row(bottom, 0), row(bottom, 1), -1)
    for n in range(len(up)):
        rim_a[n] = jnp.where(even, up[n], down[n])
        rim_b[n] = jnp.where(even, down[n], up[n])


def collided(fields, forcing):
    pair_sum, pair_diff = {}, {}
    for i in range(1, 19, 2):
        pair_sum[i] = fields[i] + fields[i + 1]
        pair_diff[i] = fields[i] - fields[i + 1]
    density = fields[0]
    for i in range(1, 19, 2):
        density = density + pair_sum[i]
    momentum = []
    for k in range(3):
        total = relax_time * forcing[k]
        for i in range(1, 19, 2):
            if velocities[i, k] == 1:
                total = total + pair_diff[i]
            elif velocities[i, k] == -1:
                total = total - pair_diff[i]
        momentum.append(total)
    inverse = 1.0 / density
    keep = 1.0 - 1.0 / relax_time
    squares = momentum[0] * momentum[0] + momentum[1] * momentum[1] + momentum[2] * momentum[2]
    level = density - 1.5 * inverse * squares
    curve = 4.5 * inverse
    result = [None] * 19
    result[0] = keep * fields[0] + (lattice_weights[0] / relax_time) * level
    for i in range(1, 19, 2):
        along = None
        for k in range(3):
            if velocities[i, k] == 1:
                along = momentum[k] if along is None else along + momentum[k]
            elif velocities[i, k] == -1:
                along = -momentum[k] if along is None else along - momentum[k]
        share = lattice_weights[i] / relax_time
        even = share * (level + curve * along * along)
        odd = (3.0 * share) * along
        result[i] = keep * fields[i] + (even + odd)
        result[i + 1] = keep * fields[i + 1] + (even - odd)
    return result


def keep_tile(relaxed, tiles, x, t, values):
    for i in range(19):
        if t < tiles:
            relaxed[i, x, SUB + SUB * t : 2 * SUB + SUB * t, :] = values[i]
        else:
            relaxed[i, x, 0:SUB, :] = values[i]
            relaxed[i, x, SUB + SUB * tiles : 2 * SUB + SUB * tiles, :] = values[i]


def write_faces(relaxed, slabs, tiles, face_a, face_b):
    even = lax.rem(lax.axis_index("gx"), 2) == 0
    for n in range(5):
        for t in range(tiles + 1):
            low = SUB + SUB * t
            east = relaxed[going_east[n], slabs - 1, low : low + SUB, :]
            west = relaxed[going_west[n], 0, low : low + SUB, :]
            face_a[n, SUB * t : SUB * t + SUB, :] = jnp.where(even, east, west)
            face_b[n, SUB * t : SUB * t + SUB, :] = jnp.where(even, west, east)


def unpack_faces(face_a, face_b, tiles, rim_west, rim_east):
    even = lax.rem(lax.axis_index("gx"), 2) == 0
    for n in range(5):
        for t in range(tiles + 1):
            a = face_a[n, SUB * t : SUB * t + SUB, :]
            b = face_b[n, SUB * t : SUB * t + SUB, :]
            west = jnp.where(even, b, a)
            east = jnp.where(even, a, b)
            low = SUB + SUB * t
            rim_west[n, low : low + SUB, :] = west
            rim_east[n, low : low + SUB, :] = east
            if t == tiles:
                rim_west[n, 0:SUB, :] = west
                rim_east[n, 0:SUB, :] = east


def streamed(relaxed, rim_west, rim_east, slabs, tiles, x, t, walls):
    lane, sub = lane_iota(), sub_iota()

    def rows(i, plane, low):
        if plane < 0:
            return rim_west[going_east.index(i), low : low + SUB, :]
        if plane >= slabs:
            return rim_east[going_west.index(i), low : low + SUB, :]
        return relaxed[i, plane, low : low + SUB, :]

    low = SUB + SUB * t if t < tiles else 0
    high = SUB + SUB * tiles
    result = []
    for i in range(19):
        ex, ey, ez = (int(v) for v in velocities[i])
        plane = x - ex
        if t < tiles or ey == 0:
            source = rows(i, plane, low - ey)
        elif ey == 1:
            source = jnp.where(
                sub >= 4, pltpu.roll(rows(i, plane, 0), 1, 0), rows(i, plane, high - 1)
            )
        else:
            source = jnp.where(
                sub >= 4, rows(i, plane, 1), pltpu.roll(rows(i, plane, high), SUB - 1, 0)
            )
        outside = None
        if ez == 1:
            source = pltpu.roll(source, 1, 1)
            outside = lane == 0
        elif ez == -1:
            source = pltpu.roll(source, LANES - 1, 1)
            outside = lane == LANES - 1
        wall = None
        if t == 0 and ey == 1:
            wall = (sub == 0) & walls[0]
        if t == tiles - 1 and ey == -1:
            wall = (sub == SUB - 1) & walls[1]
        if wall is not None:
            outside = wall if outside is None else outside | wall
        if outside is not None:
            source = jnp.where(outside, relaxed[opposite[i], x, low : low + SUB, :], source)
        result.append(source)
    return result


def wall_flags():
    strip = lax.axis_index("gy")
    return strip == 0, strip == lax.axis_size("gy") - 1


def first_kernel(
    capacity,
    got,
    populations,
    rim_a,
    rim_b,
    relaxed,
    face_a,
    face_b,
    forcing,
    items,
    codes,
    arrived,
    placed,
    rim,
    listing,
    spare,
    crowd,
    sem,
):
    slabs, strip_cells = populations.shape[1], populations.shape[2]
    tiles = strip_cells // SUB
    sources = got.shape[0]
    nowhere = SUB * LANES
    lane, sub = lane_iota(), sub_iota()
    arrived[pl.ds(sources * 16, 16), :] = jnp.zeros((16, LANES), jnp.float32)

    def gather(s, _):
        tile = got[s].astype(jnp.float32)
        upper, lower = tile[0:SUB, :], tile[SUB:16, :]
        own_lanes = lane < REST_LANE
        back = LANES - REST_LANE
        new_upper = jnp.where(own_lanes, upper + pltpu.roll(upper, back, 1), upper)
        new_lower = jnp.where(own_lanes, lower + pltpu.roll(lower, back, 1), lower)
        if 2 * capacity > WIDE_DUPS:
            here = (lane >= REST_LANE) & (lane < REST_LANE + GROUP)
            first_rows = pltpu.roll(lower, 4, 0)
            upper_dups = jnp.where(
                sub < 4,
                pltpu.roll(first_rows, REST_LANE, 1),
                pltpu.roll(lower, REST_LANE - GROUP, 1),
            )
            lower_dups = pltpu.roll(first_rows, REST_LANE - 2 * GROUP, 1)
            new_upper = jnp.where(here, upper_dups, new_upper)
            new_lower = jnp.where(here & (sub < 4), lower_dups, new_lower)
        at = pl.multiple_of(s * 16, 16)
        arrived[pl.ds(at, SUB), :] = new_upper
        arrived[pl.ds(at + SUB, SUB), :] = new_lower
        return 0

    lax.fori_loop(0, sources, gather, 0, unroll=8)
    first_dup = CODE_LANE + capacity
    for n in range(sources // SUB):
        row = arrived[pl.ds(SUB * n * 16 + 12, SUB, stride=16), :].astype(jnp.int32)
        column = arrived[pl.ds(SUB * n * 16 + 13, SUB, stride=16), :].astype(jnp.int32)
        code = row * LANES + column - 1
        source = sub + SUB * n
        is_dup = lane >= first_dup
        slot = jnp.where(is_dup, source * 8 + lane - first_dup, source * 4 + lane - CODE_LANE)
        item = jnp.where(code >= 0, slot * 8192 + code, -1)
        busy = jnp.where(is_dup & (lane < first_dup + 2 * capacity) & (code >= 0), 1.0, 0.0)
        busy = jnp.sum(busy, axis=1, keepdims=True)
        item = jnp.where(lane == LANES - 1, jnp.where(busy > 0.0, 1, 0), item)
        corner = pltpu.roll(jnp.maximum(code, nowhere), LANES - CODE_LANE, 1)
        items[SUB * n : SUB * n + SUB, :] = jnp.where(lane < capacity, corner, item)
    copy = pltpu.make_async_copy(items, codes, sem)
    copy.start()
    even = lax.rem(lax.axis_index("gy"), 2) == 0
    rim[...] = jnp.zeros_like(rim)
    for toward in (1, -1):
        _, near, far, _ = fold_tables(toward)
        for n, i in enumerate(near + far):
            a, b = rim_a[n], rim_b[n]
            value = jnp.where(even, b, a) if toward == 1 else jnp.where(even, a, b)
            if toward == 1:
                at = 7 if n < len(near) else 6
            else:
                at = 0 if n < len(near) else 1
            rim[i, :, at, :] = value
    placed[...] = jnp.zeros_like(placed)
    copy.wait()

    def note(s, carry):
        own, some = carry
        for r in range(capacity):
            item = codes[s, CODE_LANE + r]
            listing[own >> 7, own & 127] = item
            own = own + 1 + (item >> 31)
        crowd[some] = s
        return own, some + codes[s, LANES - 1]

    own_count, some = lax.fori_loop(0, sources, note, (jnp.int32(0), jnp.int32(0)), unroll=8)

    def note_dup(n, dup):
        s = crowd[n]
        for r in range(2 * capacity):
            item = codes[s, first_dup + r]
            spare[dup] = item
            dup = dup + 1 + (item >> 31)
        return dup

    dup_count = lax.fori_loop(0, some, note_dup, jnp.int32(0))
    for j in range(STEP - 1):
        at = own_count + j
        listing[at >> 7, at & 127] = sources * 4 * 8192 + nowhere

    def moved_rows(source, z, lanes_at, steps):
        inside = (lane >= z) & (lane < z + STEN)
        rows = {}
        for h in range(2):
            tile = arrived[pl.ds(pl.multiple_of(source * 16, 16) + SUB * h, SUB), :]
            for b in range(steps):
                shift = (z - lanes_at - STEN * b + 2 * LANES) & (LANES - 1)
                rows[b, h] = jnp.where(inside, pltpu.roll(tile, shift, 1), 0.0)
        return rows

    def add_rows(rows, y):
        at = {
            (b, h): pl.ds(pl.multiple_of((y + b) * 16 + SUB * h, SUB), SUB) for b, h in rows
        }
        old = {key: placed[at[key], :] for key in rows}
        for key in rows:
            placed[at[key], :] = old[key] + rows[key]

    def place_own(n, _):
        todo = []
        for j in range(STEP):
            at = STEP * n + j
            item = listing[at >> 7, at & 127]
            slot, code = item >> 13, item & 8191
            todo.append(
                (moved_rows(slot >> 2, code & (LANES - 1), GROUP * (slot & 3), 4), code >> 7)
            )
        for rows, y in todo:
            add_rows(rows, y)
        return 0

    lax.fori_loop(0, (own_count + STEP - 1) // STEP, place_own, 0)

    def place_dup(n, _):
        item = spare[n]
        slot, code = item >> 13, item & 8191
        q = slot & 7
        low = jnp.where(q < capacity, 2, 0)
        at = 8 * q + jnp.where(q < WIDE_DUPS, DUP_LANE, REST_LANE - 8 * WIDE_DUPS)
        rows = moved_rows(slot >> 3, code & (LANES - 1), at, 2)
        add_rows(rows, (code >> 7) + low)
        return 0

    lax.fori_loop(0, dup_count, place_dup, 0)
    for x in range(slabs):
        for t in range(tiles + 1):
            push = []
            for k in range(3):
                if t < tiles:
                    value = placed[pl.ds((SUB + SUB * t) * 16 + 4 * k + x, SUB, stride=16), :]
                else:
                    value = jnp.where(
                        sub >= 4,
                        placed[pl.ds(4 * k + x, SUB, stride=16), :],
                        placed[pl.ds((SUB + SUB * tiles) * 16 + 4 * k + x, SUB, stride=16), :],
                    )
                forcing[k, x, SUB * t : SUB * t + SUB, :] = value
                push.append(value)
            if t < tiles:
                fields = [populations[i, x, SUB * t : SUB * t + SUB, :] for i in range(19)]
            else:
                fields = [rim[i, x] for i in range(19)]
            keep_tile(relaxed, tiles, x, t, collided(fields, push))
    write_faces(relaxed, slabs, tiles, face_a, face_b)


def second_kernel(before, got_a, got_b, forcing, relaxed, face_a, face_b, rim_west, rim_east):
    slabs = before.shape[1]
    tiles = before.shape[2] // SUB - 2
    unpack_faces(got_a, got_b, tiles, rim_west, rim_east)
    walls = wall_flags()
    for x in range(slabs):
        for t in range(tiles + 1):
            fields = streamed(before, rim_west, rim_east, slabs, tiles, x, t, walls)
            push = [forcing[k, x, SUB * t : SUB * t + SUB, :] for k in range(3)]
            keep_tile(relaxed, tiles, x, t, collided(fields, push))
    write_faces(relaxed, slabs, tiles, face_a, face_b)


def third_kernel(
    capacity,
    items,
    before,
    got_a,
    got_b,
    forcing,
    populations_far,
    speeds,
    corners,
    populations,
    rim_west,
    rim_east,
    fluid,
    sems,
):
    slabs = before.shape[1]
    corner_copy = pltpu.make_async_copy(items, corners, sems.at[slabs])
    corner_copy.start()
    tiles = before.shape[2] // SUB - 2
    unpack_faces(got_a, got_b, tiles, rim_west, rim_east)
    walls = wall_flags()
    copies = []
    for x in range(slabs):
        for t in range(tiles):
            fields = streamed(before, rim_west, rim_east, slabs, tiles, x, t, walls)
            density = fields[0]
            for i in range(1, 19):
                density = density + fields[i]
            inverse = 1.0 / density
            for i in range(19):
                populations[i, x, SUB * t : SUB * t + SUB, :] = fields[i]
            for k in range(3):
                total = 0.5 * forcing[k, x, SUB * t : SUB * t + SUB, :]
                for i in range(19):
                    if velocities[i, k] == 1:
                        total = total + fields[i]
                    elif velocities[i, k] == -1:
                        total = total - fields[i]
                fluid[pl.ds(SUB * t * 16 + 4 * k + x, SUB, stride=16), :] = total * inverse
        copies.append(
            pltpu.make_async_copy(populations.at[:, x], populations_far.at[:, x], sems.at[x])
        )
        copies[x].start()
    lane = lane_iota()
    corner_copy.wait()

    def pick(s, _):
        corner = [corners[s, r] for r in range(capacity)]
        tile = jnp.zeros((SUB, LANES), jnp.float32)
        for h in range(2):
            for r in range(capacity):
                y, z = (corner[r] >> 7) - SUB, corner[r] & (LANES - 1)
                for b in range(4):
                    low = GROUP * (h * capacity + r) + STEN * b
                    row = pl.multiple_of((y + b) * 16 + SUB * h, SUB)
                    shift = (low - z + LANES) & (LANES - 1)
                    moved = pltpu.roll(fluid[pl.ds(row, SUB), :], shift, 1)
                    tile = jnp.where((lane >= low) & (lane < low + STEN), moved, tile)
        speeds[s] = tile.astype(jnp.bfloat16)
        return 0

    lax.fori_loop(0, speeds.shape[0], pick, 0, unroll=8)
    for copy in copies:
        copy.wait()


def marker_kernel(
    capacity, owner, swimmer, returned, weights, velocity, total, chosen, expanded, count
):
    held = weights.shape[0]
    cells = weights.shape[1]
    targets = returned.shape[0]
    lane, sub = lane_iota(16), sub_iota(16)
    sub8, lane8 = sub_iota(), lane_iota()

    def reset(i, _):
        count[i] = 0
        return 0

    lax.fori_loop(0, targets, reset, 0, unroll=16)
    for b in range(held):
        target = owner[0, b]
        rank = count[target]
        count[target] = rank + 1
        low = GROUP * rank
        tile = returned[target].astype(jnp.float32)
        first = jnp.where((lane8 >= low) & (lane8 < low + GROUP), tile, 0.0)
        low = low + GROUP * capacity
        second = jnp.where((lane8 >= low) & (lane8 < low + GROUP), tile, 0.0)
        chosen[16 * b : 16 * b + 16, :] = jnp.concatenate([first, second], axis=0).astype(
            jnp.bfloat16
        )
    across = lax.broadcasted_iota(jnp.int32, (LANES, LANES), 1)
    down = lax.broadcasted_iota(jnp.int32, (LANES, LANES), 0)
    repeat = jnp.where(across % GROUP == down % GROUP, 1.0, 0.0).astype(jnp.bfloat16)
    own_cells = (lane // GROUP) % 4 == sub % 4
    for g in range(held // SUB):
        wide = jnp.dot(
            chosen[LANES * g : LANES * g + LANES, :], repeat, preferred_element_type=jnp.float32
        )
        for j in range(SUB):
            expanded[LANES * g + 16 * j : LANES * g + 16 * j + 16, :] = jnp.where(
                own_cells, wide[16 * j : 16 * j + 16, :], 0.0
            )
    sums = {}
    for g in range(held // SUB):
        pieces = []
        for k in range(3):
            row = None
            for x in range(4):
                part = expanded[pl.ds(LANES * g + 4 * k + x, SUB, stride=16), :]
                row = part if row is None else row + part
            pieces.append(
                jnp.concatenate(
                    [
                        jnp.where(sub8 == 2 * pair + lane8 // 64, row, 0.0).astype(jnp.bfloat16)
                        for pair in range(4)
                    ],
                    axis=1,
                )
            )
        left = jnp.concatenate(pieces, axis=0)
        right = weights[SUB * g : SUB * g + SUB].reshape(SUB * cells, LANES)
        out = speed_scale * jnp.dot(left, right, preferred_element_type=jnp.float32)
        member = jnp.zeros((SUB, LANES), jnp.int32)
        for j in range(SUB):
            member = jnp.where(sub8 == j, lax.rem(swimmer[SUB * g + j], SWIM_DEV), member)
        for k in range(3):
            part = out[SUB * k : SUB * k + SUB, :]
            velocity[k, SUB * g : SUB * g + SUB, :] = part
            for s in range(SWIM_DEV):
                term = jnp.where(member == s, part, 0.0)
                sums[k, s] = term if g == 0 else sums[k, s] + term
    table = jnp.zeros((SUB, LANES), jnp.float32)
    for (k, s), value in sums.items():
        mean = jnp.sum(value) * (1.0 / LANES)
        table = jnp.where((sub8 == k) & (lane8 == s), mean, table)
    total[...] = table[0:3, 0:SWIM_DEV]


VM = pl.BlockSpec(memory_space=pltpu.VMEM)
SM = pl.BlockSpec(memory_space=pltpu.SMEM)
FAR = pl.BlockSpec(memory_space=pltpu.HBM)


def shaped(shape, dtype=jnp.float32):
    return jax.ShapeDtypeStruct(shape, dtype)


def step(populations, marker_weights, marker_force, owner_device, stencil_base, block_swimmer):
    slab_cells, strip_cells, height = populations.shape[1:]
    strips = lax.axis_size("gy")
    devices = lax.axis_size("gx") * strips
    held = marker_weights.shape[0]
    capacity = max(2, (2 * held + devices - 1) // devices)
    padded_rows = strip_cells + 2 * SUB
    packed_rows = strip_cells + SUB
    f32 = jnp.float32
    small = pltpu.CompilerParams(vmem_limit_bytes=12 * 1024 * 1024)

    owner = owner_device.T
    force = marker_force.transpose(1, 0, 2)
    edge = shaped((27, slab_cells, height))
    edge_rows = pltpu.VMEM((19, slab_cells, SUB, height), f32)
    sent, rim_a, rim_b = pl.pallas_call(
        functools.partial(patch_kernel, capacity, strips),
        out_shape=(shaped((devices, 16, LANES), jnp.bfloat16), edge, edge),
        in_specs=[FAR] * 5,
        out_specs=(VM, VM, VM),
        scratch_shapes=[
            pltpu.SMEM(owner.shape, jnp.int32),
            pltpu.SMEM((3, held), jnp.int32),
            pltpu.VMEM(marker_weights.shape, jnp.bfloat16),
            pltpu.VMEM(force.shape, jnp.bfloat16),
            edge_rows,
            edge_rows,
            pltpu.VMEM((3, held, LANES), f32),
            pltpu.VMEM((held * 16, LANES), f32),
            pltpu.VMEM((held, 16, LANES), f32),
            pltpu.VMEM((devices, 16, LANES), f32),
            pltpu.SMEM((devices,), jnp.int32),
            pltpu.SMEM((held,), jnp.int32),
            pltpu.SMEM((held + 1,), jnp.int32),
            pltpu.SemaphoreType.DMA((9,)),
        ],
        name="patches",
    )(owner, stencil_base.T, marker_weights, force, populations)
    got = lax.all_to_all(sent, ("gx", "gy"), split_axis=0, concat_axis=0, tiled=True)
    rim_a, rim_b = swapped(rim_a, rim_b, "gy", False)
    planes = shaped((19, slab_cells, padded_rows, height))
    face = shaped((5, packed_rows, height))
    push = shaped((3, slab_cells, packed_rows, height))
    rims = [pltpu.VMEM((5, padded_rows, height), f32)] * 2
    relaxed, face_a, face_b, forcing, items = pl.pallas_call(
        functools.partial(first_kernel, capacity),
        out_shape=(planes, face, face, push, shaped((devices, LANES), jnp.int32)),
        in_specs=[VM] * 4,
        out_specs=(VM, VM, VM, VM, VM),
        scratch_shapes=[
            pltpu.SMEM((devices, LANES), jnp.int32),
            pltpu.VMEM(((devices + 1) * 16, LANES), f32),
            pltpu.VMEM((padded_rows * 16, LANES), f32),
            pltpu.VMEM((19, slab_cells, SUB, LANES), f32),
            pltpu.SMEM((SUB, LANES), jnp.int32),
            pltpu.SMEM((devices * 2 * capacity + 1,), jnp.int32),
            pltpu.SMEM((devices + 1,), jnp.int32),
            pltpu.SemaphoreType.DMA,
        ],
        compiler_params=small,
        name="first",
    )(got, populations, rim_a, rim_b)
    got_a, got_b = swapped(face_a, face_b, "gx", True)
    relaxed, face_a, face_b = pl.pallas_call(
        second_kernel,
        out_shape=(planes, face, face),
        in_specs=[VM] * 4,
        out_specs=(VM, VM, VM),
        scratch_shapes=rims,
        compiler_params=small,
        name="second",
    )(relaxed, got_a, got_b, forcing)
    got_a, got_b = swapped(face_a, face_b, "gx", True)
    fields, speeds = pl.pallas_call(
        functools.partial(third_kernel, capacity),
        out_shape=(shaped(populations.shape), shaped((devices, SUB, LANES), jnp.bfloat16)),
        in_specs=[VM, VM, VM, VM, VM],
        out_specs=(FAR, VM),
        scratch_shapes=[
            pltpu.SMEM((devices, LANES), jnp.int32),
            pltpu.VMEM(populations.shape, f32),
        ]
        + rims
        + [
            pltpu.VMEM((strip_cells * 16, LANES), f32),
            pltpu.SemaphoreType.DMA((slab_cells + 1,)),
        ],
        compiler_params=small,
        name="third",
    )(items, relaxed, got_a, got_b, forcing)
    returned = lax.all_to_all(speeds, ("gx", "gy"), split_axis=0, concat_axis=0, tiled=True)
    marker_velocity, swimmer_velocity = pl.pallas_call(
        functools.partial(marker_kernel, capacity),
        out_shape=(shaped((3, held, LANES)), shaped((3, SWIM_DEV))),
        in_specs=[SM, SM, VM, VM],
        out_specs=(VM, VM),
        scratch_shapes=[
            pltpu.VMEM((held * 16, LANES), jnp.bfloat16),
            pltpu.VMEM((held * 16, LANES), f32),
            pltpu.SMEM((devices,), jnp.int32),
        ],
        compiler_params=small,
        name="markers",
    )(owner, block_swimmer, returned, marker_weights)
    return fields, marker_velocity.transpose(1, 0, 2), swimmer_velocity


def solution(mesh):
    in_specs = (
        P(None, "gx", "gy", None),
        P(("gx", "gy"), None, None),
        P(("gx", "gy"), None, None),
        P(("gx", "gy"), None),
        P(("gx", "gy"), None),
        P(("gx", "gy")),
    )
    out_specs = (P(None, "gx", "gy", None), P(("gx", "gy"), None, None), P(None, ("gx", "gy")))
    return jax.shard_map(step, mesh=mesh, in_specs=in_specs, out_specs=out_specs, check_vma=False)
```

```python
import functools

import jax
import jax.numpy as jnp
import numpy as np
from jax import lax
from jax.experimental import pallas as pl
from jax.experimental.pallas import tpu as pltpu
from jax.sharding import PartitionSpec as P


STEN = 4
SWIM_DEV = 4
LANES = 128
SUB = 8
GROUP = STEN * STEN
CODE_LANE = 64
REST_LANE = 48
DUP_LANE = 96
WIDE_DUPS = 4
STEP = 4

velocities = np.array(
    [
        [0, 0, 0],
        [1, 0, 0],
        [-1, 0, 0],
        [0, 1, 0],
        [0, -1, 0],
        [0, 0, 1],
        [0, 0, -1],
        [1, 1, 0],
        [-1, -1, 0],
        [1, -1, 0],
        [-1, 1, 0],
        [1, 0, 1],
        [-1, 0, -1],
        [1, 0, -1],
        [-1, 0, 1],
        [0, 1, 1],
        [0, -1, -1],
        [0, 1, -1],
        [0, -1, 1],
    ]
)
opposite = [0, 2, 1, 4, 3, 6, 5, 8, 7, 10, 9, 12, 11, 14, 13, 16, 15, 18, 17]
lattice_weights = [1.0 / 3.0] + [1.0 / 18.0] * 6 + [1.0 / 36.0] * 12
relax_time = 0.8
speed_scale = 20.0
going_east = [1, 7, 9, 11, 13]
going_west = [2, 10, 8, 12, 14]
staying = [0, 3, 4, 5, 6, 15, 16, 17, 18]
FACE_FIELDS = 14


def lane_iota(rows=SUB):
    return lax.broadcasted_iota(jnp.int32, (rows, LANES), 1)


def sub_iota(rows=SUB):
    return lax.broadcasted_iota(jnp.int32, (rows, LANES), 0)


def swapped(first, second, axis, periodic):
    size = lax.axis_size(axis)
    inner = [(i, i ^ 1) for i in range(size)]
    outer = []
    for i in range(size):
        j = i + 1 if i % 2 == 1 else i - 1
        if periodic:
            outer.append((i, j % size))
        elif 0 <= j < size:
            outer.append((i, j))
    second = lax.ppermute(second, axis, outer)
    first = lax.ppermute(first, axis, inner)
    return first, second


def patch_kernel(
    capacity,
    strips,
    owner_far,
    base_far,
    weights_far,
    force_far,
    populations,
    send,
    rim_a,
    rim_b,
    owner,
    base,
    weights,
    force,
    bottom,
    top,
    rows,
    spread,
    patches,
    record,
    count,
    place,
    again,
    sems,
):
    held = weights.shape[0]
    cells = weights.shape[1]
    strip_cells = populations.shape[2]
    pieces = sems.shape[0] - 5
    part_blocks = held // pieces
    force_copy = pltpu.make_async_copy(force_far, force, sems.at[pieces])
    force_copy.start()
    copies = [
        pltpu.make_async_copy(
            weights_far.at[part_blocks * n : part_blocks * (n + 1)],
            weights.at[part_blocks * n : part_blocks * (n + 1)],
            sems.at[n],
        )
        for n in range(pieces)
    ]
    copies.append(pltpu.make_async_copy(owner_far, owner, sems.at[pieces + 1]))
    copies.append(pltpu.make_async_copy(base_far, base, sems.at[pieces + 2]))
    edge_copies = [
        pltpu.make_async_copy(populations.at[:, :, 0:SUB, :], bottom, sems.at[pieces + 3]),
        pltpu.make_async_copy(
            populations.at[:, :, strip_cells - SUB : strip_cells, :], top, sems.at[pieces + 4]
        ),
    ]
    for copy in copies + edge_copies:
        copy.start()
    targets = send.shape[0]
    lane, sub = lane_iota(16), sub_iota(16)

    def clear(i, _):
        record[i] = jnp.zeros((16, LANES), jnp.float32)
        return 0

    lax.fori_loop(0, targets, clear, 0, unroll=16)

    def reset(i, _):
        count[i] = 0
        return 0

    lax.fori_loop(0, targets, reset, 0, unroll=16)
    for copy in copies[pieces:]:
        copy.wait()
    extra = jnp.int32(0)
    for b in range(held):
        target = owner[0, b]
        rank = count[target]
        count[target] = rank + 1
        place[b] = target * 4 + rank
        strip = lax.rem(target, strips)
        y = base[1, b]
        north = (y >= strip_cells - 5) & (strip < strips - 1)
        south = (y <= 1) & (strip > 0)
        again[extra] = b * 4 + rank
        extra = extra + jnp.where(north | south, 1, 0)
    force_copy.wait()
    for k in range(3):
        rows[k] = force[k].astype(jnp.float32)
    for b in range(held):
        for k in range(3):
            spread[16 * b + 4 * k : 16 * b + 4 * k + 4, :] = jnp.broadcast_to(
                rows[k, b : b + 1, :], (4, LANES)
            )
        spread[16 * b + 12 : 16 * b + 16, :] = jnp.zeros((4, LANES), jnp.float32)
    for g in range(held // 4):
        if 4 * g % part_blocks == 0:
            copies[4 * g // part_blocks].wait()
        out = lax.dot_general(
            spread[64 * g : 64 * g + 64, :].astype(jnp.bfloat16),
            weights[4 * g : 4 * g + 4].reshape(4 * cells, LANES),
            (((1,), (1,)), ((), ())),
            preferred_element_type=jnp.float32,
        )
        for j in range(4):
            half = j // 2
            part = out[16 * j : 16 * j + 16, LANES * half : LANES * half + LANES]
            part = jnp.where(lane // GROUP == 4 * (j % 2) + sub % 4, part, 0.0)
            part = part + pltpu.roll(part, 64, 1)
            part = part + pltpu.roll(part, 32, 1)
            part = part + pltpu.roll(part, 16, 1)
            patches[g * 4 + j] = part

    def labelled(tile, slot, frame_y, z):
        label = jnp.where(sub == 12, frame_y + SUB, z + 1).astype(jnp.float32)
        return jnp.where((lane == CODE_LANE + slot) & ((sub == 12) | (sub == 13)), label, tile)

    for b in range(held):
        target, rank = place[b] >> 2, place[b] & 3
        low = GROUP * rank
        inside = (lane >= low) & (lane < low + GROUP) & (sub < 12)
        tile = jnp.where(inside, patches[b], record[target])
        record[target] = labelled(tile, rank, base[1, b], base[2, b])

    def put_again(n, _):
        item = again[n]
        b, rank = item >> 2, item & 3
        y, z = base[1, b], base[2, b]
        to_south = y <= 1
        target = owner[0, b] + jnp.where(to_south, -1, 1)
        half = jnp.where(to_south, 0, 1)
        q = rank + jnp.where(to_south, capacity, 0)
        moved = pltpu.roll(patches[b], 8 * ((q + half) & 1), 1)
        wide = q < WIDE_DUPS
        low = jnp.where(wide, DUP_LANE + 8 * q, 2 * LANES)
        tile = jnp.where((lane >= low) & (lane < low + 8) & (sub < 12), moved, record[target])
        tile = labelled(
            tile, capacity + q, y + jnp.where(to_south, strip_cells, -strip_cells), z
        )
        if 2 * capacity > WIDE_DUPS:
            last = tile[12:16, :]
            lane4 = lane_iota(4)
            for k in range(3):
                low = jnp.where(wide, 2 * LANES, GROUP * k + 8 * (q - WIDE_DUPS))
                last = jnp.where(
                    (lane4 >= low) & (lane4 < low + 8), moved[4 * k : 4 * k + 4, :], last
                )
            tile = jnp.concatenate([tile[0:12, :], last], axis=0)
        record[target] = tile
        return 0

    lax.fori_loop(0, extra, put_again, 0)
    for copy in edge_copies:
        copy.wait()
    write_rims(bottom, top, rim_a, rim_b)
    rest_lanes = (lane >= REST_LANE) & (lane < 2 * REST_LANE) & (sub < 12)

    def finish(i, _):
        tile = record[i]
        rest = tile - tile.astype(jnp.bfloat16).astype(jnp.float32)
        tile = jnp.where(rest_lanes, pltpu.roll(rest, REST_LANE, 1), tile)
        send[i] = tile.astype(jnp.bfloat16)
        return 0

    lax.fori_loop(0, targets, finish, 0, unroll=8)


def fold_tables(toward):
    ahead = [i for i in range(19) if velocities[i, 1] == toward]
    plain = 4 if toward == 1 else 3
    to_east, to_west = (9, 8) if toward == 1 else (7, 10)
    near = [i for i in range(19) if i != to_west]
    far = ahead + [0, 1, 5, plain]
    return ahead, near, far, (plain, to_east, to_west)


def rim_message(near_row, far_row, toward):
    ahead, near, far, (plain, to_east, to_west) = fold_tables(toward)
    folded = {i: near_row[i] for i in near}
    folded[plain] = near_row[plain] + 2.0 * near_row[to_west]
    folded[to_east] = near_row[to_east] - near_row[to_west]
    message = [folded[i] for i in near]
    others = [i for i in range(19) if i not in ahead]
    total = [None, None, None]
    mass = None
    for i in others:
        mass = far_row[i] if mass is None else mass + far_row[i]
        for k in (0, 2):
            if velocities[i, k] != 0:
                term = far_row[i] if velocities[i, k] == 1 else -far_row[i]
                total[k] = term if total[k] is None else total[k] + term
        if velocities[i, 1] == -toward:
            total[1] = far_row[i] if total[1] is None else total[1] + far_row[i]
    rest = {0: mass - total[0] - total[1] - total[2], 1: total[0], 5: total[2], plain: total[1]}
    return message + [rest[i] if i in rest else far_row[i] for i in far]


def write_rims(bottom, top, rim_a, rim_b):
    even = lax.rem(lax.axis_index("gy"), 2) == 0

    def row(edge, n):
        return [edge[i, :, n, :] for i in range(19)]

    up = rim_message(row(top, SUB - 1), row(top, SUB - 2), 1)
    down = rim_message(row(bottom, 0), row(bottom, 1), -1)
    for n in range(len(up)):
        rim_a[n] = jnp.where(even, up[n], down[n])
        rim_b[n] = jnp.where(even, down[n], up[n])


def collided(fields, forcing):
    pair_sum, pair_diff = {}, {}
    for i in range(1, 19, 2):
        pair_sum[i] = fields[i] + fields[i + 1]
        pair_diff[i] = fields[i] - fields[i + 1]
    density = fields[0]
    for i in range(1, 19, 2):
        density = density + pair_sum[i]
    momentum = []
    for k in range(3):
        total = relax_time * forcing[k]
        for i in range(1, 19, 2):
            if velocities[i, k] == 1:
                total = total + pair_diff[i]
            elif velocities[i, k] == -1:
                total = total - pair_diff[i]
        momentum.append(total)
    inverse = 1.0 / density
    keep = 1.0 - 1.0 / relax_time
    squares = momentum[0] * momentum[0] + momentum[1] * momentum[1] + momentum[2] * momentum[2]
    level = density - 1.5 * inverse * squares
    curve = 4.5 * inverse
    result = [None] * 19
    result[0] = keep * fields[0] + (lattice_weights[0] / relax_time) * level
    for i in range(1, 19, 2):
        along = None
        for k in range(3):
            if velocities[i, k] == 1:
                along = momentum[k] if along is None else along + momentum[k]
            elif velocities[i, k] == -1:
                along = -momentum[k] if along is None else along - momentum[k]
        share = lattice_weights[i] / relax_time
        even = share * (level + curve * along * along)
        odd = (3.0 * share) * along
        result[i] = keep * fields[i] + (even + odd)
        result[i + 1] = keep * fields[i + 1] + (even - odd)
    return result


def keep_tile(relaxed, tiles, x, t, values):
    for i in range(19):
        if t < tiles:
            relaxed[i, x, SUB + SUB * t : 2 * SUB + SUB * t, :] = values[i]
        else:
            relaxed[i, x, 0:SUB, :] = values[i]
            relaxed[i, x, SUB + SUB * tiles : 2 * SUB + SUB * tiles, :] = values[i]


def write_faces(relaxed, forcing, slabs, tiles, walls, face_a, face_b):
    even = lax.rem(lax.axis_index("gx"), 2) == 0
    for t in range(tiles + 1):
        low = SUB + SUB * t
        sides = []
        for going, plane in ((going_east, slabs - 1), (going_west, 0)):
            fields = streamed(relaxed, None, None, slabs, tiles, plane, t, walls, going + staying)
            mass = None
            for value in fields.values():
                mass = value if mass is None else mass + value
            message = [relaxed[i, plane, low : low + SUB, :] for i in going]
            message += [fields[i] for i in going] + [mass]
            for k in range(3):
                total = relax_time * forcing[k, plane, SUB * t : SUB * t + SUB, :]
                message.append(with_signs(total, fields, k))
            sides.append(message)
        for n in range(FACE_FIELDS):
            east, west = sides[0][n], sides[1][n]
            a, b = jnp.where(even, east, west), jnp.where(even, west, east)
            if t < tiles:
                at = SUB * (tiles * n + t)
                face_a[at : at + SUB, :] = a
                face_b[at : at + SUB, :] = b
            else:
                at = SUB * tiles * FACE_FIELDS + 2 * n
                for j, row in enumerate(rim_sublanes(n)):
                    face_a[at + j : at + j + 1, :] = a[row : row + 1, :]
                    face_b[at + j : at + j + 1, :] = b[row : row + 1, :]


def rim_sublanes(n):
    along = int(velocities[going_east[n], 1]) if n < 5 else 0
    return {0: (7, 0), 1: (6, 7), -1: (0, 1)}[along]


def with_signs(total, fields, k):
    for i, value in fields.items():
        if velocities[i, k] == 1:
            total = total + value
        elif velocities[i, k] == -1:
            total = total - value
    return total


def unpack_faces(face_a, face_b, tiles, rim_west, rim_east):
    even = lax.rem(lax.axis_index("gx"), 2) == 0
    for n in range(5):
        for t in range(tiles):
            at = SUB * (tiles * n + t)
            a, b = face_a[at : at + SUB, :], face_b[at : at + SUB, :]
            keep_rim(rim_west, n, tiles, t, jnp.where(even, b, a))
            keep_rim(rim_east, n, tiles, t, jnp.where(even, a, b))
        at = SUB * tiles * FACE_FIELDS + 2 * n
        for j, row in enumerate(rim_sublanes(n)):
            a, b = face_a[at + j : at + j + 1, :], face_b[at + j : at + j + 1, :]
            places = [row] if row >= 4 else [row, SUB + SUB * tiles + row]
            for place in places:
                rim_west[n, place : place + 1, :] = jnp.where(even, b, a)
                rim_east[n, place : place + 1, :] = jnp.where(even, a, b)


def keep_rim(rim, n, tiles, t, value):
    low = SUB + SUB * t
    rim[n, low : low + SUB, :] = value
    if t == tiles:
        rim[n, 0:SUB, :] = value


def relax_rim(
    relaxed, rims, slabs, tiles, walls, face_a, face_b, going, back, plane, is_west, after
):
    even = lax.rem(lax.axis_index("gx"), 2) == 0
    for t in range(tiles + 1):

        def got(n):
            at = SUB * (tiles * n + t) if t < tiles else SUB * tiles * FACE_FIELDS + 2 * n
            size = SUB if t < tiles else 1
            a, b = face_a[at : at + size, :], face_b[at : at + size, :]
            value = jnp.where(even, b, a) if is_west else jnp.where(even, a, b)
            if t < tiles:
                return value
            a, b = face_a[at + 1 : at + 2, :], face_b[at + 1 : at + 2, :]
            last = jnp.where(even, b, a) if is_west else jnp.where(even, a, b)
            return jnp.where(sub_iota() >= 4, value, last)

        fields = streamed(relaxed, rims[0], rims[1], slabs, tiles, plane, t, walls, back)
        density = got(10)
        for value in fields.values():
            density = density + value
        momentum = [with_signs(got(11 + k), fields, k) for k in range(3)]
        inward = {i: got(5 + n) for n, i in enumerate(going)}
        for n, value in enumerate(collided_some(inward, density, momentum).values()):
            keep_rim(after, n, tiles, t, value)


def collided_some(fields, density, momentum):
    inverse = 1.0 / density
    keep = 1.0 - 1.0 / relax_time
    squares = momentum[0] * momentum[0] + momentum[1] * momentum[1] + momentum[2] * momentum[2]
    level = density - 1.5 * inverse * squares
    curve = 4.5 * inverse
    result = {}
    for i, value in fields.items():
        along = jnp.zeros_like(density)
        for k in range(3):
            if velocities[i, k] == 1:
                along = along + momentum[k]
            elif velocities[i, k] == -1:
                along = along - momentum[k]
        share = lattice_weights[i] / relax_time
        result[i] = keep * value + (share * (level + curve * along * along) + (3.0 * share) * along)
    return result


def streamed(relaxed, rim_west, rim_east, slabs, tiles, x, t, walls, chosen=tuple(range(19))):
    lane, sub = lane_iota(), sub_iota()

    def rows(i, plane, low):
        if plane < 0:
            return rim_west[going_east.index(i), low : low + SUB, :]
        if plane >= slabs:
            return rim_east[going_west.index(i), low : low + SUB, :]
        return relaxed[i, plane, low : low + SUB, :]

    low = SUB + SUB * t if t < tiles else 0
    high = SUB + SUB * tiles
    result = {}
    for i in chosen:
        ex, ey, ez = (int(v) for v in velocities[i])
        plane = x - ex
        if t < tiles or ey == 0:
            source = rows(i, plane, low - ey)
        elif ey == 1:
            source = jnp.where(
                sub >= 4, pltpu.roll(rows(i, plane, 0), 1, 0), rows(i, plane, high - 1)
            )
        else:
            source = jnp.where(
                sub >= 4, rows(i, plane, 1), pltpu.roll(rows(i, plane, high), SUB - 1, 0)
            )
        outside = None
        if ez == 1:
            source = pltpu.roll(source, 1, 1)
            outside = lane == 0
        elif ez == -1:
            source = pltpu.roll(source, LANES - 1, 1)
            outside = lane == LANES - 1
        wall = None
        if t == 0 and ey == 1:
            wall = (sub == 0) & walls[0]
        if t == tiles - 1 and ey == -1:
            wall = (sub == SUB - 1) & walls[1]
        if wall is not None:
            outside = wall if outside is None else outside | wall
        if outside is not None:
            source = jnp.where(outside, rows(opposite[i], x, low), source)
        result[i] = source
    return result


def wall_flags():
    strip = lax.axis_index("gy")
    return strip == 0, strip == lax.axis_size("gy") - 1


def first_kernel(
    capacity,
    got,
    populations,
    rim_a,
    rim_b,
    relaxed,
    face_a,
    face_b,
    forcing,
    items,
    codes,
    arrived,
    placed,
    rim,
    listing,
    spare,
    crowd,
    sem,
):
    slabs, strip_cells = populations.shape[1], populations.shape[2]
    tiles = strip_cells // SUB
    sources = got.shape[0]
    nowhere = SUB * LANES
    lane, sub = lane_iota(), sub_iota()
    arrived[pl.ds(sources * 16, 16), :] = jnp.zeros((16, LANES), jnp.float32)

    def gather(s, _):
        tile = got[s].astype(jnp.float32)
        upper, lower = tile[0:SUB, :], tile[SUB:16, :]
        own_lanes = lane < REST_LANE
        back = LANES - REST_LANE
        new_upper = jnp.where(own_lanes, upper + pltpu.roll(upper, back, 1), upper)
        new_lower = jnp.where(own_lanes, lower + pltpu.roll(lower, back, 1), lower)
        if 2 * capacity > WIDE_DUPS:
            here = (lane >= REST_LANE) & (lane < REST_LANE + GROUP)
            first_rows = pltpu.roll(lower, 4, 0)
            upper_dups = jnp.where(
                sub < 4,
                pltpu.roll(first_rows, REST_LANE, 1),
                pltpu.roll(lower, REST_LANE - GROUP, 1),
            )
            lower_dups = pltpu.roll(first_rows, REST_LANE - 2 * GROUP, 1)
            new_upper = jnp.where(here, upper_dups, new_upper)
            new_lower = jnp.where(here & (sub < 4), lower_dups, new_lower)
        at = pl.multiple_of(s * 16, 16)
        arrived[pl.ds(at, SUB), :] = new_upper
        arrived[pl.ds(at + SUB, SUB), :] = new_lower
        return 0

    lax.fori_loop(0, sources, gather, 0, unroll=8)
    first_dup = CODE_LANE + capacity
    for n in range(sources // SUB):
        row = arrived[pl.ds(SUB * n * 16 + 12, SUB, stride=16), :].astype(jnp.int32)
        column = arrived[pl.ds(SUB * n * 16 + 13, SUB, stride=16), :].astype(jnp.int32)
        code = row * LANES + column - 1
        source = sub + SUB * n
        is_dup = lane >= first_dup
        slot = jnp.where(is_dup, source * 8 + lane - first_dup, source * 4 + lane - CODE_LANE)
        item = jnp.where(code >= 0, slot * 8192 + code, -1)
        busy = jnp.where(is_dup & (lane < first_dup + 2 * capacity) & (code >= 0), 1.0, 0.0)
        busy = jnp.sum(busy, axis=1, keepdims=True)
        item = jnp.where(lane == LANES - 1, jnp.where(busy > 0.0, 1, 0), item)
        corner = pltpu.roll(jnp.maximum(code, nowhere), LANES - CODE_LANE, 1)
        items[SUB * n : SUB * n + SUB, :] = jnp.where(lane < capacity, corner, item)
    copy = pltpu.make_async_copy(items, codes, sem)
    copy.start()
    even = lax.rem(lax.axis_index("gy"), 2) == 0
    rim[...] = jnp.zeros_like(rim)
    for toward in (1, -1):
        _, near, far, _ = fold_tables(toward)
        for n, i in enumerate(near + far):
            a, b = rim_a[n], rim_b[n]
            value = jnp.where(even, b, a) if toward == 1 else jnp.where(even, a, b)
            if toward == 1:
                at = 7 if n < len(near) else 6
            else:
                at = 0 if n < len(near) else 1
            rim[i, :, at, :] = value
    placed[...] = jnp.zeros_like(placed)
    copy.wait()

    def note(s, carry):
        own, some = carry
        for r in range(capacity):
            item = codes[s, CODE_LANE + r]
            listing[own >> 7, own & 127] = item
            own = own + 1 + (item >> 31)
        crowd[some] = s
        return own, some + codes[s, LANES - 1]

    own_count, some = lax.fori_loop(0, sources, note, (jnp.int32(0), jnp.int32(0)), unroll=8)

    def note_dup(n, dup):
        s = crowd[n]
        for r in range(2 * capacity):
            item = codes[s, first_dup + r]
            spare[dup] = item
            dup = dup + 1 + (item >> 31)
        return dup

    dup_count = lax.fori_loop(0, some, note_dup, jnp.int32(0))
    for j in range(STEP - 1):
        at = own_count + j
        listing[at >> 7, at & 127] = sources * 4 * 8192 + nowhere

    def moved_rows(source, z, lanes_at, steps):
        inside = (lane >= z) & (lane < z + STEN)
        rows = {}
        for h in range(2):
            tile = arrived[pl.ds(pl.multiple_of(source * 16, 16) + SUB * h, SUB), :]
            for b in range(steps):
                shift = (z - lanes_at - STEN * b + 2 * LANES) & (LANES - 1)
                rows[b, h] = jnp.where(inside, pltpu.roll(tile, shift, 1), 0.0)
        return rows

    def add_rows(rows, y):
        at = {
            (b, h): pl.ds(pl.multiple_of((y + b) * 16 + SUB * h, SUB), SUB) for b, h in rows
        }
        old = {key: placed[at[key], :] for key in rows}
        for key in rows:
            placed[at[key], :] = old[key] + rows[key]

    def place_own(n, _):
        todo = []
        for j in range(STEP):
            at = STEP * n + j
            item = listing[at >> 7, at & 127]
            slot, code = item >> 13, item & 8191
            todo.append(
                (moved_rows(slot >> 2, code & (LANES - 1), GROUP * (slot & 3), 4), code >> 7)
            )
        for rows, y in todo:
            add_rows(rows, y)
        return 0

    lax.fori_loop(0, (own_count + STEP - 1) // STEP, place_own, 0)

    def place_dup(n, _):
        item = spare[n]
        slot, code = item >> 13, item & 8191
        q = slot & 7
        low = jnp.where(q < capacity, 2, 0)
        at = 8 * q + jnp.where(q < WIDE_DUPS, DUP_LANE, REST_LANE - 8 * WIDE_DUPS)
        rows = moved_rows(slot >> 3, code & (LANES - 1), at, 2)
        add_rows(rows, (code >> 7) + low)
        return 0

    lax.fori_loop(0, dup_count, place_dup, 0)
    for x in range(slabs):
        for t in range(tiles + 1):
            push = []
            for k in range(3):
                if t < tiles:
                    value = placed[pl.ds((SUB + SUB * t) * 16 + 4 * k + x, SUB, stride=16), :]
                else:
                    value = jnp.where(
                        sub >= 4,
                        placed[pl.ds(4 * k + x, SUB, stride=16), :],
                        placed[pl.ds((SUB + SUB * tiles) * 16 + 4 * k + x, SUB, stride=16), :],
                    )
                forcing[k, x, SUB * t : SUB * t + SUB, :] = value
                push.append(value)
            if t < tiles:
                fields = [populations[i, x, SUB * t : SUB * t + SUB, :] for i in range(19)]
            else:
                fields = [rim[i, x] for i in range(19)]
            keep_tile(relaxed, tiles, x, t, collided(fields, push))
    write_faces(relaxed, forcing, slabs, tiles, wall_flags(), face_a, face_b)


def second_kernel(
    capacity,
    items,
    before,
    got_a,
    got_b,
    forcing,
    populations_far,
    speeds,
    corners,
    populations,
    relaxed,
    rim_west,
    rim_east,
    after_west,
    after_east,
    fluid,
    sems,
):
    slabs = before.shape[1]
    corner_copy = pltpu.make_async_copy(items, corners, sems.at[slabs])
    corner_copy.start()
    tiles = before.shape[2] // SUB - 2
    unpack_faces(got_a, got_b, tiles, rim_west, rim_east)
    walls = wall_flags()
    rims = (rim_west, rim_east)
    relax_rim(
        before, rims, slabs, tiles, walls, got_a, got_b, going_east, going_west, -1, True, after_west
    )
    relax_rim(
        before,
        rims,
        slabs,
        tiles,
        walls,
        got_a,
        got_b,
        going_west,
        going_east,
        slabs,
        False,
        after_east,
    )
    for x in range(slabs):
        for t in range(tiles + 1):
            fields = streamed(before, rim_west, rim_east, slabs, tiles, x, t, walls)
            push = [forcing[k, x, SUB * t : SUB * t + SUB, :] for k in range(3)]
            keep_tile(relaxed, tiles, x, t, collided(fields, push))
    copies = []
    for x in range(slabs):
        for t in range(tiles):
            fields = streamed(relaxed, after_west, after_east, slabs, tiles, x, t, walls)
            density = fields[0]
            for i in range(1, 19):
                density = density + fields[i]
            inverse = 1.0 / density
            for i in range(19):
                populations[i, x, SUB * t : SUB * t + SUB, :] = fields[i]
            for k in range(3):
                total = 0.5 * forcing[k, x, SUB * t : SUB * t + SUB, :]
                for i in range(19):
                    if velocities[i, k] == 1:
                        total = total + fields[i]
                    elif velocities[i, k] == -1:
                        total = total - fields[i]
                fluid[pl.ds(SUB * t * 16 + 4 * k + x, SUB, stride=16), :] = total * inverse
        copies.append(
            pltpu.make_async_copy(populations.at[:, x], populations_far.at[:, x], sems.at[x])
        )
        copies[x].start()
    lane = lane_iota()
    corner_copy.wait()

    def pick(s, _):
        corner = [corners[s, r] for r in range(capacity)]
        tile = jnp.zeros((SUB, LANES), jnp.float32)
        for h in range(2):
            for r in range(capacity):
                y, z = (corner[r] >> 7) - SUB, corner[r] & (LANES - 1)
                for b in range(4):
                    low = GROUP * (h * capacity + r) + STEN * b
                    row = pl.multiple_of((y + b) * 16 + SUB * h, SUB)
                    shift = (low - z + LANES) & (LANES - 1)
                    moved = pltpu.roll(fluid[pl.ds(row, SUB), :], shift, 1)
                    tile = jnp.where((lane >= low) & (lane < low + STEN), moved, tile)
        speeds[s] = tile.astype(jnp.bfloat16)
        return 0

    lax.fori_loop(0, speeds.shape[0], pick, 0, unroll=8)
    for copy in copies:
        copy.wait()


def marker_kernel(
    capacity, owner, swimmer, returned, weights, velocity, total, chosen, expanded, count
):
    held = weights.shape[0]
    cells = weights.shape[1]
    targets = returned.shape[0]
    lane, sub = lane_iota(16), sub_iota(16)
    sub8, lane8 = sub_iota(), lane_iota()

    def reset(i, _):
        count[i] = 0
        return 0

    lax.fori_loop(0, targets, reset, 0, unroll=16)
    for b in range(held):
        target = owner[0, b]
        rank = count[target]
        count[target] = rank + 1
        low = GROUP * rank
        tile = returned[target].astype(jnp.float32)
        first = jnp.where((lane8 >= low) & (lane8 < low + GROUP), tile, 0.0)
        low = low + GROUP * capacity
        second = jnp.where((lane8 >= low) & (lane8 < low + GROUP), tile, 0.0)
        chosen[16 * b : 16 * b + 16, :] = jnp.concatenate([first, second], axis=0).astype(
            jnp.bfloat16
        )
    across = lax.broadcasted_iota(jnp.int32, (LANES, LANES), 1)
    down = lax.broadcasted_iota(jnp.int32, (LANES, LANES), 0)
    repeat = jnp.where(across % GROUP == down % GROUP, 1.0, 0.0).astype(jnp.bfloat16)
    own_cells = (lane // GROUP) % 4 == sub % 4
    for g in range(held // SUB):
        wide = jnp.dot(
            chosen[LANES * g : LANES * g + LANES, :], repeat, preferred_element_type=jnp.float32
        )
        for j in range(SUB):
            expanded[LANES * g + 16 * j : LANES * g + 16 * j + 16, :] = jnp.where(
                own_cells, wide[16 * j : 16 * j + 16, :], 0.0
            )
    sums = {}
    for g in range(held // SUB):
        pieces = []
        for k in range(3):
            row = None
            for x in range(4):
                part = expanded[pl.ds(LANES * g + 4 * k + x, SUB, stride=16), :]
                row = part if row is None else row + part
            pieces.append(
                jnp.concatenate(
                    [
                        jnp.where(sub8 == 2 * pair + lane8 // 64, row, 0.0).astype(jnp.bfloat16)
                        for pair in range(4)
                    ],
                    axis=1,
                )
            )
        left = jnp.concatenate(pieces, axis=0)
        right = weights[SUB * g : SUB * g + SUB].reshape(SUB * cells, LANES)
        out = speed_scale * jnp.dot(left, right, preferred_element_type=jnp.float32)
        member = jnp.zeros((SUB, LANES), jnp.int32)
        for j in range(SUB):
            member = jnp.where(sub8 == j, lax.rem(swimmer[SUB * g + j], SWIM_DEV), member)
        for k in range(3):
            part = out[SUB * k : SUB * k + SUB, :]
            velocity[k, SUB * g : SUB * g + SUB, :] = part
            for s in range(SWIM_DEV):
                term = jnp.where(member == s, part, 0.0)
                sums[k, s] = term if g == 0 else sums[k, s] + term
    table = jnp.zeros((SUB, LANES), jnp.float32)
    for (k, s), value in sums.items():
        mean = jnp.sum(value) * (1.0 / LANES)
        table = jnp.where((sub8 == k) & (lane8 == s), mean, table)
    total[...] = table[0:3, 0:SWIM_DEV]


VM = pl.BlockSpec(memory_space=pltpu.VMEM)
SM = pl.BlockSpec(memory_space=pltpu.SMEM)
FAR = pl.BlockSpec(memory_space=pltpu.HBM)


def shaped(shape, dtype=jnp.float32):
    return jax.ShapeDtypeStruct(shape, dtype)


def step(populations, marker_weights, marker_force, owner_device, stencil_base, block_swimmer):
    slab_cells, strip_cells, height = populations.shape[1:]
    strips = lax.axis_size("gy")
    devices = lax.axis_size("gx") * strips
    held = marker_weights.shape[0]
    capacity = max(2, (2 * held + devices - 1) // devices)
    padded_rows = strip_cells + 2 * SUB
    packed_rows = strip_cells + SUB
    f32 = jnp.float32
    small = pltpu.CompilerParams(vmem_limit_bytes=12 * 1024 * 1024)

    owner = owner_device.T
    force = marker_force.transpose(1, 0, 2)
    edge = shaped((27, slab_cells, height))
    edge_rows = pltpu.VMEM((19, slab_cells, SUB, height), f32)
    sent, rim_a, rim_b = pl.pallas_call(
        functools.partial(patch_kernel, capacity, strips),
        out_shape=(shaped((devices, 16, LANES), jnp.bfloat16), edge, edge),
        in_specs=[FAR] * 5,
        out_specs=(VM, VM, VM),
        scratch_shapes=[
            pltpu.SMEM(owner.shape, jnp.int32),
            pltpu.SMEM((3, held), jnp.int32),
            pltpu.VMEM(marker_weights.shape, jnp.bfloat16),
            pltpu.VMEM(force.shape, jnp.bfloat16),
            edge_rows,
            edge_rows,
            pltpu.VMEM((3, held, LANES), f32),
            pltpu.VMEM((held * 16, LANES), f32),
            pltpu.VMEM((held, 16, LANES), f32),
            pltpu.VMEM((devices, 16, LANES), f32),
            pltpu.SMEM((devices,), jnp.int32),
            pltpu.SMEM((held,), jnp.int32),
            pltpu.SMEM((held + 1,), jnp.int32),
            pltpu.SemaphoreType.DMA((9,)),
        ],
        name="patches",
    )(owner, stencil_base.T, marker_weights, force, populations)
    got = lax.all_to_all(sent, ("gx", "gy"), split_axis=0, concat_axis=0, tiled=True)
    rim_a, rim_b = swapped(rim_a, rim_b, "gy", False)
    planes = shaped((19, slab_cells, padded_rows, height))
    face = shaped((FACE_FIELDS * strip_cells + 4 * SUB, height))
    push = shaped((3, slab_cells, packed_rows, height))
    rims = [pltpu.VMEM((5, padded_rows, height), f32)] * 4
    relaxed, face_a, face_b, forcing, items = pl.pallas_call(
        functools.partial(first_kernel, capacity),
        out_shape=(planes, face, face, push, shaped((devices, LANES), jnp.int32)),
        in_specs=[VM] * 4,
        out_specs=(VM, VM, VM, VM, VM),
        scratch_shapes=[
            pltpu.SMEM((devices, LANES), jnp.int32),
            pltpu.VMEM(((devices + 1) * 16, LANES), f32),
            pltpu.VMEM((padded_rows * 16, LANES), f32),
            pltpu.VMEM((19, slab_cells, SUB, LANES), f32),
            pltpu.SMEM((SUB, LANES), jnp.int32),
            pltpu.SMEM((devices * 2 * capacity + 1,), jnp.int32),
            pltpu.SMEM((devices + 1,), jnp.int32),
            pltpu.SemaphoreType.DMA,
        ],
        compiler_params=small,
        name="first",
    )(got, populations, rim_a, rim_b)
    got_a, got_b = swapped(face_a, face_b, "gx", True)
    fields, speeds = pl.pallas_call(
        functools.partial(second_kernel, capacity),
        out_shape=(shaped(populations.shape), shaped((devices, SUB, LANES), jnp.bfloat16)),
        in_specs=[VM, VM, VM, VM, VM],
        out_specs=(FAR, VM),
        scratch_shapes=[
            pltpu.SMEM((devices, LANES), jnp.int32),
            pltpu.VMEM(populations.shape, f32),
            pltpu.VMEM(planes.shape, f32),
        ]
        + rims
        + [
            pltpu.VMEM((strip_cells * 16, LANES), f32),
            pltpu.SemaphoreType.DMA((slab_cells + 1,)),
        ],
        compiler_params=small,
        name="second",
    )(items, relaxed, got_a, got_b, forcing)
    returned = lax.all_to_all(speeds, ("gx", "gy"), split_axis=0, concat_axis=0, tiled=True)
    marker_velocity, swimmer_velocity = pl.pallas_call(
        functools.partial(marker_kernel, capacity),
        out_shape=(shaped((3, held, LANES)), shaped((3, SWIM_DEV))),
        in_specs=[SM, SM, VM, VM],
        out_specs=(VM, VM),
        scratch_shapes=[
            pltpu.VMEM((held * 16, LANES), jnp.bfloat16),
            pltpu.VMEM((held * 16, LANES), f32),
            pltpu.SMEM((devices,), jnp.int32),
        ],
        compiler_params=small,
        name="markers",
    )(owner, block_swimmer, returned, marker_weights)
    return fields, marker_velocity.transpose(1, 0, 2), swimmer_velocity


def solution(mesh):
    in_specs = (
        P(None, "gx", "gy", None),
        P(("gx", "gy"), None, None),
        P(("gx", "gy"), None, None),
        P(("gx", "gy"), None),
        P(("gx", "gy"), None),
        P(("gx", "gy")),
    )
    out_specs = (P(None, "gx", "gy", None), P(("gx", "gy"), None, None), P(None, ("gx", "gy")))
    return jax.shard_map(step, mesh=mesh, in_specs=in_specs, out_specs=out_specs, check_vma=False)
```

```python
import functools

import jax
import jax.numpy as jnp
import numpy as np
from jax import lax
from jax.experimental import pallas as pl
from jax.experimental.pallas import tpu as pltpu
from jax.sharding import PartitionSpec as P


STEN = 4
SWIM_DEV = 4
LANES = 128
SUB = 8
GROUP = STEN * STEN
CODE_LANE = 64
REST_LANE = 48
DUP_LANE = 96
WIDE_DUPS = 4
STEP = 4

velocities = np.array(
    [
        [0, 0, 0],
        [1, 0, 0],
        [-1, 0, 0],
        [0, 1, 0],
        [0, -1, 0],
        [0, 0, 1],
        [0, 0, -1],
        [1, 1, 0],
        [-1, -1, 0],
        [1, -1, 0],
        [-1, 1, 0],
        [1, 0, 1],
        [-1, 0, -1],
        [1, 0, -1],
        [-1, 0, 1],
        [0, 1, 1],
        [0, -1, -1],
        [0, 1, -1],
        [0, -1, 1],
    ]
)
opposite = [0, 2, 1, 4, 3, 6, 5, 8, 7, 10, 9, 12, 11, 14, 13, 16, 15, 18, 17]
lattice_weights = [1.0 / 3.0] + [1.0 / 18.0] * 6 + [1.0 / 36.0] * 12
relax_time = 0.8
speed_scale = 20.0
going_east = [1, 7, 9, 11, 13]
going_west = [2, 10, 8, 12, 14]
staying = [0, 3, 4, 5, 6, 15, 16, 17, 18]
FACE_FIELDS = 14


def lane_iota(rows=SUB):
    return lax.broadcasted_iota(jnp.int32, (rows, LANES), 1)


def sub_iota(rows=SUB):
    return lax.broadcasted_iota(jnp.int32, (rows, LANES), 0)


def swapped(first, second, axis, periodic):
    size = lax.axis_size(axis)
    inner = [(i, i ^ 1) for i in range(size)]
    outer = []
    for i in range(size):
        j = i + 1 if i % 2 == 1 else i - 1
        if periodic:
            outer.append((i, j % size))
        elif 0 <= j < size:
            outer.append((i, j))
    second = lax.ppermute(second, axis, outer)
    first = lax.ppermute(first, axis, inner)
    return first, second


def patch_kernel(
    capacity,
    strips,
    owner_far,
    base_far,
    weights_far,
    force_far,
    populations,
    send,
    rim_a,
    rim_b,
    owner,
    base,
    weights,
    force,
    bottom,
    top,
    rows,
    spread,
    patches,
    record,
    count,
    place,
    again,
    sems,
):
    held = weights.shape[0]
    cells = weights.shape[1]
    strip_cells = populations.shape[2]
    pieces = sems.shape[0] - 5
    part_blocks = held // pieces
    force_copy = pltpu.make_async_copy(force_far, force, sems.at[pieces])
    force_copy.start()
    copies = [
        pltpu.make_async_copy(
            weights_far.at[part_blocks * n : part_blocks * (n + 1)],
            weights.at[part_blocks * n : part_blocks * (n + 1)],
            sems.at[n],
        )
        for n in range(pieces)
    ]
    copies.append(pltpu.make_async_copy(owner_far, owner, sems.at[pieces + 1]))
    copies.append(pltpu.make_async_copy(base_far, base, sems.at[pieces + 2]))
    edge_copies = [
        pltpu.make_async_copy(populations.at[:, :, 0:SUB, :], bottom, sems.at[pieces + 3]),
        pltpu.make_async_copy(
            populations.at[:, :, strip_cells - SUB : strip_cells, :], top, sems.at[pieces + 4]
        ),
    ]
    for copy in copies + edge_copies:
        copy.start()
    targets = send.shape[0]
    lane, sub = lane_iota(16), sub_iota(16)

    def clear(i, _):
        record[i] = jnp.zeros((16, LANES), jnp.float32)
        return 0

    lax.fori_loop(0, targets, clear, 0, unroll=16)

    def reset(i, _):
        count[i] = 0
        return 0

    lax.fori_loop(0, targets, reset, 0, unroll=16)
    for copy in copies[pieces:]:
        copy.wait()
    extra = jnp.int32(0)
    for b in range(held):
        target = owner[0, b]
        rank = count[target]
        count[target] = rank + 1
        place[b] = target * 4 + rank
        strip = lax.rem(target, strips)
        y = base[1, b]
        north = (y >= strip_cells - 5) & (strip < strips - 1)
        south = (y <= 1) & (strip > 0)
        again[extra] = b * 4 + rank
        extra = extra + jnp.where(north | south, 1, 0)
    force_copy.wait()
    for k in range(3):
        rows[k] = force[k].astype(jnp.float32)
    for b in range(held):
        for k in range(3):
            spread[16 * b + 4 * k : 16 * b + 4 * k + 4, :] = jnp.broadcast_to(
                rows[k, b : b + 1, :], (4, LANES)
            )
        spread[16 * b + 12 : 16 * b + 16, :] = jnp.zeros((4, LANES), jnp.float32)
    for g in range(held // 4):
        if 4 * g % part_blocks == 0:
            copies[4 * g // part_blocks].wait()
        out = lax.dot_general(
            spread[64 * g : 64 * g + 64, :].astype(jnp.bfloat16),
            weights[4 * g : 4 * g + 4].reshape(4 * cells, LANES),
            (((1,), (1,)), ((), ())),
            preferred_element_type=jnp.float32,
        )
        for j in range(4):
            half = j // 2
            part = out[16 * j : 16 * j + 16, LANES * half : LANES * half + LANES]
            part = jnp.where(lane // GROUP == 4 * (j % 2) + sub % 4, part, 0.0)
            part = part + pltpu.roll(part, 64, 1)
            part = part + pltpu.roll(part, 32, 1)
            part = part + pltpu.roll(part, 16, 1)
            patches[g * 4 + j] = part

    def labelled(tile, slot, frame_y, z):
        label = jnp.where(sub == 12, frame_y + SUB, z + 1).astype(jnp.float32)
        return jnp.where((lane == CODE_LANE + slot) & ((sub == 12) | (sub == 13)), label, tile)

    for b in range(held):
        target, rank = place[b] >> 2, place[b] & 3
        low = GROUP * rank
        inside = (lane >= low) & (lane < low + GROUP) & (sub < 12)
        tile = jnp.where(inside, patches[b], record[target])
        record[target] = labelled(tile, rank, base[1, b], base[2, b])

    def put_again(n, _):
        item = again[n]
        b, rank = item >> 2, item & 3
        y, z = base[1, b], base[2, b]
        to_south = y <= 1
        target = owner[0, b] + jnp.where(to_south, -1, 1)
        half = jnp.where(to_south, 0, 1)
        q = rank + jnp.where(to_south, capacity, 0)
        moved = pltpu.roll(patches[b], 8 * ((q + half) & 1), 1)
        wide = q < WIDE_DUPS
        low = jnp.where(wide, DUP_LANE + 8 * q, 2 * LANES)
        tile = jnp.where((lane >= low) & (lane < low + 8) & (sub < 12), moved, record[target])
        tile = labelled(
            tile, capacity + q, y + jnp.where(to_south, strip_cells, -strip_cells), z
        )
        if 2 * capacity > WIDE_DUPS:
            last = tile[12:16, :]
            lane4 = lane_iota(4)
            for k in range(3):
                low = jnp.where(wide, 2 * LANES, GROUP * k + 8 * (q - WIDE_DUPS))
                last = jnp.where(
                    (lane4 >= low) & (lane4 < low + 8), moved[4 * k : 4 * k + 4, :], last
                )
            tile = jnp.concatenate([tile[0:12, :], last], axis=0)
        record[target] = tile
        return 0

    lax.fori_loop(0, extra, put_again, 0)
    for copy in edge_copies:
        copy.wait()
    write_rims(bottom, top, rim_a, rim_b)
    rest_lanes = (lane >= REST_LANE) & (lane < 2 * REST_LANE) & (sub < 12)

    def finish(i, _):
        tile = record[i]
        rest = tile - tile.astype(jnp.bfloat16).astype(jnp.float32)
        tile = jnp.where(rest_lanes, pltpu.roll(rest, REST_LANE, 1), tile)
        send[i] = tile.astype(jnp.bfloat16)
        return 0

    lax.fori_loop(0, targets, finish, 0, unroll=8)


def fold_tables(toward):
    ahead = [i for i in range(19) if velocities[i, 1] == toward]
    plain = 4 if toward == 1 else 3
    to_east, to_west = (9, 8) if toward == 1 else (7, 10)
    near = [i for i in range(19) if i != to_west]
    far = ahead + [0, 1, 5, plain]
    return ahead, near, far, (plain, to_east, to_west)


def rim_message(near_row, far_row, toward):
    ahead, near, far, (plain, to_east, to_west) = fold_tables(toward)
    folded = {i: near_row[i] for i in near}
    folded[plain] = near_row[plain] + 2.0 * near_row[to_west]
    folded[to_east] = near_row[to_east] - near_row[to_west]
    message = [folded[i] for i in near]
    others = [i for i in range(19) if i not in ahead]
    total = [None, None, None]
    mass = None
    for i in others:
        mass = far_row[i] if mass is None else mass + far_row[i]
        for k in (0, 2):
            if velocities[i, k] != 0:
                term = far_row[i] if velocities[i, k] == 1 else -far_row[i]
                total[k] = term if total[k] is None else total[k] + term
        if velocities[i, 1] == -toward:
            total[1] = far_row[i] if total[1] is None else total[1] + far_row[i]
    rest = {0: mass - total[0] - total[1] - total[2], 1: total[0], 5: total[2], plain: total[1]}
    return message + [rest[i] if i in rest else far_row[i] for i in far]


def write_rims(bottom, top, rim_a, rim_b):
    even = lax.rem(lax.axis_index("gy"), 2) == 0

    def row(edge, n):
        return [edge[i, :, n, :] for i in range(19)]

    up = rim_message(row(top, SUB - 1), row(top, SUB - 2), 1)
    down = rim_message(row(bottom, 0), row(bottom, 1), -1)
    for n in range(len(up)):
        rim_a[n] = jnp.where(even, up[n], down[n])
        rim_b[n] = jnp.where(even, down[n], up[n])


def collided(fields, forcing):
    pair_sum, pair_diff = {}, {}
    for i in range(1, 19, 2):
        pair_sum[i] = fields[i] + fields[i + 1]
        pair_diff[i] = fields[i] - fields[i + 1]
    density = fields[0]
    for i in range(1, 19, 2):
        density = density + pair_sum[i]
    momentum = []
    for k in range(3):
        total = relax_time * forcing[k]
        for i in range(1, 19, 2):
            if velocities[i, k] == 1:
                total = total + pair_diff[i]
            elif velocities[i, k] == -1:
                total = total - pair_diff[i]
        momentum.append(total)
    inverse = 1.0 / density
    keep = 1.0 - 1.0 / relax_time
    squares = momentum[0] * momentum[0] + momentum[1] * momentum[1] + momentum[2] * momentum[2]
    level = density - 1.5 * inverse * squares
    curve = 4.5 * inverse
    result = [None] * 19
    result[0] = keep * fields[0] + (lattice_weights[0] / relax_time) * level
    for i in range(1, 19, 2):
        along = None
        for k in range(3):
            if velocities[i, k] == 1:
                along = momentum[k] if along is None else along + momentum[k]
            elif velocities[i, k] == -1:
                along = -momentum[k] if along is None else along - momentum[k]
        share = lattice_weights[i] / relax_time
        even = share * (level + curve * along * along)
        odd = (3.0 * share) * along
        result[i] = keep * fields[i] + (even + odd)
        result[i + 1] = keep * fields[i + 1] + (even - odd)
    return result


def keep_tile(relaxed, tiles, x, t, values):
    for i in range(19):
        if t < tiles:
            relaxed[i, x, SUB + SUB * t : 2 * SUB + SUB * t, :] = values[i]
        else:
            relaxed[i, x, 0:SUB, :] = values[i]
            relaxed[i, x, SUB + SUB * tiles : 2 * SUB + SUB * tiles, :] = values[i]


def write_faces(relaxed, forcing, slabs, tiles, walls, face_a, face_b):
    even = lax.rem(lax.axis_index("gx"), 2) == 0
    for t in range(tiles + 1):
        low = SUB + SUB * t
        sides = []
        for going, plane in ((going_east, slabs - 1), (going_west, 0)):
            fields = streamed(relaxed, None, None, slabs, tiles, plane, t, walls, going + staying)
            mass = None
            for value in fields.values():
                mass = value if mass is None else mass + value
            message = [relaxed[i, plane, low : low + SUB, :] for i in going]
            message += [fields[i] for i in going] + [mass]
            for k in range(3):
                total = relax_time * forcing[k, plane, SUB * t : SUB * t + SUB, :]
                message.append(with_signs(total, fields, k))
            sides.append(message)
        for n in range(FACE_FIELDS):
            east, west = sides[0][n], sides[1][n]
            a, b = jnp.where(even, east, west), jnp.where(even, west, east)
            if t < tiles:
                at = SUB * (tiles * n + t)
                face_a[at : at + SUB, :] = a
                face_b[at : at + SUB, :] = b
            else:
                at = SUB * tiles * FACE_FIELDS + 2 * n
                for j, row in enumerate(rim_sublanes(n)):
                    face_a[at + j : at + j + 1, :] = a[row : row + 1, :]
                    face_b[at + j : at + j + 1, :] = b[row : row + 1, :]


def rim_sublanes(n):
    along = int(velocities[going_east[n], 1]) if n < 5 else 0
    return {0: (7, 0), 1: (6, 7), -1: (0, 1)}[along]


def with_signs(total, fields, k):
    for i, value in fields.items():
        if velocities[i, k] == 1:
            total = total + value
        elif velocities[i, k] == -1:
            total = total - value
    return total


def unpack_faces(face_a, face_b, tiles, rim_west, rim_east):
    even = lax.rem(lax.axis_index("gx"), 2) == 0
    for n in range(5):
        for t in range(tiles):
            at = SUB * (tiles * n + t)
            a, b = face_a[at : at + SUB, :], face_b[at : at + SUB, :]
            keep_rim(rim_west, n, tiles, t, jnp.where(even, b, a))
            keep_rim(rim_east, n, tiles, t, jnp.where(even, a, b))
        at = SUB * tiles * FACE_FIELDS + 2 * n
        for j, row in enumerate(rim_sublanes(n)):
            a, b = face_a[at + j : at + j + 1, :], face_b[at + j : at + j + 1, :]
            places = [row] if row >= 4 else [row, SUB + SUB * tiles + row]
            for place in places:
                rim_west[n, place : place + 1, :] = jnp.where(even, b, a)
                rim_east[n, place : place + 1, :] = jnp.where(even, a, b)


def keep_rim(rim, n, tiles, t, value):
    low = SUB + SUB * t
    rim[n, low : low + SUB, :] = value
    if t == tiles:
        rim[n, 0:SUB, :] = value


def relax_rim(
    relaxed, rims, slabs, tiles, walls, face_a, face_b, going, back, plane, is_west, after
):
    even = lax.rem(lax.axis_index("gx"), 2) == 0
    for t in range(tiles + 1):

        def got(n):
            at = SUB * (tiles * n + t) if t < tiles else SUB * tiles * FACE_FIELDS + 2 * n
            size = SUB if t < tiles else 1
            a, b = face_a[at : at + size, :], face_b[at : at + size, :]
            value = jnp.where(even, b, a) if is_west else jnp.where(even, a, b)
            if t < tiles:
                return value
            a, b = face_a[at + 1 : at + 2, :], face_b[at + 1 : at + 2, :]
            last = jnp.where(even, b, a) if is_west else jnp.where(even, a, b)
            return jnp.where(sub_iota() >= 4, value, last)

        fields = streamed(relaxed, rims[0], rims[1], slabs, tiles, plane, t, walls, back)
        density = got(10)
        for value in fields.values():
            density = density + value
        momentum = [with_signs(got(11 + k), fields, k) for k in range(3)]
        inward = {i: got(5 + n) for n, i in enumerate(going)}
        for n, value in enumerate(collided_some(inward, density, momentum).values()):
            keep_rim(after, n, tiles, t, value)


def collided_some(fields, density, momentum):
    inverse = 1.0 / density
    keep = 1.0 - 1.0 / relax_time
    squares = momentum[0] * momentum[0] + momentum[1] * momentum[1] + momentum[2] * momentum[2]
    level = density - 1.5 * inverse * squares
    curve = 4.5 * inverse
    result = {}
    for i, value in fields.items():
        along = jnp.zeros_like(density)
        for k in range(3):
            if velocities[i, k] == 1:
                along = along + momentum[k]
            elif velocities[i, k] == -1:
                along = along - momentum[k]
        share = lattice_weights[i] / relax_time
        result[i] = keep * value + (share * (level + curve * along * along) + (3.0 * share) * along)
    return result


def streamed(relaxed, rim_west, rim_east, slabs, tiles, x, t, walls, chosen=tuple(range(19))):
    lane, sub = lane_iota(), sub_iota()

    def rows(i, plane, low):
        if plane < 0:
            return rim_west[going_east.index(i), low : low + SUB, :]
        if plane >= slabs:
            return rim_east[going_west.index(i), low : low + SUB, :]
        return relaxed[i, plane, low : low + SUB, :]

    low = SUB + SUB * t if t < tiles else 0
    high = SUB + SUB * tiles
    result = {}
    for i in chosen:
        ex, ey, ez = (int(v) for v in velocities[i])
        plane = x - ex
        if t < tiles or ey == 0:
            source = rows(i, plane, low - ey)
        elif ey == 1:
            source = jnp.where(
                sub >= 4, pltpu.roll(rows(i, plane, 0), 1, 0), rows(i, plane, high - 1)
            )
        else:
            source = jnp.where(
                sub >= 4, rows(i, plane, 1), pltpu.roll(rows(i, plane, high), SUB - 1, 0)
            )
        outside = None
        if ez == 1:
            source = pltpu.roll(source, 1, 1)
            outside = lane == 0
        elif ez == -1:
            source = pltpu.roll(source, LANES - 1, 1)
            outside = lane == LANES - 1
        wall = None
        if t == 0 and ey == 1:
            wall = (sub == 0) & walls[0]
        if t == tiles - 1 and ey == -1:
            wall = (sub == SUB - 1) & walls[1]
        if wall is not None:
            outside = wall if outside is None else outside | wall
        if outside is not None:
            source = jnp.where(outside, rows(opposite[i], x, low), source)
        result[i] = source
    return result


def wall_flags():
    strip = lax.axis_index("gy")
    return strip == 0, strip == lax.axis_size("gy") - 1


def place_kernel(
    capacity, got, placed, items, codes, arrived, listing, spare, crowd, sem
):
    sources = got.shape[0]
    nowhere = SUB * LANES
    lane, sub = lane_iota(), sub_iota()
    arrived[pl.ds(sources * 16, 16), :] = jnp.zeros((16, LANES), jnp.float32)
    for s in range(sources):
        arrived[16 * s + SUB : 16 * s + 16, :] = got[s].astype(jnp.float32)[SUB:16, :]
    first_dup = CODE_LANE + capacity
    for n in range(sources // SUB):
        row = arrived[pl.ds(SUB * n * 16 + 12, SUB, stride=16), :].astype(jnp.int32)
        column = arrived[pl.ds(SUB * n * 16 + 13, SUB, stride=16), :].astype(jnp.int32)
        code = row * LANES + column - 1
        source = sub + SUB * n
        is_dup = lane >= first_dup
        slot = jnp.where(is_dup, source * 8 + lane - first_dup, source * 4 + lane - CODE_LANE)
        item = jnp.where(code >= 0, slot * 8192 + code, -1)
        busy = jnp.where(is_dup & (lane < first_dup + 2 * capacity) & (code >= 0), 1.0, 0.0)
        busy = jnp.sum(busy, axis=1, keepdims=True)
        item = jnp.where(lane == LANES - 1, jnp.where(busy > 0.0, 1, 0), item)
        corner = pltpu.roll(jnp.maximum(code, nowhere), LANES - CODE_LANE, 1)
        items[SUB * n : SUB * n + SUB, :] = jnp.where(lane < capacity, corner, item)
    copy = pltpu.make_async_copy(items, codes, sem)
    copy.start()

    def gather(s, _):
        tile = got[s].astype(jnp.float32)
        upper, lower = tile[0:SUB, :], tile[SUB:16, :]
        own_lanes = lane < REST_LANE
        back = LANES - REST_LANE
        new_upper = jnp.where(own_lanes, upper + pltpu.roll(upper, back, 1), upper)
        new_lower = jnp.where(own_lanes, lower + pltpu.roll(lower, back, 1), lower)
        if 2 * capacity > WIDE_DUPS:
            here = (lane >= REST_LANE) & (lane < REST_LANE + GROUP)
            first_rows = pltpu.roll(lower, 4, 0)
            upper_dups = jnp.where(
                sub < 4,
                pltpu.roll(first_rows, REST_LANE, 1),
                pltpu.roll(lower, REST_LANE - GROUP, 1),
            )
            lower_dups = pltpu.roll(first_rows, REST_LANE - 2 * GROUP, 1)
            new_upper = jnp.where(here, upper_dups, new_upper)
            new_lower = jnp.where(here & (sub < 4), lower_dups, new_lower)
        at = pl.multiple_of(s * 16, 16)
        arrived[pl.ds(at, SUB), :] = new_upper
        arrived[pl.ds(at + SUB, SUB), :] = new_lower
        return 0

    lax.fori_loop(0, sources, gather, 0, unroll=8)
    placed[...] = jnp.zeros_like(placed)
    copy.wait()

    def note(s, carry):
        own, some = carry
        for r in range(capacity):
            item = codes[s, CODE_LANE + r]
            listing[own >> 7, own & 127] = item
            own = own + 1 + (item >> 31)
        crowd[some] = s
        return own, some + codes[s, LANES - 1]

    own_count, some = lax.fori_loop(0, sources, note, (jnp.int32(0), jnp.int32(0)), unroll=8)

    def note_dup(n, dup):
        s = crowd[n]
        for r in range(2 * capacity):
            item = codes[s, first_dup + r]
            spare[dup] = item
            dup = dup + 1 + (item >> 31)
        return dup

    dup_count = lax.fori_loop(0, some, note_dup, jnp.int32(0))
    for j in range(STEP - 1):
        at = own_count + j
        listing[at >> 7, at & 127] = sources * 4 * 8192 + nowhere

    def moved_rows(source, z, lanes_at, steps):
        inside = (lane >= z) & (lane < z + STEN)
        rows = {}
        for h in range(2):
            tile = arrived[pl.ds(pl.multiple_of(source * 16, 16) + SUB * h, SUB), :]
            for b in range(steps):
                shift = (z - lanes_at - STEN * b + 2 * LANES) & (LANES - 1)
                rows[b, h] = jnp.where(inside, pltpu.roll(tile, shift, 1), 0.0)
        return rows

    def add_rows(rows, y):
        at = {
            (b, h): pl.ds(pl.multiple_of((y + b) * 16 + SUB * h, SUB), SUB) for b, h in rows
        }
        old = {key: placed[at[key], :] for key in rows}
        for key in rows:
            placed[at[key], :] = old[key] + rows[key]

    def place_own(n, _):
        todo = []
        for j in range(STEP):
            at = STEP * n + j
            item = listing[at >> 7, at & 127]
            slot, code = item >> 13, item & 8191
            todo.append(
                (moved_rows(slot >> 2, code & (LANES - 1), GROUP * (slot & 3), 4), code >> 7)
            )
        for rows, y in todo:
            add_rows(rows, y)
        return 0

    lax.fori_loop(0, (own_count + STEP - 1) // STEP, place_own, 0)

    def place_dup(n, _):
        item = spare[n]
        slot, code = item >> 13, item & 8191
        q = slot & 7
        low = jnp.where(q < capacity, 2, 0)
        at = 8 * q + jnp.where(q < WIDE_DUPS, DUP_LANE, REST_LANE - 8 * WIDE_DUPS)
        rows = moved_rows(slot >> 3, code & (LANES - 1), at, 2)
        add_rows(rows, (code >> 7) + low)
        return 0

    lax.fori_loop(0, dup_count, place_dup, 0)


def first_kernel(placed, populations, rim_a, rim_b, relaxed, face_a, face_b, forcing, rim):
    slabs, strip_cells = populations.shape[1], populations.shape[2]
    tiles = strip_cells // SUB
    sub = sub_iota()
    even = lax.rem(lax.axis_index("gy"), 2) == 0
    rim[...] = jnp.zeros_like(rim)
    for toward in (1, -1):
        _, near, far, _ = fold_tables(toward)
        for n, i in enumerate(near + far):
            a, b = rim_a[n], rim_b[n]
            value = jnp.where(even, b, a) if toward == 1 else jnp.where(even, a, b)
            if toward == 1:
                at = 7 if n < len(near) else 6
            else:
                at = 0 if n < len(near) else 1
            rim[i, :, at, :] = value
    for x in range(slabs):
        for t in range(tiles + 1):
            push = []
            for k in range(3):
                if t < tiles:
                    value = placed[pl.ds((SUB + SUB * t) * 16 + 4 * k + x, SUB, stride=16), :]
                else:
                    value = jnp.where(
                        sub >= 4,
                        placed[pl.ds(4 * k + x, SUB, stride=16), :],
                        placed[pl.ds((SUB + SUB * tiles) * 16 + 4 * k + x, SUB, stride=16), :],
                    )
                forcing[k, x, SUB * t : SUB * t + SUB, :] = value
                push.append(value)
            if t < tiles:
                fields = [populations[i, x, SUB * t : SUB * t + SUB, :] for i in range(19)]
            else:
                fields = [rim[i, x] for i in range(19)]
            keep_tile(relaxed, tiles, x, t, collided(fields, push))
    write_faces(relaxed, forcing, slabs, tiles, wall_flags(), face_a, face_b)


def second_kernel(
    capacity,
    items,
    before,
    got_a,
    got_b,
    forcing,
    populations_far,
    speeds,
    corners,
    populations,
    relaxed,
    rim_west,
    rim_east,
    after_west,
    after_east,
    fluid,
    sems,
):
    slabs = before.shape[1]
    corner_copy = pltpu.make_async_copy(items, corners, sems.at[slabs])
    corner_copy.start()
    tiles = before.shape[2] // SUB - 2
    unpack_faces(got_a, got_b, tiles, rim_west, rim_east)
    walls = wall_flags()
    rims = (rim_west, rim_east)
    relax_rim(
        before, rims, slabs, tiles, walls, got_a, got_b, going_east, going_west, -1, True, after_west
    )
    relax_rim(
        before,
        rims,
        slabs,
        tiles,
        walls,
        got_a,
        got_b,
        going_west,
        going_east,
        slabs,
        False,
        after_east,
    )
    for x in range(slabs):
        for t in range(tiles + 1):
            fields = streamed(before, rim_west, rim_east, slabs, tiles, x, t, walls)
            push = [forcing[k, x, SUB * t : SUB * t + SUB, :] for k in range(3)]
            keep_tile(relaxed, tiles, x, t, collided(fields, push))
    copies = []
    for x in range(slabs):
        for t in range(tiles):
            fields = streamed(relaxed, after_west, after_east, slabs, tiles, x, t, walls)
            density = fields[0]
            for i in range(1, 19):
                density = density + fields[i]
            inverse = 1.0 / density
            for i in range(19):
                populations[i, x, SUB * t : SUB * t + SUB, :] = fields[i]
            for k in range(3):
                total = 0.5 * forcing[k, x, SUB * t : SUB * t + SUB, :]
                for i in range(19):
                    if velocities[i, k] == 1:
                        total = total + fields[i]
                    elif velocities[i, k] == -1:
                        total = total - fields[i]
                fluid[pl.ds(SUB * t * 16 + 4 * k + x, SUB, stride=16), :] = total * inverse
        copies.append(
            pltpu.make_async_copy(populations.at[:, x], populations_far.at[:, x], sems.at[x])
        )
        copies[x].start()
    lane = lane_iota()
    corner_copy.wait()

    def pick(s, _):
        corner = [corners[s, r] for r in range(capacity)]
        tile = jnp.zeros((SUB, LANES), jnp.float32)
        for h in range(2):
            for r in range(capacity):
                y, z = (corner[r] >> 7) - SUB, corner[r] & (LANES - 1)
                for b in range(4):
                    low = GROUP * (h * capacity + r) + STEN * b
                    row = pl.multiple_of((y + b) * 16 + SUB * h, SUB)
                    shift = (low - z + LANES) & (LANES - 1)
                    moved = pltpu.roll(fluid[pl.ds(row, SUB), :], shift, 1)
                    tile = jnp.where((lane >= low) & (lane < low + STEN), moved, tile)
        speeds[s] = tile.astype(jnp.bfloat16)
        return 0

    lax.fori_loop(0, speeds.shape[0], pick, 0, unroll=8)
    for copy in copies:
        copy.wait()


def marker_kernel(
    capacity, owner, swimmer, returned, weights, velocity, total, chosen, expanded, count
):
    held = weights.shape[0]
    cells = weights.shape[1]
    targets = returned.shape[0]
    lane, sub = lane_iota(16), sub_iota(16)
    sub8, lane8 = sub_iota(), lane_iota()

    def reset(i, _):
        count[i] = 0
        return 0

    lax.fori_loop(0, targets, reset, 0, unroll=16)
    for b in range(held):
        target = owner[0, b]
        rank = count[target]
        count[target] = rank + 1
        low = GROUP * rank
        tile = returned[target].astype(jnp.float32)
        first = jnp.where((lane8 >= low) & (lane8 < low + GROUP), tile, 0.0)
        low = low + GROUP * capacity
        second = jnp.where((lane8 >= low) & (lane8 < low + GROUP), tile, 0.0)
        chosen[16 * b : 16 * b + 16, :] = jnp.concatenate([first, second], axis=0).astype(
            jnp.bfloat16
        )
    across = lax.broadcasted_iota(jnp.int32, (LANES, LANES), 1)
    down = lax.broadcasted_iota(jnp.int32, (LANES, LANES), 0)
    repeat = jnp.where(across % GROUP == down % GROUP, 1.0, 0.0).astype(jnp.bfloat16)
    own_cells = (lane // GROUP) % 4 == sub % 4
    for g in range(held // SUB):
        wide = jnp.dot(
            chosen[LANES * g : LANES * g + LANES, :], repeat, preferred_element_type=jnp.float32
        )
        for j in range(SUB):
            expanded[LANES * g + 16 * j : LANES * g + 16 * j + 16, :] = jnp.where(
                own_cells, wide[16 * j : 16 * j + 16, :], 0.0
            )
    sums = {}
    for g in range(held // SUB):
        pieces = []
        for k in range(3):
            row = None
            for x in range(4):
                part = expanded[pl.ds(LANES * g + 4 * k + x, SUB, stride=16), :]
                row = part if row is None else row + part
            pieces.append(
                jnp.concatenate(
                    [
                        jnp.where(sub8 == 2 * pair + lane8 // 64, row, 0.0).astype(jnp.bfloat16)
                        for pair in range(4)
                    ],
                    axis=1,
                )
            )
        left = jnp.concatenate(pieces, axis=0)
        right = weights[SUB * g : SUB * g + SUB].reshape(SUB * cells, LANES)
        out = speed_scale * jnp.dot(left, right, preferred_element_type=jnp.float32)
        member = jnp.zeros((SUB, LANES), jnp.int32)
        for j in range(SUB):
            member = jnp.where(sub8 == j, lax.rem(swimmer[SUB * g + j], SWIM_DEV), member)
        for k in range(3):
            part = out[SUB * k : SUB * k + SUB, :]
            velocity[k, SUB * g : SUB * g + SUB, :] = part
            for s in range(SWIM_DEV):
                term = jnp.where(member == s, part, 0.0)
                sums[k, s] = term if g == 0 else sums[k, s] + term
    table = jnp.zeros((SUB, LANES), jnp.float32)
    for (k, s), value in sums.items():
        mean = jnp.sum(value) * (1.0 / LANES)
        table = jnp.where((sub8 == k) & (lane8 == s), mean, table)
    total[...] = table[0:3, 0:SWIM_DEV]


VM = pl.BlockSpec(memory_space=pltpu.VMEM)
SM = pl.BlockSpec(memory_space=pltpu.SMEM)
FAR = pl.BlockSpec(memory_space=pltpu.HBM)


def shaped(shape, dtype=jnp.float32):
    return jax.ShapeDtypeStruct(shape, dtype)


def step(populations, marker_weights, marker_force, owner_device, stencil_base, block_swimmer):
    slab_cells, strip_cells, height = populations.shape[1:]
    strips = lax.axis_size("gy")
    devices = lax.axis_size("gx") * strips
    held = marker_weights.shape[0]
    capacity = max(2, (2 * held + devices - 1) // devices)
    padded_rows = strip_cells + 2 * SUB
    packed_rows = strip_cells + SUB
    f32 = jnp.float32
    small = pltpu.CompilerParams(vmem_limit_bytes=12 * 1024 * 1024)

    owner = owner_device.T
    force = marker_force.transpose(1, 0, 2)
    edge = shaped((27, slab_cells, height))
    edge_rows = pltpu.VMEM((19, slab_cells, SUB, height), f32)
    sent, rim_a, rim_b = pl.pallas_call(
        functools.partial(patch_kernel, capacity, strips),
        out_shape=(shaped((devices, 16, LANES), jnp.bfloat16), edge, edge),
        in_specs=[FAR] * 5,
        out_specs=(VM, VM, VM),
        scratch_shapes=[
            pltpu.SMEM(owner.shape, jnp.int32),
            pltpu.SMEM((3, held), jnp.int32),
            pltpu.VMEM(marker_weights.shape, jnp.bfloat16),
            pltpu.VMEM(force.shape, jnp.bfloat16),
            edge_rows,
            edge_rows,
            pltpu.VMEM((3, held, LANES), f32),
            pltpu.VMEM((held * 16, LANES), f32),
            pltpu.VMEM((held, 16, LANES), f32),
            pltpu.VMEM((devices, 16, LANES), f32),
            pltpu.SMEM((devices,), jnp.int32),
            pltpu.SMEM((held,), jnp.int32),
            pltpu.SMEM((held + 1,), jnp.int32),
            pltpu.SemaphoreType.DMA((9,)),
        ],
        name="patches",
    )(owner, stencil_base.T, marker_weights, force, populations)
    got = lax.all_to_all(sent, ("gx", "gy"), split_axis=0, concat_axis=0, tiled=True)
    rim_a, rim_b = swapped(rim_a, rim_b, "gy", False)
    planes = shaped((19, slab_cells, padded_rows, height))
    face = shaped((FACE_FIELDS * strip_cells + 4 * SUB, height))
    push = shaped((3, slab_cells, packed_rows, height))
    rims = [pltpu.VMEM((5, padded_rows, height), f32)] * 4
    placed, items = pl.pallas_call(
        functools.partial(place_kernel, capacity),
        out_shape=(shaped((padded_rows * 16, LANES)), shaped((devices, LANES), jnp.int32)),
        in_specs=[VM],
        out_specs=(VM, VM),
        scratch_shapes=[
            pltpu.SMEM((devices, LANES), jnp.int32),
            pltpu.VMEM(((devices + 1) * 16, LANES), f32),
            pltpu.SMEM((SUB, LANES), jnp.int32),
            pltpu.SMEM((devices * 2 * capacity + 1,), jnp.int32),
            pltpu.SMEM((devices + 1,), jnp.int32),
            pltpu.SemaphoreType.DMA,
        ],
        compiler_params=small,
        name="place",
    )(got)
    relaxed, face_a, face_b, forcing = pl.pallas_call(
        first_kernel,
        out_shape=(planes, face, face, push),
        in_specs=[VM] * 4,
        out_specs=(VM, VM, VM, VM),
        scratch_shapes=[pltpu.VMEM((19, slab_cells, SUB, LANES), f32)],
        compiler_params=small,
        name="first",
    )(placed, populations, rim_a, rim_b)
    got_a, got_b = swapped(face_a, face_b, "gx", True)
    fields, speeds = pl.pallas_call(
        functools.partial(second_kernel, capacity),
        out_shape=(shaped(populations.shape), shaped((devices, SUB, LANES), jnp.bfloat16)),
        in_specs=[VM, VM, VM, VM, VM],
        out_specs=(FAR, VM),
        scratch_shapes=[
            pltpu.SMEM((devices, LANES), jnp.int32),
            pltpu.VMEM(populations.shape, f32),
            pltpu.VMEM(planes.shape, f32),
        ]
        + rims
        + [
            pltpu.VMEM((strip_cells * 16, LANES), f32),
            pltpu.SemaphoreType.DMA((slab_cells + 1,)),
        ],
        compiler_params=small,
        name="second",
    )(items, relaxed, got_a, got_b, forcing)
    returned = lax.all_to_all(speeds, ("gx", "gy"), split_axis=0, concat_axis=0, tiled=True)
    marker_velocity, swimmer_velocity = pl.pallas_call(
        functools.partial(marker_kernel, capacity),
        out_shape=(shaped((3, held, LANES)), shaped((3, SWIM_DEV))),
        in_specs=[SM, SM, VM, VM],
        out_specs=(VM, VM),
        scratch_shapes=[
            pltpu.VMEM((held * 16, LANES), jnp.bfloat16),
            pltpu.VMEM((held * 16, LANES), f32),
            pltpu.SMEM((devices,), jnp.int32),
        ],
        compiler_params=small,
        name="markers",
    )(owner, block_swimmer, returned, marker_weights)
    return fields, marker_velocity.transpose(1, 0, 2), swimmer_velocity


def solution(mesh):
    in_specs = (
        P(None, "gx", "gy", None),
        P(("gx", "gy"), None, None),
        P(("gx", "gy"), None, None),
        P(("gx", "gy"), None),
        P(("gx", "gy"), None),
        P(("gx", "gy")),
    )
    out_specs = (P(None, "gx", "gy", None), P(("gx", "gy"), None, None), P(None, ("gx", "gy")))
    return jax.shard_map(step, mesh=mesh, in_specs=in_specs, out_specs=out_specs, check_vma=False)
```

```python
import functools

import jax
import jax.numpy as jnp
import numpy as np
from jax import lax
from jax.experimental import pallas as pl
from jax.experimental.pallas import tpu as pltpu
from jax.sharding import PartitionSpec as P


STEN = 4
SWIM_DEV = 4
LANES = 128
SUB = 8
GROUP = STEN * STEN
CODE_LANE = 64
REST_LANE = 48
DUP_LANE = 96
WIDE_DUPS = 4
STEP = 8
DUP_STEP = 4

velocities = np.array(
    [
        [0, 0, 0],
        [1, 0, 0],
        [-1, 0, 0],
        [0, 1, 0],
        [0, -1, 0],
        [0, 0, 1],
        [0, 0, -1],
        [1, 1, 0],
        [-1, -1, 0],
        [1, -1, 0],
        [-1, 1, 0],
        [1, 0, 1],
        [-1, 0, -1],
        [1, 0, -1],
        [-1, 0, 1],
        [0, 1, 1],
        [0, -1, -1],
        [0, 1, -1],
        [0, -1, 1],
    ]
)
opposite = [0, 2, 1, 4, 3, 6, 5, 8, 7, 10, 9, 12, 11, 14, 13, 16, 15, 18, 17]
lattice_weights = [1.0 / 3.0] + [1.0 / 18.0] * 6 + [1.0 / 36.0] * 12
relax_time = 0.8
speed_scale = 20.0
going_east = [1, 7, 9, 11, 13]
going_west = [2, 10, 8, 12, 14]
staying = [0, 3, 4, 5, 6, 15, 16, 17, 18]
FACE_FIELDS = 14


def lane_iota(rows=SUB):
    return lax.broadcasted_iota(jnp.int32, (rows, LANES), 1)


def sub_iota(rows=SUB):
    return lax.broadcasted_iota(jnp.int32, (rows, LANES), 0)


def swapped(first, second, axis, periodic):
    size = lax.axis_size(axis)
    inner = [(i, i ^ 1) for i in range(size)]
    outer = []
    for i in range(size):
        j = i + 1 if i % 2 == 1 else i - 1
        if periodic:
            outer.append((i, j % size))
        elif 0 <= j < size:
            outer.append((i, j))
    second = lax.ppermute(second, axis, outer)
    first = lax.ppermute(first, axis, inner)
    return first, second


def patch_kernel(
    capacity,
    strips,
    owner_far,
    base_far,
    weights_far,
    force_far,
    populations,
    send,
    rim_a,
    rim_b,
    owner,
    base,
    weights,
    force,
    bottom,
    top,
    rows,
    spread,
    patches,
    record,
    count,
    place,
    again,
    sems,
):
    held = weights.shape[0]
    cells = weights.shape[1]
    strip_cells = populations.shape[2]
    pieces = sems.shape[0] - 5
    part_blocks = held // pieces
    force_copy = pltpu.make_async_copy(force_far, force, sems.at[pieces])
    force_copy.start()
    copies = [
        pltpu.make_async_copy(
            weights_far.at[part_blocks * n : part_blocks * (n + 1)],
            weights.at[part_blocks * n : part_blocks * (n + 1)],
            sems.at[n],
        )
        for n in range(pieces)
    ]
    copies.append(pltpu.make_async_copy(owner_far, owner, sems.at[pieces + 1]))
    copies.append(pltpu.make_async_copy(base_far, base, sems.at[pieces + 2]))
    edge_copies = [
        pltpu.make_async_copy(populations.at[:, :, 0:SUB, :], bottom, sems.at[pieces + 3]),
        pltpu.make_async_copy(
            populations.at[:, :, strip_cells - SUB : strip_cells, :], top, sems.at[pieces + 4]
        ),
    ]
    for copy in copies + edge_copies:
        copy.start()
    targets = send.shape[0]
    lane, sub = lane_iota(16), sub_iota(16)

    def clear(i, _):
        record[i] = jnp.zeros((16, LANES), jnp.float32)
        return 0

    lax.fori_loop(0, targets, clear, 0, unroll=16)

    def reset(i, _):
        count[i] = 0
        return 0

    lax.fori_loop(0, targets, reset, 0, unroll=16)
    extra = jnp.int32(0)
    powers = strips & (strips - 1) == 0
    force_copy.wait()
    for k in range(3):
        rows[k] = force[k].astype(jnp.float32)
    for b in range(held):
        for k in range(3):
            spread[16 * b + 4 * k : 16 * b + 4 * k + 4, :] = jnp.broadcast_to(
                rows[k, b : b + 1, :], (4, LANES)
            )
        spread[16 * b + 12 : 16 * b + 16, :] = jnp.zeros((4, LANES), jnp.float32)
    for g in range(held // 4):
        if g == 0:
            for copy in copies[pieces:]:
                copy.wait()
        if 4 * g % part_blocks == 0:
            copies[4 * g // part_blocks].wait()
        for b in range(4 * g, 4 * g + 4):
            target = owner[0, b]
            rank = count[target]
            count[target] = rank + 1
            place[b] = target * 4 + rank
            strip = target & (strips - 1) if powers else lax.rem(target, strips)
            y = base[1, b]
            north = (y >= strip_cells - 5) & (strip < strips - 1)
            south = (y <= 1) & (strip > 0)
            again[extra] = b * 4 + rank
            extra = extra + jnp.where(north | south, 1, 0)
        out = lax.dot_general(
            spread[64 * g : 64 * g + 64, :].astype(jnp.bfloat16),
            weights[4 * g : 4 * g + 4].reshape(4 * cells, LANES),
            (((1,), (1,)), ((), ())),
            preferred_element_type=jnp.float32,
        )
        for j in range(4):
            half = j // 2
            part = out[16 * j : 16 * j + 16, LANES * half : LANES * half + LANES]
            part = jnp.where(lane // GROUP == 4 * (j % 2) + sub % 4, part, 0.0)
            part = part + pltpu.roll(part, 64, 1)
            part = part + pltpu.roll(part, 32, 1)
            part = part + pltpu.roll(part, 16, 1)
            patches[g * 4 + j] = part

    def labelled(tile, slot, frame_y, z):
        label = jnp.where(sub == 12, frame_y + SUB, z + 1).astype(jnp.float32)
        return jnp.where((lane == CODE_LANE + slot) & ((sub == 12) | (sub == 13)), label, tile)

    for b in range(held):
        target, rank = place[b] >> 2, place[b] & 3
        low = GROUP * rank
        inside = (lane >= low) & (lane < low + GROUP) & (sub < 12)
        tile = jnp.where(inside, patches[b], record[target])
        record[target] = labelled(tile, rank, base[1, b], base[2, b])

    for j in range(DUP_STEP - 1):
        again[extra + j] = -1

    def put_again(n, _):
        todo = []
        for j in range(DUP_STEP):
            item = again[DUP_STEP * n + j]
            none = item < 0
            b, rank = jnp.where(none, 0, item >> 2), item & 3
            y, z = base[1, b], base[2, b]
            to_south = y <= 1
            target = jnp.where(none, targets, owner[0, b] + jnp.where(to_south, -1, 1))
            half = jnp.where(to_south, 0, 1)
            q = rank + jnp.where(to_south, capacity, 0)
            moved = pltpu.roll(patches[b], 8 * ((q + half) & 1), 1)
            frame_y = y + jnp.where(to_south, strip_cells, -strip_cells)
            todo.append((target, q, moved, frame_y, z))
        for target, q, moved, frame_y, z in todo:
            wide = q < WIDE_DUPS
            low = jnp.where(wide, DUP_LANE + 8 * q, 2 * LANES)
            tile = jnp.where((lane >= low) & (lane < low + 8) & (sub < 12), moved, record[target])
            tile = labelled(tile, capacity + q, frame_y, z)
            if 2 * capacity > WIDE_DUPS:
                last = tile[12:16, :]
                lane4 = lane_iota(4)
                for k in range(3):
                    low = jnp.where(wide, 2 * LANES, GROUP * k + 8 * (q - WIDE_DUPS))
                    last = jnp.where(
                        (lane4 >= low) & (lane4 < low + 8), moved[4 * k : 4 * k + 4, :], last
                    )
                tile = jnp.concatenate([tile[0:12, :], last], axis=0)
            record[target] = tile
        return 0

    lax.fori_loop(0, (extra + DUP_STEP - 1) // DUP_STEP, put_again, 0)
    for copy in edge_copies:
        copy.wait()
    write_rims(bottom, top, rim_a, rim_b)
    rest_lanes = (lane >= REST_LANE) & (lane < 2 * REST_LANE) & (sub < 12)

    def finish(i, _):
        tile = record[i]
        rest = tile - tile.astype(jnp.bfloat16).astype(jnp.float32)
        tile = jnp.where(rest_lanes, pltpu.roll(rest, REST_LANE, 1), tile)
        send[i] = tile.astype(jnp.bfloat16)
        return 0

    lax.fori_loop(0, targets, finish, 0, unroll=8)


def fold_tables(toward):
    ahead = [i for i in range(19) if velocities[i, 1] == toward]
    plain = 4 if toward == 1 else 3
    to_east, to_west = (9, 8) if toward == 1 else (7, 10)
    near = [i for i in range(19) if i != to_west]
    far = ahead + [0, 1, 5, plain]
    return ahead, near, far, (plain, to_east, to_west)


def rim_message(near_row, far_row, toward):
    ahead, near, far, (plain, to_east, to_west) = fold_tables(toward)
    folded = {i: near_row[i] for i in near}
    folded[plain] = near_row[plain] + 2.0 * near_row[to_west]
    folded[to_east] = near_row[to_east] - near_row[to_west]
    message = [folded[i] for i in near]
    others = [i for i in range(19) if i not in ahead]
    total = [None, None, None]
    mass = None
    for i in others:
        mass = far_row[i] if mass is None else mass + far_row[i]
        for k in (0, 2):
            if velocities[i, k] != 0:
                term = far_row[i] if velocities[i, k] == 1 else -far_row[i]
                total[k] = term if total[k] is None else total[k] + term
        if velocities[i, 1] == -toward:
            total[1] = far_row[i] if total[1] is None else total[1] + far_row[i]
    rest = {0: mass - total[0] - total[1] - total[2], 1: total[0], 5: total[2], plain: total[1]}
    return message + [rest[i] if i in rest else far_row[i] for i in far]


def write_rims(bottom, top, rim_a, rim_b):
    even = lax.rem(lax.axis_index("gy"), 2) == 0

    def row(edge, n):
        return [edge[i, :, n, :] for i in range(19)]

    up = rim_message(row(top, SUB - 1), row(top, SUB - 2), 1)
    down = rim_message(row(bottom, 0), row(bottom, 1), -1)
    for n in range(len(up)):
        rim_a[n] = jnp.where(even, up[n], down[n])
        rim_b[n] = jnp.where(even, down[n], up[n])


def collided(fields, forcing):
    pair_sum, pair_diff = {}, {}
    for i in range(1, 19, 2):
        pair_sum[i] = fields[i] + fields[i + 1]
        pair_diff[i] = fields[i] - fields[i + 1]
    density = fields[0]
    for i in range(1, 19, 2):
        density = density + pair_sum[i]
    momentum = []
    for k in range(3):
        total = relax_time * forcing[k]
        for i in range(1, 19, 2):
            if velocities[i, k] == 1:
                total = total + pair_diff[i]
            elif velocities[i, k] == -1:
                total = total - pair_diff[i]
        momentum.append(total)
    inverse = 1.0 / density
    keep = 1.0 - 1.0 / relax_time
    squares = momentum[0] * momentum[0] + momentum[1] * momentum[1] + momentum[2] * momentum[2]
    level = density - 1.5 * inverse * squares
    curve = 4.5 * inverse
    result = [None] * 19
    result[0] = keep * fields[0] + (lattice_weights[0] / relax_time) * level
    for i in range(1, 19, 2):
        along = None
        for k in range(3):
            if velocities[i, k] == 1:
                along = momentum[k] if along is None else along + momentum[k]
            elif velocities[i, k] == -1:
                along = -momentum[k] if along is None else along - momentum[k]
        share = lattice_weights[i] / relax_time
        even = share * (level + curve * along * along)
        odd = (3.0 * share) * along
        result[i] = keep * fields[i] + (even + odd)
        result[i + 1] = keep * fields[i + 1] + (even - odd)
    return result


def keep_tile(relaxed, tiles, x, t, values):
    for i in range(19):
        if t < tiles:
            relaxed[i, x, SUB + SUB * t : 2 * SUB + SUB * t, :] = values[i]
        else:
            relaxed[i, x, 0:SUB, :] = values[i]
            relaxed[i, x, SUB + SUB * tiles : 2 * SUB + SUB * tiles, :] = values[i]


def write_faces(relaxed, forcing, slabs, tiles, walls, face_a, face_b):
    even = lax.rem(lax.axis_index("gx"), 2) == 0
    for t in range(tiles + 1):
        low = SUB + SUB * t
        sides = []
        for going, plane in ((going_east, slabs - 1), (going_west, 0)):
            fields = streamed(relaxed, None, None, slabs, tiles, plane, t, walls, going + staying)
            mass = None
            for value in fields.values():
                mass = value if mass is None else mass + value
            message = [relaxed[i, plane, low : low + SUB, :] for i in going]
            message += [fields[i] for i in going] + [mass]
            for k in range(3):
                total = relax_time * forcing[k, plane, SUB * t : SUB * t + SUB, :]
                message.append(with_signs(total, fields, k))
            sides.append(message)
        for n in range(FACE_FIELDS):
            east, west = sides[0][n], sides[1][n]
            a, b = jnp.where(even, east, west), jnp.where(even, west, east)
            if t < tiles:
                at = SUB * (tiles * n + t)
                face_a[at : at + SUB, :] = a
                face_b[at : at + SUB, :] = b
            else:
                at = SUB * tiles * FACE_FIELDS + 2 * n
                for j, row in enumerate(rim_sublanes(n)):
                    face_a[at + j : at + j + 1, :] = a[row : row + 1, :]
                    face_b[at + j : at + j + 1, :] = b[row : row + 1, :]


def rim_sublanes(n):
    along = int(velocities[going_east[n], 1]) if n < 5 else 0
    return {0: (7, 0), 1: (6, 7), -1: (0, 1)}[along]


def with_signs(total, fields, k):
    for i, value in fields.items():
        if velocities[i, k] == 1:
            total = total + value
        elif velocities[i, k] == -1:
            total = total - value
    return total


def unpack_faces(face_a, face_b, tiles, rim_west, rim_east):
    even = lax.rem(lax.axis_index("gx"), 2) == 0
    for n in range(5):
        for t in range(tiles):
            at = SUB * (tiles * n + t)
            a, b = face_a[at : at + SUB, :], face_b[at : at + SUB, :]
            keep_rim(rim_west, n, tiles, t, jnp.where(even, b, a))
            keep_rim(rim_east, n, tiles, t, jnp.where(even, a, b))
        at = SUB * tiles * FACE_FIELDS + 2 * n
        for j, row in enumerate(rim_sublanes(n)):
            a, b = face_a[at + j : at + j + 1, :], face_b[at + j : at + j + 1, :]
            places = [row] if row >= 4 else [row, SUB + SUB * tiles + row]
            for place in places:
                rim_west[n, place : place + 1, :] = jnp.where(even, b, a)
                rim_east[n, place : place + 1, :] = jnp.where(even, a, b)


def keep_rim(rim, n, tiles, t, value):
    low = SUB + SUB * t
    rim[n, low : low + SUB, :] = value
    if t == tiles:
        rim[n, 0:SUB, :] = value


def relax_rim(
    relaxed, rims, slabs, tiles, walls, face_a, face_b, going, back, plane, is_west, after
):
    even = lax.rem(lax.axis_index("gx"), 2) == 0
    for t in range(tiles + 1):

        def got(n):
            at = SUB * (tiles * n + t) if t < tiles else SUB * tiles * FACE_FIELDS + 2 * n
            size = SUB if t < tiles else 1
            a, b = face_a[at : at + size, :], face_b[at : at + size, :]
            value = jnp.where(even, b, a) if is_west else jnp.where(even, a, b)
            if t < tiles:
                return value
            a, b = face_a[at + 1 : at + 2, :], face_b[at + 1 : at + 2, :]
            last = jnp.where(even, b, a) if is_west else jnp.where(even, a, b)
            return jnp.where(sub_iota() >= 4, value, last)

        fields = streamed(relaxed, rims[0], rims[1], slabs, tiles, plane, t, walls, back)
        density = got(10)
        for value in fields.values():
            density = density + value
        momentum = [with_signs(got(11 + k), fields, k) for k in range(3)]
        inward = {i: got(5 + n) for n, i in enumerate(going)}
        for n, value in enumerate(collided_some(inward, density, momentum).values()):
            keep_rim(after, n, tiles, t, value)


def collided_some(fields, density, momentum):
    inverse = 1.0 / density
    keep = 1.0 - 1.0 / relax_time
    squares = momentum[0] * momentum[0] + momentum[1] * momentum[1] + momentum[2] * momentum[2]
    level = density - 1.5 * inverse * squares
    curve = 4.5 * inverse
    result = {}
    for i, value in fields.items():
        along = jnp.zeros_like(density)
        for k in range(3):
            if velocities[i, k] == 1:
                along = along + momentum[k]
            elif velocities[i, k] == -1:
                along = along - momentum[k]
        share = lattice_weights[i] / relax_time
        result[i] = keep * value + (share * (level + curve * along * along) + (3.0 * share) * along)
    return result


def streamed(relaxed, rim_west, rim_east, slabs, tiles, x, t, walls, chosen=tuple(range(19))):
    lane, sub = lane_iota(), sub_iota()

    def rows(i, plane, low):
        if plane < 0:
            return rim_west[going_east.index(i), low : low + SUB, :]
        if plane >= slabs:
            return rim_east[going_west.index(i), low : low + SUB, :]
        return relaxed[i, plane, low : low + SUB, :]

    low = SUB + SUB * t if t < tiles else 0
    high = SUB + SUB * tiles
    result = {}
    for i in chosen:
        ex, ey, ez = (int(v) for v in velocities[i])
        plane = x - ex
        if t < tiles or ey == 0:
            source = rows(i, plane, low - ey)
        elif ey == 1:
            source = jnp.where(
                sub >= 4, pltpu.roll(rows(i, plane, 0), 1, 0), rows(i, plane, high - 1)
            )
        else:
            source = jnp.where(
                sub >= 4, rows(i, plane, 1), pltpu.roll(rows(i, plane, high), SUB - 1, 0)
            )
        outside = None
        if ez == 1:
            source = pltpu.roll(source, 1, 1)
            outside = lane == 0
        elif ez == -1:
            source = pltpu.roll(source, LANES - 1, 1)
            outside = lane == LANES - 1
        wall = None
        if t == 0 and ey == 1:
            wall = (sub == 0) & walls[0]
        if t == tiles - 1 and ey == -1:
            wall = (sub == SUB - 1) & walls[1]
        if wall is not None:
            outside = wall if outside is None else outside | wall
        if outside is not None:
            source = jnp.where(outside, rows(opposite[i], x, low), source)
        result[i] = source
    return result


def wall_flags():
    strip = lax.axis_index("gy")
    return strip == 0, strip == lax.axis_size("gy") - 1


def place_kernel(
    capacity, got, placed, items, codes, arrived, listing, spare, crowd, sem
):
    sources = got.shape[0]
    nowhere = SUB * LANES
    lane, sub = lane_iota(), sub_iota()
    arrived[pl.ds(sources * 16, 16), :] = jnp.zeros((16, LANES), jnp.float32)
    for s in range(sources):
        arrived[16 * s + SUB : 16 * s + 16, :] = got[s].astype(jnp.float32)[SUB:16, :]
    first_dup = CODE_LANE + capacity
    for n in range(sources // SUB):
        row = arrived[pl.ds(SUB * n * 16 + 12, SUB, stride=16), :].astype(jnp.int32)
        column = arrived[pl.ds(SUB * n * 16 + 13, SUB, stride=16), :].astype(jnp.int32)
        code = row * LANES + column - 1
        source = sub + SUB * n
        is_dup = lane >= first_dup
        slot = jnp.where(is_dup, source * 8 + lane - first_dup, source * 4 + lane - CODE_LANE)
        item = jnp.where(code >= 0, slot * 8192 + code, -1)
        busy = jnp.where(is_dup & (lane < first_dup + 2 * capacity) & (code >= 0), 1.0, 0.0)
        busy = jnp.sum(busy, axis=1, keepdims=True)
        item = jnp.where(lane == LANES - 1, jnp.where(busy > 0.0, 1, 0), item)
        corner = pltpu.roll(jnp.maximum(code, nowhere), LANES - CODE_LANE, 1)
        items[SUB * n : SUB * n + SUB, :] = jnp.where(lane < capacity, corner, item)
    copy = pltpu.make_async_copy(items, codes, sem)
    copy.start()

    def gather(s, _):
        tile = got[s].astype(jnp.float32)
        upper, lower = tile[0:SUB, :], tile[SUB:16, :]
        own_lanes = lane < REST_LANE
        back = LANES - REST_LANE
        new_upper = jnp.where(own_lanes, upper + pltpu.roll(upper, back, 1), upper)
        new_lower = jnp.where(own_lanes, lower + pltpu.roll(lower, back, 1), lower)
        if 2 * capacity > WIDE_DUPS:
            here = (lane >= REST_LANE) & (lane < REST_LANE + GROUP)
            first_rows = pltpu.roll(lower, 4, 0)
            upper_dups = jnp.where(
                sub < 4,
                pltpu.roll(first_rows, REST_LANE, 1),
                pltpu.roll(lower, REST_LANE - GROUP, 1),
            )
            lower_dups = pltpu.roll(first_rows, REST_LANE - 2 * GROUP, 1)
            new_upper = jnp.where(here, upper_dups, new_upper)
            new_lower = jnp.where(here & (sub < 4), lower_dups, new_lower)
        at = pl.multiple_of(s * 16, 16)
        arrived[pl.ds(at, SUB), :] = new_upper
        arrived[pl.ds(at + SUB, SUB), :] = new_lower
        return 0

    lax.fori_loop(0, sources, gather, 0, unroll=8)
    placed[...] = jnp.zeros_like(placed)
    copy.wait()

    def note(s, carry):
        own, some = carry
        for r in range(capacity):
            item = codes[s, CODE_LANE + r]
            listing[own >> 7, own & 127] = item
            own = own + 1 + (item >> 31)
        crowd[some] = s
        return own, some + codes[s, LANES - 1]

    own_count, some = lax.fori_loop(0, sources, note, (jnp.int32(0), jnp.int32(0)), unroll=8)

    def note_dup(n, dup):
        s = crowd[n]
        for r in range(2 * capacity):
            item = codes[s, first_dup + r]
            spare[dup] = item
            dup = dup + 1 + (item >> 31)
        return dup

    dup_count = lax.fori_loop(0, some, note_dup, jnp.int32(0))
    for j in range(STEP - 1):
        at = own_count + j
        listing[at >> 7, at & 127] = sources * 4 * 8192 + nowhere
    for j in range(DUP_STEP - 1):
        spare[dup_count + j] = sources * 8 * 8192 + nowhere

    def moved_rows(source, z, lanes_at, steps):
        inside = (lane >= z) & (lane < z + STEN)
        rows = {}
        for h in range(2):
            tile = arrived[pl.ds(pl.multiple_of(source * 16, 16) + SUB * h, SUB), :]
            for b in range(steps):
                shift = (z - lanes_at - STEN * b + 2 * LANES) & (LANES - 1)
                rows[b, h] = jnp.where(inside, pltpu.roll(tile, shift, 1), 0.0)
        return rows

    def add_rows(rows, y):
        at = {
            (b, h): pl.ds(pl.multiple_of((y + b) * 16 + SUB * h, SUB), SUB) for b, h in rows
        }
        old = {key: placed[at[key], :] for key in rows}
        for key in rows:
            placed[at[key], :] = old[key] + rows[key]

    def place_own(n, _):
        todo = []
        for j in range(STEP):
            at = STEP * n + j
            item = listing[at >> 7, at & 127]
            slot, code = item >> 13, item & 8191
            todo.append(
                (moved_rows(slot >> 2, code & (LANES - 1), GROUP * (slot & 3), 4), code >> 7)
            )
        for rows, y in todo:
            add_rows(rows, y)
        return 0

    lax.fori_loop(0, (own_count + STEP - 1) // STEP, place_own, 0)

    def place_dup(n, _):
        todo = []
        for j in range(DUP_STEP):
            item = spare[DUP_STEP * n + j]
            slot, code = item >> 13, item & 8191
            q = slot & 7
            low = jnp.where(q < capacity, 2, 0)
            at = 8 * q + jnp.where(q < WIDE_DUPS, DUP_LANE, REST_LANE - 8 * WIDE_DUPS)
            rows = moved_rows(slot >> 3, code & (LANES - 1), at, 2)
            todo.append((rows, (code >> 7) + low))
        for rows, y in todo:
            add_rows(rows, y)
        return 0

    lax.fori_loop(0, (dup_count + DUP_STEP - 1) // DUP_STEP, place_dup, 0)


def first_kernel(placed, populations, rim_a, rim_b, relaxed, face_a, face_b, forcing, rim):
    slabs, strip_cells = populations.shape[1], populations.shape[2]
    tiles = strip_cells // SUB
    sub = sub_iota()
    even = lax.rem(lax.axis_index("gy"), 2) == 0
    rim[...] = jnp.zeros_like(rim)
    for toward in (1, -1):
        _, near, far, _ = fold_tables(toward)
        for n, i in enumerate(near + far):
            a, b = rim_a[n], rim_b[n]
            value = jnp.where(even, b, a) if toward == 1 else jnp.where(even, a, b)
            if toward == 1:
                at = 7 if n < len(near) else 6
            else:
                at = 0 if n < len(near) else 1
            rim[i, :, at, :] = value
    for x in range(slabs):
        for t in range(tiles + 1):
            push = []
            for k in range(3):
                if t < tiles:
                    value = placed[pl.ds((SUB + SUB * t) * 16 + 4 * k + x, SUB, stride=16), :]
                else:
                    value = jnp.where(
                        sub >= 4,
                        placed[pl.ds(4 * k + x, SUB, stride=16), :],
                        placed[pl.ds((SUB + SUB * tiles) * 16 + 4 * k + x, SUB, stride=16), :],
                    )
                forcing[k, x, SUB * t : SUB * t + SUB, :] = value
                push.append(value)
            if t < tiles:
                fields = [populations[i, x, SUB * t : SUB * t + SUB, :] for i in range(19)]
            else:
                fields = [rim[i, x] for i in range(19)]
            keep_tile(relaxed, tiles, x, t, collided(fields, push))
    write_faces(relaxed, forcing, slabs, tiles, wall_flags(), face_a, face_b)


def second_kernel(
    capacity,
    items,
    before,
    got_a,
    got_b,
    forcing,
    populations_far,
    speeds,
    corners,
    populations,
    relaxed,
    rim_west,
    rim_east,
    after_west,
    after_east,
    fluid,
    sems,
):
    slabs = before.shape[1]
    corner_copy = pltpu.make_async_copy(items, corners, sems.at[slabs])
    corner_copy.start()
    tiles = before.shape[2] // SUB - 2
    unpack_faces(got_a, got_b, tiles, rim_west, rim_east)
    walls = wall_flags()
    rims = (rim_west, rim_east)
    relax_rim(
        before, rims, slabs, tiles, walls, got_a, got_b, going_east, going_west, -1, True, after_west
    )
    relax_rim(
        before,
        rims,
        slabs,
        tiles,
        walls,
        got_a,
        got_b,
        going_west,
        going_east,
        slabs,
        False,
        after_east,
    )
    for x in range(slabs):
        for t in range(tiles + 1):
            fields = streamed(before, rim_west, rim_east, slabs, tiles, x, t, walls)
            push = [forcing[k, x, SUB * t : SUB * t + SUB, :] for k in range(3)]
            keep_tile(relaxed, tiles, x, t, collided(fields, push))
    copies = []
    for x in range(slabs):
        for t in range(tiles):
            fields = streamed(relaxed, after_west, after_east, slabs, tiles, x, t, walls)
            density = fields[0]
            for i in range(1, 19):
                density = density + fields[i]
            inverse = 1.0 / density
            for i in range(19):
                populations[i, x, SUB * t : SUB * t + SUB, :] = fields[i]
            for k in range(3):
                total = 0.5 * forcing[k, x, SUB * t : SUB * t + SUB, :]
                for i in range(19):
                    if velocities[i, k] == 1:
                        total = total + fields[i]
                    elif velocities[i, k] == -1:
                        total = total - fields[i]
                speed = total * inverse
                for b in range(4):
                    moved = speed if b == 0 else pltpu.roll(speed, STEN * b, 1)
                    fluid[b, pl.ds(SUB * t * 16 + 4 * k + x, SUB, stride=16), :] = moved
        copies.append(
            pltpu.make_async_copy(populations.at[:, x], populations_far.at[:, x], sems.at[x])
        )
        copies[x].start()
    lane = lane_iota()
    corner_copy.wait()

    def pick(s, _):
        corner = [corners[s, r] for r in range(capacity)]
        tile = jnp.zeros((SUB, LANES), jnp.float32)
        for r in range(capacity):
            y, z = (corner[r] >> 7) - SUB, corner[r] & (LANES - 1)
            beyond = (lane - z) & (LANES - 1)
            for h in range(2):
                rows = [
                    fluid[b, pl.ds(pl.multiple_of((y + b) * 16 + SUB * h, SUB), SUB), :]
                    for b in range(4)
                ]
                low = GROUP * (h * capacity + r)
                cube = jnp.where(beyond < 2 * STEN, rows[1], jnp.where(beyond < 3 * STEN, rows[2], rows[3]))
                cube = jnp.where(beyond < STEN, rows[0], cube)
                moved = pltpu.roll(cube, (low - z + LANES) & (LANES - 1), 1)
                tile = jnp.where((lane >= low) & (lane < low + GROUP), moved, tile)
        speeds[s] = tile.astype(jnp.bfloat16)
        return 0

    lax.fori_loop(0, speeds.shape[0], pick, 0, unroll=8)
    for copy in copies:
        copy.wait()


def marker_kernel(
    capacity, owner, swimmer, returned, weights, velocity, total, chosen, expanded, count
):
    held = weights.shape[0]
    cells = weights.shape[1]
    targets = returned.shape[0]
    lane, sub = lane_iota(16), sub_iota(16)
    sub8, lane8 = sub_iota(), lane_iota()

    def reset(i, _):
        count[i] = 0
        return 0

    lax.fori_loop(0, targets, reset, 0, unroll=16)
    for b in range(held):
        target = owner[0, b]
        rank = count[target]
        count[target] = rank + 1
        low = GROUP * rank
        tile = returned[target].astype(jnp.float32)
        first = jnp.where((lane8 >= low) & (lane8 < low + GROUP), tile, 0.0)
        low = low + GROUP * capacity
        second = jnp.where((lane8 >= low) & (lane8 < low + GROUP), tile, 0.0)
        chosen[16 * b : 16 * b + 16, :] = jnp.concatenate([first, second], axis=0).astype(
            jnp.bfloat16
        )
    across = lax.broadcasted_iota(jnp.int32, (LANES, LANES), 1)
    down = lax.broadcasted_iota(jnp.int32, (LANES, LANES), 0)
    repeat = jnp.where(across % GROUP == down % GROUP, 1.0, 0.0).astype(jnp.bfloat16)
    own_cells = (lane // GROUP) % 4 == sub % 4
    for g in range(held // SUB):
        wide = jnp.dot(
            chosen[LANES * g : LANES * g + LANES, :], repeat, preferred_element_type=jnp.float32
        )
        for j in range(SUB):
            expanded[LANES * g + 16 * j : LANES * g + 16 * j + 16, :] = jnp.where(
                own_cells, wide[16 * j : 16 * j + 16, :], 0.0
            )
    sums = {}
    for g in range(held // SUB):
        pieces = []
        for k in range(3):
            row = None
            for x in range(4):
                part = expanded[pl.ds(LANES * g + 4 * k + x, SUB, stride=16), :]
                row = part if row is None else row + part
            pieces.append(
                jnp.concatenate(
                    [
                        jnp.where(sub8 == 2 * pair + lane8 // 64, row, 0.0).astype(jnp.bfloat16)
                        for pair in range(4)
                    ],
                    axis=1,
                )
            )
        left = jnp.concatenate(pieces, axis=0)
        right = weights[SUB * g : SUB * g + SUB].reshape(SUB * cells, LANES)
        out = speed_scale * jnp.dot(left, right, preferred_element_type=jnp.float32)
        member = jnp.zeros((SUB, LANES), jnp.int32)
        for j in range(SUB):
            member = jnp.where(sub8 == j, lax.rem(swimmer[SUB * g + j], SWIM_DEV), member)
        for k in range(3):
            part = out[SUB * k : SUB * k + SUB, :]
            velocity[k, SUB * g : SUB * g + SUB, :] = part
            for s in range(SWIM_DEV):
                term = jnp.where(member == s, part, 0.0)
                sums[k, s] = term if g == 0 else sums[k, s] + term
    table = jnp.zeros((SUB, LANES), jnp.float32)
    for (k, s), value in sums.items():
        mean = jnp.sum(value) * (1.0 / LANES)
        table = jnp.where((sub8 == k) & (lane8 == s), mean, table)
    total[...] = table[0:3, 0:SWIM_DEV]


VM = pl.BlockSpec(memory_space=pltpu.VMEM)
SM = pl.BlockSpec(memory_space=pltpu.SMEM)
FAR = pl.BlockSpec(memory_space=pltpu.HBM)


def shaped(shape, dtype=jnp.float32):
    return jax.ShapeDtypeStruct(shape, dtype)


def step(populations, marker_weights, marker_force, owner_device, stencil_base, block_swimmer):
    slab_cells, strip_cells, height = populations.shape[1:]
    strips = lax.axis_size("gy")
    devices = lax.axis_size("gx") * strips
    held = marker_weights.shape[0]
    capacity = max(2, (2 * held + devices - 1) // devices)
    padded_rows = strip_cells + 2 * SUB
    packed_rows = strip_cells + SUB
    f32 = jnp.float32
    small = pltpu.CompilerParams(vmem_limit_bytes=12 * 1024 * 1024)

    owner = owner_device.T
    force = marker_force.transpose(1, 0, 2)
    edge = shaped((27, slab_cells, height))
    edge_rows = pltpu.VMEM((19, slab_cells, SUB, height), f32)
    sent, rim_a, rim_b = pl.pallas_call(
        functools.partial(patch_kernel, capacity, strips),
        out_shape=(shaped((devices, 16, LANES), jnp.bfloat16), edge, edge),
        in_specs=[FAR] * 5,
        out_specs=(VM, VM, VM),
        scratch_shapes=[
            pltpu.SMEM(owner.shape, jnp.int32),
            pltpu.SMEM((3, held), jnp.int32),
            pltpu.VMEM(marker_weights.shape, jnp.bfloat16),
            pltpu.VMEM(force.shape, jnp.bfloat16),
            edge_rows,
            edge_rows,
            pltpu.VMEM((3, held, LANES), f32),
            pltpu.VMEM((held * 16, LANES), f32),
            pltpu.VMEM((held, 16, LANES), f32),
            pltpu.VMEM((devices + 1, 16, LANES), f32),
            pltpu.SMEM((devices,), jnp.int32),
            pltpu.SMEM((held,), jnp.int32),
            pltpu.SMEM((held + DUP_STEP,), jnp.int32),
            pltpu.SemaphoreType.DMA((9,)),
        ],
        name="patches",
    )(owner, stencil_base.T, marker_weights, force, populations)
    got = lax.all_to_all(sent, ("gx", "gy"), split_axis=0, concat_axis=0, tiled=True)
    rim_a, rim_b = swapped(rim_a, rim_b, "gy", False)
    planes = shaped((19, slab_cells, padded_rows, height))
    face = shaped((FACE_FIELDS * strip_cells + 4 * SUB, height))
    push = shaped((3, slab_cells, packed_rows, height))
    rims = [pltpu.VMEM((5, padded_rows, height), f32)] * 4
    placed, items = pl.pallas_call(
        functools.partial(place_kernel, capacity),
        out_shape=(shaped((padded_rows * 16, LANES)), shaped((devices, LANES), jnp.int32)),
        in_specs=[VM],
        out_specs=(VM, VM),
        scratch_shapes=[
            pltpu.SMEM((devices, LANES), jnp.int32),
            pltpu.VMEM(((devices + 1) * 16, LANES), f32),
            pltpu.SMEM((SUB, LANES), jnp.int32),
            pltpu.SMEM((devices * 2 * capacity + DUP_STEP,), jnp.int32),
            pltpu.SMEM((devices + 1,), jnp.int32),
            pltpu.SemaphoreType.DMA,
        ],
        compiler_params=small,
        name="place",
    )(got)
    relaxed, face_a, face_b, forcing = pl.pallas_call(
        first_kernel,
        out_shape=(planes, face, face, push),
        in_specs=[VM] * 4,
        out_specs=(VM, VM, VM, VM),
        scratch_shapes=[pltpu.VMEM((19, slab_cells, SUB, LANES), f32)],
        compiler_params=small,
        name="first",
    )(placed, populations, rim_a, rim_b)
    got_a, got_b = swapped(face_a, face_b, "gx", True)
    fields, speeds = pl.pallas_call(
        functools.partial(second_kernel, capacity),
        out_shape=(shaped(populations.shape), shaped((devices, SUB, LANES), jnp.bfloat16)),
        in_specs=[VM, VM, VM, VM, VM],
        out_specs=(FAR, VM),
        scratch_shapes=[
            pltpu.SMEM((devices, LANES), jnp.int32),
            pltpu.VMEM(populations.shape, f32),
            pltpu.VMEM(planes.shape, f32),
        ]
        + rims
        + [
            pltpu.VMEM((4, strip_cells * 16, LANES), f32),
            pltpu.SemaphoreType.DMA((slab_cells + 1,)),
        ],
        compiler_params=small,
        name="second",
    )(items, relaxed, got_a, got_b, forcing)
    returned = lax.all_to_all(speeds, ("gx", "gy"), split_axis=0, concat_axis=0, tiled=True)
    marker_velocity, swimmer_velocity = pl.pallas_call(
        functools.partial(marker_kernel, capacity),
        out_shape=(shaped((3, held, LANES)), shaped((3, SWIM_DEV))),
        in_specs=[SM, SM, VM, VM],
        out_specs=(VM, VM),
        scratch_shapes=[
            pltpu.VMEM((held * 16, LANES), jnp.bfloat16),
            pltpu.VMEM((held * 16, LANES), f32),
            pltpu.SMEM((devices,), jnp.int32),
        ],
        compiler_params=small,
        name="markers",
    )(owner, block_swimmer, returned, marker_weights)
    return fields, marker_velocity.transpose(1, 0, 2), swimmer_velocity


def solution(mesh):
    in_specs = (
        P(None, "gx", "gy", None),
        P(("gx", "gy"), None, None),
        P(("gx", "gy"), None, None),
        P(("gx", "gy"), None),
        P(("gx", "gy"), None),
        P(("gx", "gy")),
    )
    out_specs = (P(None, "gx", "gy", None), P(("gx", "gy"), None, None), P(None, ("gx", "gy")))
    return jax.shard_map(step, mesh=mesh, in_specs=in_specs, out_specs=out_specs, check_vma=False)
```

```python
import functools

import jax
import jax.numpy as jnp
import numpy as np
from jax import lax
from jax.experimental import pallas as pl
from jax.experimental.pallas import tpu as pltpu
from jax.sharding import PartitionSpec as P


STEN = 4
SWIM_DEV = 4
LANES = 128
SUB = 8
GROUP = STEN * STEN
CODE_LANE = 64
REST_LANE = 48
DUP_LANE = 96
WIDE_DUPS = 4
STEP = 8
DUP_STEP = 4

velocities = np.array(
    [
        [0, 0, 0],
        [1, 0, 0],
        [-1, 0, 0],
        [0, 1, 0],
        [0, -1, 0],
        [0, 0, 1],
        [0, 0, -1],
        [1, 1, 0],
        [-1, -1, 0],
        [1, -1, 0],
        [-1, 1, 0],
        [1, 0, 1],
        [-1, 0, -1],
        [1, 0, -1],
        [-1, 0, 1],
        [0, 1, 1],
        [0, -1, -1],
        [0, 1, -1],
        [0, -1, 1],
    ]
)
opposite = [0, 2, 1, 4, 3, 6, 5, 8, 7, 10, 9, 12, 11, 14, 13, 16, 15, 18, 17]
lattice_weights = [1.0 / 3.0] + [1.0 / 18.0] * 6 + [1.0 / 36.0] * 12
relax_time = 0.8
speed_scale = 20.0
going_east = [1, 7, 9, 11, 13]
going_west = [2, 10, 8, 12, 14]
staying = [0, 3, 4, 5, 6, 15, 16, 17, 18]
FACE_FIELDS = 14


def lane_iota(rows=SUB):
    return lax.broadcasted_iota(jnp.int32, (rows, LANES), 1)


def sub_iota(rows=SUB):
    return lax.broadcasted_iota(jnp.int32, (rows, LANES), 0)


def swapped(first, second, axis, periodic):
    size = lax.axis_size(axis)
    inner = [(i, i ^ 1) for i in range(size)]
    outer = []
    for i in range(size):
        j = i + 1 if i % 2 == 1 else i - 1
        if periodic:
            outer.append((i, j % size))
        elif 0 <= j < size:
            outer.append((i, j))
    second = lax.ppermute(second, axis, outer)
    first = lax.ppermute(first, axis, inner)
    return first, second


def patch_kernel(
    capacity,
    strips,
    owner_far,
    base_far,
    weights_far,
    force_far,
    populations,
    send,
    rim_a,
    rim_b,
    owner,
    base,
    weights,
    force,
    bottom,
    top,
    rows,
    spread,
    patches,
    record,
    count,
    place,
    again,
    sems,
):
    held = weights.shape[0]
    cells = weights.shape[1]
    strip_cells = populations.shape[2]
    pieces = sems.shape[0] - 5
    part_blocks = held // pieces
    force_copy = pltpu.make_async_copy(force_far, force, sems.at[pieces])
    force_copy.start()
    copies = [
        pltpu.make_async_copy(
            weights_far.at[part_blocks * n : part_blocks * (n + 1)],
            weights.at[part_blocks * n : part_blocks * (n + 1)],
            sems.at[n],
        )
        for n in range(pieces)
    ]
    copies.append(pltpu.make_async_copy(owner_far, owner, sems.at[pieces + 1]))
    copies.append(pltpu.make_async_copy(base_far, base, sems.at[pieces + 2]))
    edge_copies = [
        pltpu.make_async_copy(populations.at[:, :, 0:SUB, :], bottom, sems.at[pieces + 3]),
        pltpu.make_async_copy(
            populations.at[:, :, strip_cells - SUB : strip_cells, :], top, sems.at[pieces + 4]
        ),
    ]
    for copy in copies + edge_copies:
        copy.start()
    targets = send.shape[0]
    lane, sub = lane_iota(16), sub_iota(16)

    def clear(i, _):
        record[i] = jnp.zeros((16, LANES), jnp.float32)
        return 0

    lax.fori_loop(0, targets, clear, 0, unroll=16)

    def reset(i, _):
        count[i] = 0
        return 0

    lax.fori_loop(0, targets, reset, 0, unroll=16)
    extra = jnp.int32(0)
    powers = strips & (strips - 1) == 0
    force_copy.wait()
    for k in range(3):
        rows[k] = force[k].astype(jnp.float32)
    for b in range(held):
        for k in range(3):
            spread[16 * b + 4 * k : 16 * b + 4 * k + 4, :] = jnp.broadcast_to(
                rows[k, b : b + 1, :], (4, LANES)
            )
        spread[16 * b + 12 : 16 * b + 16, :] = jnp.zeros((4, LANES), jnp.float32)
    for g in range(held // 4):
        if g == 0:
            for copy in copies[pieces:]:
                copy.wait()
        if 4 * g % part_blocks == 0:
            copies[4 * g // part_blocks].wait()
        for b in range(4 * g, 4 * g + 4):
            target = owner[0, b]
            rank = count[target]
            count[target] = rank + 1
            place[b] = target * 4 + rank
            strip = target & (strips - 1) if powers else lax.rem(target, strips)
            y = base[1, b]
            north = (y >= strip_cells - 5) & (strip < strips - 1)
            south = (y <= 1) & (strip > 0)
            again[extra] = b * 4 + rank
            extra = extra + jnp.where(north | south, 1, 0)
        out = lax.dot_general(
            spread[64 * g : 64 * g + 64, :].astype(jnp.bfloat16),
            weights[4 * g : 4 * g + 4].reshape(4 * cells, LANES),
            (((1,), (1,)), ((), ())),
            preferred_element_type=jnp.float32,
        )
        for j in range(4):
            half = j // 2
            part = out[16 * j : 16 * j + 16, LANES * half : LANES * half + LANES]
            part = jnp.where(lane // GROUP == 4 * (j % 2) + sub % 4, part, 0.0)
            part = part + pltpu.roll(part, 64, 1)
            part = part + pltpu.roll(part, 32, 1)
            part = part + pltpu.roll(part, 16, 1)
            patches[g * 4 + j] = part

    def labelled(tile, slot, frame_y, z):
        label = jnp.where(sub == 12, frame_y + SUB, z + 1).astype(jnp.float32)
        return jnp.where((lane == CODE_LANE + slot) & ((sub == 12) | (sub == 13)), label, tile)

    for b in range(held):
        target, rank = place[b] >> 2, place[b] & 3
        low = GROUP * rank
        inside = (lane >= low) & (lane < low + GROUP) & (sub < 12)
        tile = jnp.where(inside, patches[b], record[target])
        record[target] = labelled(tile, rank, base[1, b], base[2, b])

    for j in range(DUP_STEP - 1):
        again[extra + j] = -1

    def put_again(n, _):
        todo = []
        for j in range(DUP_STEP):
            item = again[DUP_STEP * n + j]
            none = item < 0
            b, rank = jnp.where(none, 0, item >> 2), item & 3
            y, z = base[1, b], base[2, b]
            to_south = y <= 1
            target = jnp.where(none, targets, owner[0, b] + jnp.where(to_south, -1, 1))
            half = jnp.where(to_south, 0, 1)
            q = rank + jnp.where(to_south, capacity, 0)
            moved = pltpu.roll(patches[b], 8 * ((q + half) & 1), 1)
            frame_y = y + jnp.where(to_south, strip_cells, -strip_cells)
            todo.append((target, q, moved, frame_y, z))
        for target, q, moved, frame_y, z in todo:
            wide = q < WIDE_DUPS
            low = jnp.where(wide, DUP_LANE + 8 * q, 2 * LANES)
            tile = jnp.where((lane >= low) & (lane < low + 8) & (sub < 12), moved, record[target])
            tile = labelled(tile, capacity + q, frame_y, z)
            if 2 * capacity > WIDE_DUPS:
                last = tile[12:16, :]
                lane4 = lane_iota(4)
                for k in range(3):
                    low = jnp.where(wide, 2 * LANES, GROUP * k + 8 * (q - WIDE_DUPS))
                    last = jnp.where(
                        (lane4 >= low) & (lane4 < low + 8), moved[4 * k : 4 * k + 4, :], last
                    )
                tile = jnp.concatenate([tile[0:12, :], last], axis=0)
            record[target] = tile
        return 0

    lax.fori_loop(0, (extra + DUP_STEP - 1) // DUP_STEP, put_again, 0)
    for copy in edge_copies:
        copy.wait()
    write_rims(bottom, top, rim_a, rim_b)
    rest_lanes = (lane >= REST_LANE) & (lane < 2 * REST_LANE) & (sub < 12)

    def finish(i, _):
        tile = record[i]
        rest = tile - tile.astype(jnp.bfloat16).astype(jnp.float32)
        tile = jnp.where(rest_lanes, pltpu.roll(rest, REST_LANE, 1), tile)
        send[i] = tile.astype(jnp.bfloat16)
        return 0

    lax.fori_loop(0, targets, finish, 0, unroll=8)


def fold_tables(toward):
    ahead = [i for i in range(19) if velocities[i, 1] == toward]
    plain = 4 if toward == 1 else 3
    to_east, to_west = (9, 8) if toward == 1 else (7, 10)
    near = [i for i in range(19) if i != to_west]
    far = ahead + [0, 1, 5, plain]
    return ahead, near, far, (plain, to_east, to_west)


def rim_message(near_row, far_row, toward):
    ahead, near, far, (plain, to_east, to_west) = fold_tables(toward)
    folded = {i: near_row[i] for i in near}
    folded[plain] = near_row[plain] + 2.0 * near_row[to_west]
    folded[to_east] = near_row[to_east] - near_row[to_west]
    message = [folded[i] for i in near]
    others = [i for i in range(19) if i not in ahead]
    total = [None, None, None]
    mass = None
    for i in others:
        mass = far_row[i] if mass is None else mass + far_row[i]
        for k in (0, 2):
            if velocities[i, k] != 0:
                term = far_row[i] if velocities[i, k] == 1 else -far_row[i]
                total[k] = term if total[k] is None else total[k] + term
        if velocities[i, 1] == -toward:
            total[1] = far_row[i] if total[1] is None else total[1] + far_row[i]
    rest = {0: mass - total[0] - total[1] - total[2], 1: total[0], 5: total[2], plain: total[1]}
    return message + [rest[i] if i in rest else far_row[i] for i in far]


def write_rims(bottom, top, rim_a, rim_b):
    even = lax.rem(lax.axis_index("gy"), 2) == 0

    def row(edge, n):
        return [edge[i, :, n, :] for i in range(19)]

    up = rim_message(row(top, SUB - 1), row(top, SUB - 2), 1)
    down = rim_message(row(bottom, 0), row(bottom, 1), -1)
    for n in range(len(up)):
        rim_a[n] = jnp.where(even, up[n], down[n])
        rim_b[n] = jnp.where(even, down[n], up[n])


def collided(fields, forcing):
    pair_sum, pair_diff = {}, {}
    for i in range(1, 19, 2):
        pair_sum[i] = fields[i] + fields[i + 1]
        pair_diff[i] = fields[i] - fields[i + 1]
    density = fields[0]
    for i in range(1, 19, 2):
        density = density + pair_sum[i]
    momentum = []
    for k in range(3):
        total = relax_time * forcing[k]
        for i in range(1, 19, 2):
            if velocities[i, k] == 1:
                total = total + pair_diff[i]
            elif velocities[i, k] == -1:
                total = total - pair_diff[i]
        momentum.append(total)
    inverse = 1.0 / density
    keep = 1.0 - 1.0 / relax_time
    squares = momentum[0] * momentum[0] + momentum[1] * momentum[1] + momentum[2] * momentum[2]
    level = density - 1.5 * inverse * squares
    curve = 4.5 * inverse
    result = [None] * 19
    result[0] = keep * fields[0] + (lattice_weights[0] / relax_time) * level
    for i in range(1, 19, 2):
        along = None
        for k in range(3):
            if velocities[i, k] == 1:
                along = momentum[k] if along is None else along + momentum[k]
            elif velocities[i, k] == -1:
                along = -momentum[k] if along is None else along - momentum[k]
        share = lattice_weights[i] / relax_time
        even = share * (level + curve * along * along)
        odd = (3.0 * share) * along
        result[i] = keep * fields[i] + (even + odd)
        result[i + 1] = keep * fields[i + 1] + (even - odd)
    return result


def keep_tile(relaxed, tiles, x, t, values):
    for i in range(19):
        if t < tiles:
            relaxed[i, x, SUB + SUB * t : 2 * SUB + SUB * t, :] = values[i]
        else:
            relaxed[i, x, 0:SUB, :] = values[i]
            relaxed[i, x, SUB + SUB * tiles : 2 * SUB + SUB * tiles, :] = values[i]


def write_faces(relaxed, forcing, slabs, tiles, walls, face_a, face_b):
    even = lax.rem(lax.axis_index("gx"), 2) == 0
    for t in range(tiles + 1):
        low = SUB + SUB * t
        sides = []
        for going, plane in ((going_east, slabs - 1), (going_west, 0)):
            fields = streamed(relaxed, None, None, slabs, tiles, plane, t, walls, going + staying)
            mass = None
            for value in fields.values():
                mass = value if mass is None else mass + value
            message = [relaxed[i, plane, low : low + SUB, :] for i in going]
            message += [fields[i] for i in going] + [mass]
            for k in range(3):
                total = relax_time * forcing[k, plane, SUB * t : SUB * t + SUB, :]
                message.append(with_signs(total, fields, k))
            sides.append(message)
        for n in range(FACE_FIELDS):
            east, west = sides[0][n], sides[1][n]
            a, b = jnp.where(even, east, west), jnp.where(even, west, east)
            if t < tiles:
                at = SUB * (tiles * n + t)
                face_a[at : at + SUB, :] = a
                face_b[at : at + SUB, :] = b
            else:
                at = SUB * tiles * FACE_FIELDS + 2 * n
                for j, row in enumerate(rim_sublanes(n)):
                    face_a[at + j : at + j + 1, :] = a[row : row + 1, :]
                    face_b[at + j : at + j + 1, :] = b[row : row + 1, :]


def rim_sublanes(n):
    along = int(velocities[going_east[n], 1]) if n < 5 else 0
    return {0: (7, 0), 1: (6, 7), -1: (0, 1)}[along]


def with_signs(total, fields, k):
    for i, value in fields.items():
        if velocities[i, k] == 1:
            total = total + value
        elif velocities[i, k] == -1:
            total = total - value
    return total


def unpack_faces(face_a, face_b, tiles, rim_west, rim_east):
    even = lax.rem(lax.axis_index("gx"), 2) == 0
    for n in range(5):
        for t in range(tiles):
            at = SUB * (tiles * n + t)
            a, b = face_a[at : at + SUB, :], face_b[at : at + SUB, :]
            keep_rim(rim_west, n, tiles, t, jnp.where(even, b, a))
            keep_rim(rim_east, n, tiles, t, jnp.where(even, a, b))
        at = SUB * tiles * FACE_FIELDS + 2 * n
        for j, row in enumerate(rim_sublanes(n)):
            a, b = face_a[at + j : at + j + 1, :], face_b[at + j : at + j + 1, :]
            places = [row] if row >= 4 else [row, SUB + SUB * tiles + row]
            for place in places:
                rim_west[n, place : place + 1, :] = jnp.where(even, b, a)
                rim_east[n, place : place + 1, :] = jnp.where(even, a, b)


def keep_rim(rim, n, tiles, t, value):
    low = SUB + SUB * t
    rim[n, low : low + SUB, :] = value
    if t == tiles:
        rim[n, 0:SUB, :] = value


def relax_rim(
    relaxed, rims, slabs, tiles, walls, face_a, face_b, going, back, plane, is_west, after
):
    even = lax.rem(lax.axis_index("gx"), 2) == 0
    for t in range(tiles + 1):

        def got(n):
            at = SUB * (tiles * n + t) if t < tiles else SUB * tiles * FACE_FIELDS + 2 * n
            size = SUB if t < tiles else 1
            a, b = face_a[at : at + size, :], face_b[at : at + size, :]
            value = jnp.where(even, b, a) if is_west else jnp.where(even, a, b)
            if t < tiles:
                return value
            a, b = face_a[at + 1 : at + 2, :], face_b[at + 1 : at + 2, :]
            last = jnp.where(even, b, a) if is_west else jnp.where(even, a, b)
            return jnp.where(sub_iota() >= 4, value, last)

        fields = streamed(relaxed, rims[0], rims[1], slabs, tiles, plane, t, walls, back)
        density = got(10)
        for value in fields.values():
            density = density + value
        momentum = [with_signs(got(11 + k), fields, k) for k in range(3)]
        inward = {i: got(5 + n) for n, i in enumerate(going)}
        for n, value in enumerate(collided_some(inward, density, momentum).values()):
            keep_rim(after, n, tiles, t, value)


def collided_some(fields, density, momentum):
    inverse = 1.0 / density
    keep = 1.0 - 1.0 / relax_time
    squares = momentum[0] * momentum[0] + momentum[1] * momentum[1] + momentum[2] * momentum[2]
    level = density - 1.5 * inverse * squares
    curve = 4.5 * inverse
    result = {}
    for i, value in fields.items():
        along = jnp.zeros_like(density)
        for k in range(3):
            if velocities[i, k] == 1:
                along = along + momentum[k]
            elif velocities[i, k] == -1:
                along = along - momentum[k]
        share = lattice_weights[i] / relax_time
        result[i] = keep * value + (share * (level + curve * along * along) + (3.0 * share) * along)
    return result


def streamed(relaxed, rim_west, rim_east, slabs, tiles, x, t, walls, chosen=tuple(range(19))):
    lane, sub = lane_iota(), sub_iota()

    def rows(i, plane, low):
        if plane < 0:
            return rim_west[going_east.index(i), low : low + SUB, :]
        if plane >= slabs:
            return rim_east[going_west.index(i), low : low + SUB, :]
        return relaxed[i, plane, low : low + SUB, :]

    low = SUB + SUB * t if t < tiles else 0
    high = SUB + SUB * tiles
    result = {}
    for i in chosen:
        ex, ey, ez = (int(v) for v in velocities[i])
        plane = x - ex
        if t < tiles or ey == 0:
            source = rows(i, plane, low - ey)
        elif ey == 1:
            source = jnp.where(
                sub >= 4, pltpu.roll(rows(i, plane, 0), 1, 0), rows(i, plane, high - 1)
            )
        else:
            source = jnp.where(
                sub >= 4, rows(i, plane, 1), pltpu.roll(rows(i, plane, high), SUB - 1, 0)
            )
        outside = None
        if ez == 1:
            source = pltpu.roll(source, 1, 1)
            outside = lane == 0
        elif ez == -1:
            source = pltpu.roll(source, LANES - 1, 1)
            outside = lane == LANES - 1
        wall = None
        if t == 0 and ey == 1:
            wall = (sub == 0) & walls[0]
        if t == tiles - 1 and ey == -1:
            wall = (sub == SUB - 1) & walls[1]
        if wall is not None:
            outside = wall if outside is None else outside | wall
        if outside is not None:
            source = jnp.where(outside, rows(opposite[i], x, low), source)
        result[i] = source
    return result


def wall_flags():
    strip = lax.axis_index("gy")
    return strip == 0, strip == lax.axis_size("gy") - 1


def place_kernel(
    capacity, got, placed, items, codes, arrived, listing, spare, crowd, sem
):
    sources = got.shape[0]
    nowhere = SUB * LANES
    lane, sub = lane_iota(), sub_iota()
    arrived[pl.ds(sources * 16, 16), :] = jnp.zeros((16, LANES), jnp.float32)
    for s in range(sources):
        arrived[16 * s + SUB : 16 * s + 16, :] = got[s].astype(jnp.float32)[SUB:16, :]
    first_dup = CODE_LANE + capacity
    for n in range(sources // SUB):
        row = arrived[pl.ds(SUB * n * 16 + 12, SUB, stride=16), :].astype(jnp.int32)
        column = arrived[pl.ds(SUB * n * 16 + 13, SUB, stride=16), :].astype(jnp.int32)
        code = row * LANES + column - 1
        source = sub + SUB * n
        is_dup = lane >= first_dup
        slot = jnp.where(is_dup, source * 8 + lane - first_dup, source * 4 + lane - CODE_LANE)
        item = jnp.where(code >= 0, slot * 8192 + code, -1)
        busy = jnp.where(is_dup & (lane < first_dup + 2 * capacity) & (code >= 0), 1.0, 0.0)
        busy = jnp.sum(busy, axis=1, keepdims=True)
        item = jnp.where(lane == LANES - 1, jnp.where(busy > 0.0, 1, 0), item)
        corner = pltpu.roll(jnp.maximum(code, nowhere), LANES - CODE_LANE, 1)
        items[SUB * n : SUB * n + SUB, :] = jnp.where(lane < capacity, corner, item)
    copy = pltpu.make_async_copy(items, codes, sem)
    copy.start()

    def gather(s, _):
        tile = got[s].astype(jnp.float32)
        upper, lower = tile[0:SUB, :], tile[SUB:16, :]
        own_lanes = lane < REST_LANE
        back = LANES - REST_LANE
        new_upper = jnp.where(own_lanes, upper + pltpu.roll(upper, back, 1), upper)
        new_lower = jnp.where(own_lanes, lower + pltpu.roll(lower, back, 1), lower)
        if 2 * capacity > WIDE_DUPS:
            here = (lane >= REST_LANE) & (lane < REST_LANE + GROUP)
            first_rows = pltpu.roll(lower, 4, 0)
            upper_dups = jnp.where(
                sub < 4,
                pltpu.roll(first_rows, REST_LANE, 1),
                pltpu.roll(lower, REST_LANE - GROUP, 1),
            )
            lower_dups = pltpu.roll(first_rows, REST_LANE - 2 * GROUP, 1)
            new_upper = jnp.where(here, upper_dups, new_upper)
            new_lower = jnp.where(here & (sub < 4), lower_dups, new_lower)
        at = pl.multiple_of(s * 16, 16)
        arrived[pl.ds(at, SUB), :] = new_upper
        arrived[pl.ds(at + SUB, SUB), :] = new_lower
        return 0

    lax.fori_loop(0, sources, gather, 0, unroll=8)
    placed[...] = jnp.zeros_like(placed)
    copy.wait()

    def note(s, carry):
        own, some = carry
        for r in range(capacity):
            item = codes[s, CODE_LANE + r]
            listing[own >> 7, own & 127] = item
            own = own + 1 + (item >> 31)
        crowd[some] = s
        return own, some + codes[s, LANES - 1]

    own_count, some = lax.fori_loop(0, sources, note, (jnp.int32(0), jnp.int32(0)), unroll=8)

    def note_dup(n, dup):
        s = crowd[n]
        for r in range(2 * capacity):
            item = codes[s, first_dup + r]
            spare[dup] = item
            dup = dup + 1 + (item >> 31)
        return dup

    dup_count = lax.fori_loop(0, some, note_dup, jnp.int32(0))
    for j in range(STEP - 1):
        at = own_count + j
        listing[at >> 7, at & 127] = sources * 4 * 8192 + nowhere
    for j in range(DUP_STEP - 1):
        spare[dup_count + j] = sources * 8 * 8192 + nowhere

    def moved_rows(source, z, lanes_at, steps):
        inside = (lane >= z) & (lane < z + STEN)
        rows = {}
        for h in range(2):
            tile = arrived[pl.ds(pl.multiple_of(source * 16, 16) + SUB * h, SUB), :]
            for b in range(steps):
                shift = (z - lanes_at - STEN * b + 2 * LANES) & (LANES - 1)
                rows[b, h] = jnp.where(inside, pltpu.roll(tile, shift, 1), 0.0)
        return rows

    def add_rows(rows, y):
        at = {
            (b, h): pl.ds(pl.multiple_of((y + b) * 16 + SUB * h, SUB), SUB) for b, h in rows
        }
        old = {key: placed[at[key], :] for key in rows}
        for key in rows:
            placed[at[key], :] = old[key] + rows[key]

    def place_own(n, _):
        todo = []
        for j in range(STEP):
            at = STEP * n + j
            item = listing[at >> 7, at & 127]
            slot, code = item >> 13, item & 8191
            todo.append(
                (moved_rows(slot >> 2, code & (LANES - 1), GROUP * (slot & 3), 4), code >> 7)
            )
        for rows, y in todo:
            add_rows(rows, y)
        return 0

    lax.fori_loop(0, (own_count + STEP - 1) // STEP, place_own, 0)

    def place_dup(n, _):
        todo = []
        for j in range(DUP_STEP):
            item = spare[DUP_STEP * n + j]
            slot, code = item >> 13, item & 8191
            q = slot & 7
            low = jnp.where(q < capacity, 2, 0)
            at = 8 * q + jnp.where(q < WIDE_DUPS, DUP_LANE, REST_LANE - 8 * WIDE_DUPS)
            rows = moved_rows(slot >> 3, code & (LANES - 1), at, 2)
            todo.append((rows, (code >> 7) + low))
        for rows, y in todo:
            add_rows(rows, y)
        return 0

    lax.fori_loop(0, (dup_count + DUP_STEP - 1) // DUP_STEP, place_dup, 0)


def first_kernel(placed, populations, rim_a, rim_b, relaxed, face_a, face_b, forcing, rim):
    slabs, strip_cells = populations.shape[1], populations.shape[2]
    tiles = strip_cells // SUB
    sub = sub_iota()
    even = lax.rem(lax.axis_index("gy"), 2) == 0
    rim[...] = jnp.zeros_like(rim)
    for toward in (1, -1):
        _, near, far, _ = fold_tables(toward)
        for n, i in enumerate(near + far):
            a, b = rim_a[n], rim_b[n]
            value = jnp.where(even, b, a) if toward == 1 else jnp.where(even, a, b)
            if toward == 1:
                at = 7 if n < len(near) else 6
            else:
                at = 0 if n < len(near) else 1
            rim[i, :, at, :] = value
    for x in range(slabs):
        for t in range(tiles + 1):
            push = []
            for k in range(3):
                if t < tiles:
                    value = placed[pl.ds((SUB + SUB * t) * 16 + 4 * k + x, SUB, stride=16), :]
                else:
                    value = jnp.where(
                        sub >= 4,
                        placed[pl.ds(4 * k + x, SUB, stride=16), :],
                        placed[pl.ds((SUB + SUB * tiles) * 16 + 4 * k + x, SUB, stride=16), :],
                    )
                forcing[k, x, SUB * t : SUB * t + SUB, :] = value
                push.append(value)
            if t < tiles:
                fields = [populations[i, x, SUB * t : SUB * t + SUB, :] for i in range(19)]
            else:
                fields = [rim[i, x] for i in range(19)]
            keep_tile(relaxed, tiles, x, t, collided(fields, push))
    write_faces(relaxed, forcing, slabs, tiles, wall_flags(), face_a, face_b)


def second_kernel(
    capacity,
    items,
    before,
    got_a,
    got_b,
    forcing,
    populations_far,
    speeds,
    corners,
    populations,
    relaxed,
    rim_west,
    rim_east,
    after_west,
    after_east,
    fluid,
    sems,
):
    slabs = before.shape[1]
    corner_copy = pltpu.make_async_copy(items, corners, sems.at[slabs])
    corner_copy.start()
    tiles = before.shape[2] // SUB - 2
    unpack_faces(got_a, got_b, tiles, rim_west, rim_east)
    walls = wall_flags()
    rims = (rim_west, rim_east)

    def relax_side(is_west):
        relax_rim(
            before,
            rims,
            slabs,
            tiles,
            walls,
            got_a,
            got_b,
            going_east if is_west else going_west,
            going_west if is_west else going_east,
            -1 if is_west else slabs,
            is_west,
            after_west if is_west else after_east,
        )

    def relax_plane(x):
        for t in range(tiles + 1):
            fields = streamed(before, rim_west, rim_east, slabs, tiles, x, t, walls)
            push = [forcing[k, x, SUB * t : SUB * t + SUB, :] for k in range(3)]
            keep_tile(relaxed, tiles, x, t, collided(fields, push))

    relax_side(True)
    relax_plane(0)
    copies = []
    for x in range(slabs):
        if x + 1 < slabs:
            relax_plane(x + 1)
        else:
            relax_side(False)
        for t in range(tiles):
            fields = streamed(relaxed, after_west, after_east, slabs, tiles, x, t, walls)
            density = fields[0]
            for i in range(1, 19):
                density = density + fields[i]
            inverse = 1.0 / density
            for i in range(19):
                populations[i, x, SUB * t : SUB * t + SUB, :] = fields[i]
            for k in range(3):
                total = 0.5 * forcing[k, x, SUB * t : SUB * t + SUB, :]
                for i in range(19):
                    if velocities[i, k] == 1:
                        total = total + fields[i]
                    elif velocities[i, k] == -1:
                        total = total - fields[i]
                speed = total * inverse
                for b in range(4):
                    moved = speed if b == 0 else pltpu.roll(speed, STEN * b, 1)
                    fluid[b, pl.ds(SUB * t * 16 + 4 * k + x, SUB, stride=16), :] = moved
        copies.append(
            pltpu.make_async_copy(populations.at[:, x], populations_far.at[:, x], sems.at[x])
        )
        copies[x].start()
    lane = lane_iota()
    corner_copy.wait()

    def pick(s, _):
        corner = [corners[s, r] for r in range(capacity)]
        tile = jnp.zeros((SUB, LANES), jnp.float32)
        for r in range(capacity):
            y, z = (corner[r] >> 7) - SUB, corner[r] & (LANES - 1)
            beyond = (lane - z) & (LANES - 1)
            for h in range(2):
                rows = [
                    fluid[b, pl.ds(pl.multiple_of((y + b) * 16 + SUB * h, SUB), SUB), :]
                    for b in range(4)
                ]
                low = GROUP * (h * capacity + r)
                cube = jnp.where(beyond < 2 * STEN, rows[1], jnp.where(beyond < 3 * STEN, rows[2], rows[3]))
                cube = jnp.where(beyond < STEN, rows[0], cube)
                moved = pltpu.roll(cube, (low - z + LANES) & (LANES - 1), 1)
                tile = jnp.where((lane >= low) & (lane < low + GROUP), moved, tile)
        speeds[s] = tile.astype(jnp.bfloat16)
        return 0

    lax.fori_loop(0, speeds.shape[0], pick, 0, unroll=8)
    for copy in copies:
        copy.wait()


def marker_kernel(
    capacity, owner, swimmer, returned, weights, velocity, total, chosen, expanded, count
):
    held = weights.shape[0]
    cells = weights.shape[1]
    targets = returned.shape[0]
    lane, sub = lane_iota(16), sub_iota(16)
    sub8, lane8 = sub_iota(), lane_iota()

    def reset(i, _):
        count[i] = 0
        return 0

    lax.fori_loop(0, targets, reset, 0, unroll=16)
    for b in range(held):
        target = owner[0, b]
        rank = count[target]
        count[target] = rank + 1
        low = GROUP * rank
        tile = returned[target].astype(jnp.float32)
        first = jnp.where((lane8 >= low) & (lane8 < low + GROUP), tile, 0.0)
        low = low + GROUP * capacity
        second = jnp.where((lane8 >= low) & (lane8 < low + GROUP), tile, 0.0)
        chosen[16 * b : 16 * b + 16, :] = jnp.concatenate([first, second], axis=0).astype(
            jnp.bfloat16
        )
    across = lax.broadcasted_iota(jnp.int32, (LANES, LANES), 1)
    down = lax.broadcasted_iota(jnp.int32, (LANES, LANES), 0)
    repeat = jnp.where(across % GROUP == down % GROUP, 1.0, 0.0).astype(jnp.bfloat16)
    own_cells = (lane // GROUP) % 4 == sub % 4
    for g in range(held // SUB):
        wide = jnp.dot(
            chosen[LANES * g : LANES * g + LANES, :], repeat, preferred_element_type=jnp.float32
        )
        for j in range(SUB):
            expanded[LANES * g + 16 * j : LANES * g + 16 * j + 16, :] = jnp.where(
                own_cells, wide[16 * j : 16 * j + 16, :], 0.0
            )
    sums = {}
    for g in range(held // SUB):
        pieces = []
        for k in range(3):
            row = None
            for x in range(4):
                part = expanded[pl.ds(LANES * g + 4 * k + x, SUB, stride=16), :]
                row = part if row is None else row + part
            pieces.append(
                jnp.concatenate(
                    [
                        jnp.where(sub8 == 2 * pair + lane8 // 64, row, 0.0).astype(jnp.bfloat16)
                        for pair in range(4)
                    ],
                    axis=1,
                )
            )
        left = jnp.concatenate(pieces, axis=0)
        right = weights[SUB * g : SUB * g + SUB].reshape(SUB * cells, LANES)
        out = speed_scale * jnp.dot(left, right, preferred_element_type=jnp.float32)
        member = jnp.zeros((SUB, LANES), jnp.int32)
        for j in range(SUB):
            member = jnp.where(sub8 == j, lax.rem(swimmer[SUB * g + j], SWIM_DEV), member)
        for k in range(3):
            part = out[SUB * k : SUB * k + SUB, :]
            velocity[k, SUB * g : SUB * g + SUB, :] = part
            for s in range(SWIM_DEV):
                term = jnp.where(member == s, part, 0.0)
                sums[k, s] = term if g == 0 else sums[k, s] + term
    table = jnp.zeros((SUB, LANES), jnp.float32)
    for (k, s), value in sums.items():
        mean = jnp.sum(value) * (1.0 / LANES)
        table = jnp.where((sub8 == k) & (lane8 == s), mean, table)
    total[...] = table[0:3, 0:SWIM_DEV]


VM = pl.BlockSpec(memory_space=pltpu.VMEM)
SM = pl.BlockSpec(memory_space=pltpu.SMEM)
FAR = pl.BlockSpec(memory_space=pltpu.HBM)


def shaped(shape, dtype=jnp.float32):
    return jax.ShapeDtypeStruct(shape, dtype)


def step(populations, marker_weights, marker_force, owner_device, stencil_base, block_swimmer):
    slab_cells, strip_cells, height = populations.shape[1:]
    strips = lax.axis_size("gy")
    devices = lax.axis_size("gx") * strips
    held = marker_weights.shape[0]
    capacity = max(2, (2 * held + devices - 1) // devices)
    padded_rows = strip_cells + 2 * SUB
    packed_rows = strip_cells + SUB
    f32 = jnp.float32
    small = pltpu.CompilerParams(vmem_limit_bytes=12 * 1024 * 1024)

    owner = owner_device.T
    force = marker_force.transpose(1, 0, 2)
    edge = shaped((27, slab_cells, height))
    edge_rows = pltpu.VMEM((19, slab_cells, SUB, height), f32)
    sent, rim_a, rim_b = pl.pallas_call(
        functools.partial(patch_kernel, capacity, strips),
        out_shape=(shaped((devices, 16, LANES), jnp.bfloat16), edge, edge),
        in_specs=[FAR] * 5,
        out_specs=(VM, VM, VM),
        scratch_shapes=[
            pltpu.SMEM(owner.shape, jnp.int32),
            pltpu.SMEM((3, held), jnp.int32),
            pltpu.VMEM(marker_weights.shape, jnp.bfloat16),
            pltpu.VMEM(force.shape, jnp.bfloat16),
            edge_rows,
            edge_rows,
            pltpu.VMEM((3, held, LANES), f32),
            pltpu.VMEM((held * 16, LANES), f32),
            pltpu.VMEM((held, 16, LANES), f32),
            pltpu.VMEM((devices + 1, 16, LANES), f32),
            pltpu.SMEM((devices,), jnp.int32),
            pltpu.SMEM((held,), jnp.int32),
            pltpu.SMEM((held + DUP_STEP,), jnp.int32),
            pltpu.SemaphoreType.DMA((9,)),
        ],
        name="patches",
    )(owner, stencil_base.T, marker_weights, force, populations)
    got = lax.all_to_all(sent, ("gx", "gy"), split_axis=0, concat_axis=0, tiled=True)
    rim_a, rim_b = swapped(rim_a, rim_b, "gy", False)
    planes = shaped((19, slab_cells, padded_rows, height))
    face = shaped((FACE_FIELDS * strip_cells + 4 * SUB, height))
    push = shaped((3, slab_cells, packed_rows, height))
    rims = [pltpu.VMEM((5, padded_rows, height), f32)] * 4
    placed, items = pl.pallas_call(
        functools.partial(place_kernel, capacity),
        out_shape=(shaped((padded_rows * 16, LANES)), shaped((devices, LANES), jnp.int32)),
        in_specs=[VM],
        out_specs=(VM, VM),
        scratch_shapes=[
            pltpu.SMEM((devices, LANES), jnp.int32),
            pltpu.VMEM(((devices + 1) * 16, LANES), f32),
            pltpu.SMEM((SUB, LANES), jnp.int32),
            pltpu.SMEM((devices * 2 * capacity + DUP_STEP,), jnp.int32),
            pltpu.SMEM((devices + 1,), jnp.int32),
            pltpu.SemaphoreType.DMA,
        ],
        compiler_params=small,
        name="place",
    )(got)
    relaxed, face_a, face_b, forcing = pl.pallas_call(
        first_kernel,
        out_shape=(planes, face, face, push),
        in_specs=[VM] * 4,
        out_specs=(VM, VM, VM, VM),
        scratch_shapes=[pltpu.VMEM((19, slab_cells, SUB, LANES), f32)],
        compiler_params=small,
        name="first",
    )(placed, populations, rim_a, rim_b)
    got_a, got_b = swapped(face_a, face_b, "gx", True)
    fields, speeds = pl.pallas_call(
        functools.partial(second_kernel, capacity),
        out_shape=(shaped(populations.shape), shaped((devices, SUB, LANES), jnp.bfloat16)),
        in_specs=[VM, VM, VM, VM, VM],
        out_specs=(FAR, VM),
        scratch_shapes=[
            pltpu.SMEM((devices, LANES), jnp.int32),
            pltpu.VMEM(populations.shape, f32),
            pltpu.VMEM(planes.shape, f32),
        ]
        + rims
        + [
            pltpu.VMEM((4, strip_cells * 16, LANES), f32),
            pltpu.SemaphoreType.DMA((slab_cells + 1,)),
        ],
        compiler_params=small,
        name="second",
    )(items, relaxed, got_a, got_b, forcing)
    returned = lax.all_to_all(speeds, ("gx", "gy"), split_axis=0, concat_axis=0, tiled=True)
    marker_velocity, swimmer_velocity = pl.pallas_call(
        functools.partial(marker_kernel, capacity),
        out_shape=(shaped((3, held, LANES)), shaped((3, SWIM_DEV))),
        in_specs=[SM, SM, VM, VM],
        out_specs=(VM, VM),
        scratch_shapes=[
            pltpu.VMEM((held * 16, LANES), jnp.bfloat16),
            pltpu.VMEM((held * 16, LANES), f32),
            pltpu.SMEM((devices,), jnp.int32),
        ],
        compiler_params=small,
        name="markers",
    )(owner, block_swimmer, returned, marker_weights)
    return fields, marker_velocity.transpose(1, 0, 2), swimmer_velocity


def solution(mesh):
    in_specs = (
        P(None, "gx", "gy", None),
        P(("gx", "gy"), None, None),
        P(("gx", "gy"), None, None),
        P(("gx", "gy"), None),
        P(("gx", "gy"), None),
        P(("gx", "gy")),
    )
    out_specs = (P(None, "gx", "gy", None), P(("gx", "gy"), None, None), P(None, ("gx", "gy")))
    return jax.shard_map(step, mesh=mesh, in_specs=in_specs, out_specs=out_specs, check_vma=False)
```
